128 devices in a mesh: tenant: 16 (over z, y_lo, core), row: 8 (over x, y_hi).
Axes of the slice: x: 4, y: 4 (y_hi: 2, y_lo: 2; y = y_hi * 2 + y_lo), z: 4, core: 2. Of those that a mesh axis runs over, the one named last changes fastest.
Arguments:
- b_factors: float32 [128, 16, 8192], P('tenant', None, 'row'), may hold values from -6 to 6
- a_factors: float32 [128, 16, 8192], P('tenant', None, 'row'), may hold values from -6 to 6
- u_start: float32 [8192, 256], P('row'), may hold values from -0.0625 to 0.0625
- v_start: float32 [8192, 256], P('row'), may hold values from -0.0625 to 0.0625
Outputs:
- u_scaled: float32 [8192, 256], P('row')
- v_scaled: float32 [8192, 256], P('row')
- core_left: float32 [128, 16, 256], P('tenant')
- core_right: float32 [128, 16, 256], P('tenant')
The draws below stay inside these ranges and needn't reach their ends.
All inputs are finite; a program needn't handle non-finite values.
Results may differ from the reference program's by a relative error of at most 0.0003.
Values sent between devices are 32-bit elements; how exact they have to be, the bound alone decides.
No kernel may reach another device: no remote copies, remote signals or barrier semaphores. Data moves between devices by JAX's collectives and lax.ppermute only.
A program may use at most 64 MiB of HBM per device.

```python
import math
import jax
import jax.numpy as jnp
from jax import lax

D = 8192
K = 256
R = 16
SWEEPS = 1
NT = 128


def steps_of(stream_key, dims, shards, low, largest):
    def one(axis_at, parts):
        heights = jax.random.uniform(jax.random.fold_in(jax.random.fold_in(stream_key, 6), axis_at), (parts,), jnp.float32, low / len(shards), largest / len(shards))
        return jnp.repeat(jnp.exp(heights), dims[axis_at] // parts).reshape((-1,) + (1,) * (len(dims) - axis_at - 1))

    level = one(*shards[0])
    for cut in shards[1:]:
        level = level * one(*cut)
    return level


def noise(stream_key, shape, scale, limit, cuts=(), kind=jnp.bfloat16):
    drawn = scale * jax.random.normal(stream_key, shape, jnp.float32)
    if cuts:
        drawn = drawn * steps_of(stream_key, shape, cuts, -0.22, 0.18)
    return jnp.clip(drawn, -limit, limit).astype(kind)


def setup_inputs(seed: int = 0) -> dict:
    streams_of = jax.random.split(jax.random.key(seed), 5)
    return {
        "b_factors": noise(streams_of[0], (NT, R, D), 1.0, 6.0, ((0, 16), (2, 8)), jnp.float32),
        "a_factors": noise(streams_of[1], (NT, R, D), 1.0, 6.0, ((0, 16), (2, 8)), jnp.float32),
        "u_start": noise(streams_of[2], (D, K), D ** -0.5, 0.0625, ((0, 8),), jnp.float32),
        "v_start": noise(streams_of[3], (D, K), D ** -0.5, 0.0625, ((0, 8),), jnp.float32),
    }


HIGH = lax.Precision.HIGHEST

def project(factors, basis):
    return jnp.einsum('trd,dk->trk', factors, basis, precision=HIGH)

def orthonormal(matrix):
    gram = jnp.dot(matrix.T, matrix, precision=HIGH)
    lower = jnp.linalg.cholesky(gram)
    return lax.linalg.triangular_solve(lower, matrix, left_side=False, lower=True, transpose_a=True)

def reference(b_factors, a_factors, u_start, v_start):
    left = project(b_factors, u_start)
    right = project(a_factors, v_start)
    basis_u = u_start
    basis_v = v_start
    for sweep in range(SWEEPS):
        weight = jnp.einsum('trk,tsk->trs', right, right, precision=HIGH)
        coeffs = jnp.einsum('trs,tsk->trk', weight, left, precision=HIGH)
        basis_u = orthonormal(jnp.einsum('trd,trk->dk', b_factors, coeffs, precision=HIGH))
        left = project(b_factors, basis_u)
        weight = jnp.einsum('trk,tsk->trs', left, left, precision=HIGH)
        coeffs = jnp.einsum('trs,tsk->trk', weight, right, precision=HIGH)
        basis_v = orthonormal(jnp.einsum('trd,trk->dk', a_factors, coeffs, precision=HIGH))
        right = project(a_factors, basis_v)
    scale = math.sqrt(D)
    return (basis_u * scale, basis_v * scale, left, right)
```

```python
import math

import jax
import jax.numpy as jnp
from jax import lax
from jax.sharding import PartitionSpec as P

D = 8192
RANK = 16
HIGH = lax.Precision.HIGH


def chip_groups(count):
    return [[2 * chip + core for chip in range(count // 2)] for core in range(2)]


def sibling_pairs(count):
    return [(i, i ^ 1) for i in range(count)]


def exchanged(tiles, axis, groups=None):
    return lax.all_to_all(tiles, axis, 0, 0, axis_index_groups=groups, tiled=True)


def sum_at_owner(tiles, axis, groups=None):
    return jnp.sum(exchanged(tiles, axis, groups), axis=0)


def gathered(x, axis, count, groups=None):
    return exchanged(jnp.broadcast_to(x, (count, *x.shape)), axis, groups)


def tenant_total(factors, coeffs):
    count = lax.axis_size("tenant")
    core = lax.axis_index("tenant") % 2
    half = factors.shape[1] // 2
    chips = count // 2

    def part(which):
        columns = lax.dynamic_slice_in_dim(factors, which * half, half, 1)
        return jnp.einsum("td,tk->dk", columns, coeffs, precision=HIGH)

    other = lax.ppermute(part(1 - core), "tenant", sibling_pairs(count))
    mine = part(core) + other
    groups = chip_groups(count)
    tile = sum_at_owner(mine.reshape(chips, half // chips, -1), "tenant", groups)
    mine = gathered(tile, "tenant", chips, groups).reshape(half, -1)
    other = lax.ppermute(mine, "tenant", sibling_pairs(count))
    return jnp.where(core == 0, jnp.concatenate([mine, other]), jnp.concatenate([other, mine]))


def row_total(arrays):
    count = lax.axis_size("row")
    tiles = jnp.concatenate([a.reshape(count, -1, a.shape[-1]) for a in arrays], axis=1)
    whole = gathered(sum_at_owner(tiles, "row"), "row", count)
    ends = [0]
    for a in arrays:
        ends.append(ends[-1] + a.size // count // a.shape[-1])
    return [whole[:, b:e].reshape(a.shape) for a, b, e in zip(arrays, ends, ends[1:])]


def weighted(side, other):
    side = side.reshape(-1, RANK, side.shape[-1])
    other = other.reshape(side.shape)
    weight = jnp.einsum("trk,tsk->trs", side, side, precision=HIGH)
    return jnp.einsum("trs,tsk->trk", weight, other, precision=HIGH).reshape(-1, other.shape[-1])


def refresh(factors, coeffs):
    total = tenant_total(factors, coeffs)
    cores, gram = row_total(
        (
            jnp.dot(factors, total, precision=HIGH),
            jnp.einsum("dk,dl->kl", total, total, precision=HIGH),
        )
    )
    lower = jnp.linalg.cholesky(gram)
    both = jnp.concatenate([total, cores])
    both = lax.linalg.triangular_solve(lower, both, left_side=False, lower=True, transpose_a=True)
    return both[: len(total)], both[len(total) :]


def local(b_factors, a_factors, u_start, v_start):
    shape = (*b_factors.shape[:2], u_start.shape[1])
    b = b_factors.reshape(-1, b_factors.shape[2])
    a = a_factors.reshape(-1, a_factors.shape[2])
    count = lax.axis_size("row")
    left = jnp.dot(b, u_start, precision=HIGH).reshape(count, -1, shape[2])
    right = jnp.dot(a, v_start, precision=HIGH).reshape(count, -1, shape[2])
    owned = sum_at_owner(jnp.concatenate([left, right], axis=1), "row")
    left, right = jnp.split(owned, 2)
    pair = gathered(jnp.concatenate([weighted(right, left), right]), "row", count)
    coeffs, right = (x.reshape(-1, shape[2]) for x in jnp.split(pair, 2, axis=1))
    basis_u, left = refresh(b, coeffs)
    basis_v, right = refresh(a, weighted(left, right))
    scale = math.sqrt(D)
    return (basis_u * scale, basis_v * scale, left.reshape(shape), right.reshape(shape))


def solution(mesh):
    in_specs = (P("tenant", None, "row"), P("tenant", None, "row"), P("row", None), P("row", None))
    out_specs = (P("row", None), P("row", None), P("tenant", None, None), P("tenant", None, None))
    return jax.shard_map(local, mesh=mesh, in_specs=in_specs, out_specs=out_specs, check_vma=False)
```

```python
import math

import jax
import jax.numpy as jnp
from jax import lax
from jax.experimental import pallas as pl
from jax.experimental.pallas import tpu as pltpu
from jax.sharding import PartitionSpec as P

D = 8192
RANK = 16
LANES = 128
SUBLANES = 8
PANEL = 32


def pieces(x):
    high = x.astype(jnp.bfloat16)
    rest = x - high.astype(jnp.float32)
    middle = rest.astype(jnp.bfloat16)
    return high, middle, (rest - middle.astype(jnp.float32)).astype(jnp.bfloat16)


def float32_product(x, y):
    xh, xm, xl = pieces(x)
    yh, ym, yl = pieces(y)
    xs = jnp.concatenate([xh, xh, xm, xh, xl, xm])
    ys = jnp.concatenate([yh, ym, yh, yl, yh, ym])
    return lax.dot_general(xs, ys, (((0,), (0,)), ((), ())), preferred_element_type=jnp.float32)


def wide(x, width):
    return jnp.concatenate([x] * (width // LANES), axis=1)


def eliminate(rows, units, start):
    width = rows[0].shape[1]
    tile = (SUBLANES, LANES)
    for m, first in enumerate(range(start, start + PANEL, SUBLANES)):
        r = [jnp.broadcast_to(rows[m][i : i + 1], rows[m].shape) for i in range(SUBLANES)]
        e = [jnp.broadcast_to(units[m][i : i + 1], tile) for i in range(SUBLANES)]
        later = range(m + 1, len(rows))

        def column(x, j):
            return jnp.broadcast_to(x[:, first + j : first + j + 1], tile)

        d = [[column(r[i], j) for j in range(SUBLANES)] for i in range(SUBLANES)]
        c = {g: [column(rows[g], j) for j in range(SUBLANES)] for g in later}
        sub = lax.broadcasted_iota(jnp.int32, rows[m].shape, 0)
        sub_tile = lax.broadcasted_iota(jnp.int32, tile, 0)
        done, done_unit = jnp.zeros_like(rows[m]), jnp.zeros_like(units[m])
        for j in range(SUBLANES):
            inverse = lax.rsqrt(d[j][j])
            p, q = r[j] * wide(inverse, width), e[j] * inverse
            done = jnp.where(sub == j, p, done)
            done_unit = jnp.where(sub_tile == j, q, done_unit)
            below = range(j + 1, SUBLANES)
            factor = {i: d[j][i] * inverse for i in below}
            for i in below:
                for other in range(i, SUBLANES):
                    d[i][other] -= factor[i] * factor[other]
                r[i] -= wide(factor[i], width) * p
                e[i] -= factor[i] * q
            for g in later:
                scale = c[g][j] * inverse
                for i in below:
                    c[g][i] -= scale * factor[i]
                rows[g] -= wide(scale, width) * p
                units[g] -= scale * q
        rows[m], units[m] = done, done_unit
    return jnp.concatenate(rows), jnp.concatenate(units)


def split(x):
    high = x.astype(jnp.bfloat16)
    return high, (x - high.astype(jnp.float32)).astype(jnp.bfloat16)


def product(x, y, x_dim=1, y_dim=0):
    dims = (((x_dim,), (y_dim,)), ((), ()))
    xh, xl = split(x)
    yh, yl = split(y)

    def part(p, q):
        return lax.dot_general(p, q, dims, preferred_element_type=jnp.float32)

    return part(xh, yh) + (part(xh, yl) + part(xl, yh))


def matrix(x):
    return x.reshape(-1, x.shape[-1])


def factor_in_place(out_ref):
    n = out_ref.shape[0]
    sub = lax.broadcasted_iota(jnp.int32, (SUBLANES, LANES), 0)
    lane = lax.broadcasted_iota(jnp.int32, (SUBLANES, LANES), 1)
    column = lax.broadcasted_iota(jnp.int32, (n, n), 1)
    for start in range(0, n, PANEL):
        end = start + PANEL
        tile = start // LANES
        rows, units = [], []
        for g in range(0, PANEL, SUBLANES):
            rows.append(out_ref[pl.ds(start + g, SUBLANES), :])
            units.append(jnp.where(lane == sub + (start % LANES + g), 1.0, 0.0))
        rows, units = eliminate(rows, units, start)
        blank = jnp.zeros_like(units)
        units = jnp.concatenate([units if t == tile else blank for t in range(n // LANES)], axis=1)
        inside = (column >= start) & (column < end)
        solved = jnp.where(inside[:PANEL], units, rows)
        out_ref[pl.ds(start, PANEL), :] = jnp.where(column[:PANEL] < end, solved, 0.0)
        if end < n:
            aligned = end // LANES * LANES
            update = float32_product(rows[:, aligned:], solved)[end - aligned :]
            rest = out_ref[pl.ds(end, n - end), :]
            out_ref[pl.ds(end, n - end), :] = jnp.where(inside[end:], 0.0, rest) - update


def call(kernel, shapes, *operands, **options):
    shapes = [jax.ShapeDtypeStruct(shape, jnp.float32) for shape in shapes]
    return pl.pallas_call(
        kernel,
        out_shape=shapes if len(shapes) > 1 else shapes[0],
        compiler_params=pltpu.CompilerParams(vmem_limit_bytes=32 << 20),
        name=kernel.__name__,
        **options,
    )(*operands)


def projections(b_ref, a_ref, u_ref, v_ref, out_ref):
    left = product(b_ref[...], u_ref[...]).reshape(-1, RANK, out_ref.shape[2])
    right = product(a_ref[...], v_ref[...]).reshape(left.shape)
    first = pl.program_id(0) == 0

    @pl.when(first)
    def _():
        out_ref[:, :RANK] = left
        out_ref[:, RANK:] = right

    @pl.when(jnp.logical_not(first))
    def _():
        out_ref[:, :RANK] += left
        out_ref[:, RANK:] += right


def owner_coefficients(tiles_ref, out_ref):
    total = jnp.sum(tiles_ref[...], axis=0)
    left, right = total[:RANK], total[RANK:]
    coeffs = product(product(right, right, 1, 1), left)
    out_ref[:, :RANK] = jnp.broadcast_to(coeffs, (len(out_ref), *coeffs.shape))
    out_ref[:, RANK:] = jnp.broadcast_to(right, (len(out_ref), *right.shape))


def owner_sum(tiles_ref, out_ref):
    out_ref[...] = jnp.broadcast_to(jnp.sum(tiles_ref[...], axis=0), out_ref.shape)


def both(x_ref, y_ref):
    return jnp.concatenate([matrix(x_ref[...]), matrix(y_ref[...])])


def both_upper(x_ref, y_ref):
    return jnp.concatenate([matrix(x_ref[:, :RANK]), matrix(y_ref[:, :RANK])])


def both_lower(x_ref, y_ref):
    return jnp.concatenate([matrix(x_ref[:, RANK:]), matrix(y_ref[:, RANK:])])


def load_sum(keep_ref, swap_ref, mine_ref, other_ref, out_ref):
    load = product(both(keep_ref, swap_ref), both_upper(mine_ref, other_ref), 0, 0)
    out_ref[...] = load.reshape(out_ref.shape)


def gram_and_cores(core_ref, keep_ref, swap_ref, basis_ref, mine_ref, other_ref, gram_ref):
    basis = matrix(basis_ref[...])
    cores = product(both(keep_ref, swap_ref), basis)
    gram_ref[...] = product(basis, basis, 0, 0)
    count, half = len(mine_ref), len(gram_ref) // 2
    mine_ref[:, :RANK] = cores[:half].reshape(count, RANK, -1)
    other_ref[:, :RANK] = cores[half:].reshape(count, RANK, -1)
    core = core_ref[0]
    mine_ref[:, RANK:] = gram_ref[pl.ds(core * half, half), :].reshape(count, RANK, -1)
    other_ref[:, RANK:] = gram_ref[pl.ds((1 - core) * half, half), :].reshape(count, RANK, -1)


def inverse_factor(core, mine_ref, other_ref, inverse_ref):
    half = len(inverse_ref) // 2
    inverse_ref[pl.ds(core * half, half), :] = matrix(mine_ref[:, RANK:])
    inverse_ref[pl.ds((1 - core) * half, half), :] = matrix(other_ref[:, RANK:])
    factor_in_place(inverse_ref)


def turn_over(
    core_ref, mine_ref, other_ref, pair_ref, pair_other_ref, keep_ref, swap_ref,
    inverse_ref, left_ref, load_ref,
):
    inverse_factor(core_ref[0], mine_ref, other_ref, inverse_ref)
    left = product(both_upper(mine_ref, other_ref), inverse_ref[...], 1, 1)
    left_ref[...] = left[: len(left) // 2].reshape(left_ref.shape)
    weight = product(left, left, 1, 1)
    tenant = [lax.broadcasted_iota(jnp.int32, weight.shape, d) // RANK for d in range(2)]
    weight = jnp.where(tenant[0] == tenant[1], weight, 0.0)
    coeffs = product(weight, both_lower(pair_ref, pair_other_ref))
    load = product(both(keep_ref, swap_ref), coeffs, 0, 0)
    load_ref[...] = load.reshape(load_ref.shape)


def scaled_basis(core, inverse, mine_ref, other_ref, out_ref):
    half = len(out_ref) // 2
    scale = math.sqrt(D)
    for place, ref in ((core, mine_ref), (1 - core, other_ref)):
        out_ref[pl.ds(place * half, half), :] = product(matrix(ref[...]), inverse, 1, 1) * scale


def left_basis(core_ref, inverse_ref, mine_ref, other_ref, out_ref):
    scaled_basis(core_ref[0], inverse_ref[...], mine_ref, other_ref, out_ref)


def finish(core_ref, mine_ref, other_ref, basis_ref, basis_other_ref, out_ref, right_ref, inverse_ref):
    inverse_factor(core_ref[0], mine_ref, other_ref, inverse_ref)
    inverse = inverse_ref[...]
    right = product(matrix(mine_ref[:, :RANK]), inverse, 1, 1)
    right_ref[...] = right.reshape(right_ref.shape)
    scaled_basis(core_ref[0], inverse, basis_ref, basis_other_ref, out_ref)


def exchanged(tiles, axis, groups=None):
    return lax.all_to_all(tiles, axis, 0, 0, axis_index_groups=groups, tiled=True)


def total(tiles, axis, groups=None, at_owner=owner_sum):
    copies = call(at_owner, [tiles.shape], exchanged(tiles, axis, groups))
    return exchanged(copies, axis, groups)


def from_sibling(x):
    count = lax.axis_size("tenant")
    return lax.ppermute(x, "tenant", [(i, i ^ 1) for i in range(count)])


def tenant_total(load):
    chips = lax.axis_size("tenant") // 2
    groups = [[2 * chip + core for chip in range(chips)] for core in range(2)]
    return total(load, "tenant", groups)


def gram_total(core, halves, basis, rank):
    count = lax.axis_size("row")
    tiles = (count, 2 * RANK, rank)
    mine, other = call(
        gram_and_cores,
        [tiles, tiles],
        core,
        *halves,
        basis,
        in_specs=with_core(3),
        scratch_shapes=[pltpu.VMEM((rank, rank), jnp.float32)],
    )
    return total(mine + from_sibling(other), "row")


def column_halves(factors, core):
    half = factors.shape[1] // 2
    keep = lax.dynamic_slice_in_dim(factors, core * half, half, 1)
    return keep, from_sibling(lax.dynamic_slice_in_dim(factors, (1 - core) * half, half, 1))


def with_core(count):
    return [pl.BlockSpec(memory_space=m) for m in (pltpu.SMEM, *[pltpu.VMEM] * count)]


def local(b_factors, a_factors, u_start, v_start):
    shape = (*b_factors.shape[:2], u_start.shape[1])
    width, rank = u_start.shape
    core = lax.axis_index("tenant") % 2
    flag = jnp.reshape(core, (1,)).astype(jnp.int32)
    b = b_factors.reshape(-1, width)
    a = a_factors.reshape(-1, width)
    b_halves, a_halves = column_halves(b, core), column_halves(a, core)

    step = width // 4
    factor_block = pl.BlockSpec((len(b), step), lambda i: (0, i))
    basis_block = pl.BlockSpec((step, rank), lambda i: (i, 0))
    tiles = (shape[0], 2 * RANK, rank)
    partial = call(
        projections,
        [tiles],
        b,
        a,
        u_start,
        v_start,
        grid=(4,),
        in_specs=[factor_block, factor_block, basis_block, basis_block],
        out_specs=pl.BlockSpec(tiles, lambda i: (0, 0, 0)),
    )
    pair = total(partial, "row", None, owner_coefficients)
    pair_other = from_sibling(pair)

    chips = lax.axis_size("tenant") // 2
    load_shape = (chips, width // 2 // chips, rank)
    load = call(load_sum, [load_shape], *b_halves, pair, pair_other)
    basis = tenant_total(load)
    basis_other = from_sibling(basis)
    mine = gram_total(flag, b_halves, basis, rank)
    inverse, left, load = call(
        turn_over,
        [(rank, rank), shape, load_shape],
        flag,
        mine,
        from_sibling(mine),
        pair,
        pair_other,
        *a_halves,
        in_specs=with_core(6),
    )
    u_scaled = call(
        left_basis, [(width, rank)], flag, inverse, basis, basis_other, in_specs=with_core(3)
    )
    basis = tenant_total(load)
    basis_other = from_sibling(basis)
    mine = gram_total(flag, a_halves, basis, rank)
    v_scaled, right = call(
        finish,
        [(width, rank), shape],
        flag,
        mine,
        from_sibling(mine),
        basis,
        basis_other,
        in_specs=with_core(4),
        scratch_shapes=[pltpu.VMEM((rank, rank), jnp.float32)],
    )
    return u_scaled, v_scaled, left, right


def solution(mesh):
    in_specs = (P("tenant", None, "row"), P("tenant", None, "row"), P("row", None), P("row", None))
    out_specs = (P("row", None), P("row", None), P("tenant", None, None), P("tenant", None, None))
    return jax.shard_map(local, mesh=mesh, in_specs=in_specs, out_specs=out_specs, check_vma=False)
```

```python
import math

import jax
import jax.numpy as jnp
from jax import lax
from jax.experimental import pallas as pl
from jax.experimental.pallas import tpu as pltpu
from jax.sharding import PartitionSpec as P

D = 8192
RANK = 16
LANES = 128
SUBLANES = 8
PANEL = 32


def pieces(x):
    high = x.astype(jnp.bfloat16)
    rest = x - high.astype(jnp.float32)
    middle = rest.astype(jnp.bfloat16)
    return high, middle, (rest - middle.astype(jnp.float32)).astype(jnp.bfloat16)


def float32_product(x, y):
    xh, xm, xl = pieces(x)
    yh, ym, yl = pieces(y)
    xs = jnp.concatenate([xh, xh, xm, xh, xl, xm])
    ys = jnp.concatenate([yh, ym, yh, yl, yh, ym])
    return lax.dot_general(xs, ys, (((0,), (0,)), ((), ())), preferred_element_type=jnp.float32)


def wide(x, width):
    return jnp.concatenate([x] * (width // LANES), axis=1)


def eliminate(rows, units, start):
    width = rows[0].shape[1]
    tile = (SUBLANES, LANES)
    for m, first in enumerate(range(start, start + PANEL, SUBLANES)):
        r = [jnp.broadcast_to(rows[m][i : i + 1], rows[m].shape) for i in range(SUBLANES)]
        e = [jnp.broadcast_to(units[m][i : i + 1], tile) for i in range(SUBLANES)]
        later = range(m + 1, len(rows))

        def column(x, j):
            return jnp.broadcast_to(x[:, first + j : first + j + 1], tile)

        d = [[column(r[i], j) for j in range(SUBLANES)] for i in range(SUBLANES)]
        c = {g: [column(rows[g], j) for j in range(SUBLANES)] for g in later}
        sub = lax.broadcasted_iota(jnp.int32, rows[m].shape, 0)
        sub_tile = lax.broadcasted_iota(jnp.int32, tile, 0)
        done, done_unit = jnp.zeros_like(rows[m]), jnp.zeros_like(units[m])
        for j in range(SUBLANES):
            inverse = lax.rsqrt(d[j][j])
            p, q = r[j] * wide(inverse, width), e[j] * inverse
            done = jnp.where(sub == j, p, done)
            done_unit = jnp.where(sub_tile == j, q, done_unit)
            below = range(j + 1, SUBLANES)
            factor = {i: d[j][i] * inverse for i in below}
            for i in below:
                for other in range(i, SUBLANES):
                    d[i][other] -= factor[i] * factor[other]
                r[i] -= wide(factor[i], width) * p
                e[i] -= factor[i] * q
            for g in later:
                scale = c[g][j] * inverse
                for i in below:
                    c[g][i] -= scale * factor[i]
                rows[g] -= wide(scale, width) * p
                units[g] -= scale * q
        rows[m], units[m] = done, done_unit
    return jnp.concatenate(rows), jnp.concatenate(units)


def split(x):
    high = x.astype(jnp.bfloat16)
    return high, (x - high.astype(jnp.float32)).astype(jnp.bfloat16)


def product(x, y, x_dim=1, y_dim=0):
    dims = (((x_dim,), (y_dim,)), ((), ()))
    xh, xl = split(x)
    yh, yl = split(y)

    def part(p, q):
        return lax.dot_general(p, q, dims, preferred_element_type=jnp.float32)

    return part(xh, yh) + (part(xh, yl) + part(xl, yh))


def matrix(x):
    return x.reshape(-1, x.shape[-1])


def factor_in_place(out_ref):
    n = out_ref.shape[0]
    sub = lax.broadcasted_iota(jnp.int32, (SUBLANES, LANES), 0)
    lane = lax.broadcasted_iota(jnp.int32, (SUBLANES, LANES), 1)
    column = lax.broadcasted_iota(jnp.int32, (n, n), 1)
    for start in range(0, n, PANEL):
        end = start + PANEL
        tile = start // LANES
        rows, units = [], []
        for g in range(0, PANEL, SUBLANES):
            rows.append(out_ref[pl.ds(start + g, SUBLANES), :])
            units.append(jnp.where(lane == sub + (start % LANES + g), 1.0, 0.0))
        rows, units = eliminate(rows, units, start)
        blank = jnp.zeros_like(units)
        units = jnp.concatenate([units if t == tile else blank for t in range(n // LANES)], axis=1)
        inside = (column >= start) & (column < end)
        solved = jnp.where(inside[:PANEL], units, rows)
        out_ref[pl.ds(start, PANEL), :] = jnp.where(column[:PANEL] < end, solved, 0.0)
        if end < n:
            aligned = end // LANES * LANES
            update = float32_product(rows[:, aligned:], solved)[end - aligned :]
            rest = out_ref[pl.ds(end, n - end), :]
            out_ref[pl.ds(end, n - end), :] = jnp.where(inside[end:], 0.0, rest) - update


def call(kernel, shapes, *operands, **options):
    shapes = [jax.ShapeDtypeStruct(shape, jnp.float32) for shape in shapes]
    return pl.pallas_call(
        kernel,
        out_shape=shapes if len(shapes) > 1 else shapes[0],
        compiler_params=pltpu.CompilerParams(vmem_limit_bytes=32 << 20),
        name=kernel.__name__,
        **options,
    )(*operands)


def projections(b_ref, a_ref, u_ref, v_ref, out_ref):
    left = product(b_ref[...], u_ref[...]).reshape(-1, RANK, out_ref.shape[2])
    right = product(a_ref[...], v_ref[...]).reshape(left.shape)
    first = pl.program_id(0) == 0

    @pl.when(first)
    def _():
        out_ref[:, :RANK] = left
        out_ref[:, RANK:] = right

    @pl.when(jnp.logical_not(first))
    def _():
        out_ref[:, :RANK] += left
        out_ref[:, RANK:] += right


def owner_coefficients(tiles_ref, out_ref):
    total = jnp.sum(tiles_ref[...], axis=0)
    left, right = total[:RANK], total[RANK:]
    coeffs = product(product(right, right, 1, 1), left)
    out_ref[:, :RANK] = jnp.broadcast_to(coeffs, (len(out_ref), *coeffs.shape))
    out_ref[:, RANK:] = jnp.broadcast_to(right, (len(out_ref), *right.shape))


def owner_sum(tiles_ref, out_ref):
    out_ref[...] = jnp.broadcast_to(jnp.sum(tiles_ref[...], axis=0), out_ref.shape)


def both(x_ref, y_ref):
    return jnp.concatenate([matrix(x_ref[...]), matrix(y_ref[...])])


def both_upper(x_ref, y_ref):
    return jnp.concatenate([matrix(x_ref[:, :RANK]), matrix(y_ref[:, :RANK])])


def both_lower(x_ref, y_ref):
    return jnp.concatenate([matrix(x_ref[:, RANK:]), matrix(y_ref[:, RANK:])])


def load_sum(keep_ref, swap_ref, mine_ref, other_ref, out_ref):
    load = product(both(keep_ref, swap_ref), both_upper(mine_ref, other_ref), 0, 0)
    out_ref[...] = load.reshape(out_ref.shape)


def gram_and_cores(core_ref, keep_ref, swap_ref, basis_ref, mine_ref, other_ref, gram_ref):
    basis = matrix(basis_ref[...])
    cores = product(both(keep_ref, swap_ref), basis)
    gram_ref[...] = product(basis, basis, 0, 0)
    count, half = len(mine_ref), len(gram_ref) // 2
    mine_ref[:, :RANK] = cores[:half].reshape(count, RANK, -1)
    other_ref[:, :RANK] = cores[half:].reshape(count, RANK, -1)
    core = core_ref[0]
    mine_ref[:, RANK:] = gram_ref[pl.ds(core * half, half), :].reshape(count, RANK, -1)
    other_ref[:, RANK:] = gram_ref[pl.ds((1 - core) * half, half), :].reshape(count, RANK, -1)


def inverse_factor(core, mine_ref, other_ref, inverse_ref):
    half = len(inverse_ref) // 2
    inverse_ref[pl.ds(core * half, half), :] = matrix(mine_ref[:, RANK:])
    inverse_ref[pl.ds((1 - core) * half, half), :] = matrix(other_ref[:, RANK:])
    factor_in_place(inverse_ref)


def turn_over(
    core_ref, mine_ref, other_ref, pair_ref, pair_other_ref, keep_ref, swap_ref,
    inverse_ref, left_ref, load_ref,
):
    inverse_factor(core_ref[0], mine_ref, other_ref, inverse_ref)
    left = product(both_upper(mine_ref, other_ref), inverse_ref[...], 1, 1)
    left_ref[...] = left[: len(left) // 2].reshape(left_ref.shape)
    weight = product(left, left, 1, 1)
    tenant = [lax.broadcasted_iota(jnp.int32, weight.shape, d) // RANK for d in range(2)]
    weight = jnp.where(tenant[0] == tenant[1], weight, 0.0)
    coeffs = product(weight, both_lower(pair_ref, pair_other_ref))
    load = product(both(keep_ref, swap_ref), coeffs, 0, 0)
    load_ref[...] = load.reshape(load_ref.shape)


def scaled_basis(core, inverse, mine_ref, other_ref, out_ref):
    half = len(out_ref) // 2
    scale = math.sqrt(D)
    for place, ref in ((core, mine_ref), (1 - core, other_ref)):
        out_ref[pl.ds(place * half, half), :] = product(matrix(ref[...]), inverse, 1, 1) * scale


def left_basis(core_ref, inverse_ref, mine_ref, other_ref, out_ref):
    scaled_basis(core_ref[0], inverse_ref[...], mine_ref, other_ref, out_ref)


def finish(core_ref, mine_ref, other_ref, basis_ref, basis_other_ref, out_ref, right_ref, inverse_ref):
    inverse_factor(core_ref[0], mine_ref, other_ref, inverse_ref)
    inverse = inverse_ref[...]
    right = product(matrix(mine_ref[:, :RANK]), inverse, 1, 1)
    right_ref[...] = right.reshape(right_ref.shape)
    scaled_basis(core_ref[0], inverse, basis_ref, basis_other_ref, out_ref)


def exchanged(tiles, axis, groups=None):
    return lax.all_to_all(tiles, axis, 0, 0, axis_index_groups=groups, tiled=True)


def total(tiles, axis, groups=None, at_owner=owner_sum):
    copies = call(at_owner, [tiles.shape], exchanged(tiles, axis, groups))
    return exchanged(copies, axis, groups)


def from_sibling(x):
    count = lax.axis_size("tenant")
    return lax.ppermute(x, "tenant", [(i, i ^ 1) for i in range(count)])


def tenant_total(load):
    chips = lax.axis_size("tenant") // 2
    groups = [[2 * chip + core for chip in range(chips)] for core in range(2)]
    return total(load, "tenant", groups)


def gram_total(core, halves, basis, rank, beside=()):
    count = lax.axis_size("row")
    tiles = (count, 2 * RANK, rank)
    mine, other = call(
        gram_and_cores,
        [tiles, tiles],
        core,
        *halves,
        basis,
        in_specs=with_core(3),
        scratch_shapes=[pltpu.VMEM((rank, rank), jnp.float32)],
    )
    other, beside = lax.optimization_barrier((from_sibling(other), beside))
    return total(mine + other, "row"), beside


def column_halves(factors, core):
    half = factors.shape[1] // 2
    keep = lax.dynamic_slice_in_dim(factors, core * half, half, 1)
    return keep, from_sibling(lax.dynamic_slice_in_dim(factors, (1 - core) * half, half, 1))


def with_core(count):
    return [pl.BlockSpec(memory_space=m) for m in (pltpu.SMEM, *[pltpu.VMEM] * count)]


def local(b_factors, a_factors, u_start, v_start):
    shape = (*b_factors.shape[:2], u_start.shape[1])
    width, rank = u_start.shape
    core = lax.axis_index("tenant") % 2
    flag = jnp.reshape(core, (1,)).astype(jnp.int32)
    b = b_factors.reshape(-1, width)
    a = a_factors.reshape(-1, width)
    b_halves, a_halves = column_halves(b, core), column_halves(a, core)

    step = width // 4
    factor_block = pl.BlockSpec((len(b), step), lambda i: (0, i))
    basis_block = pl.BlockSpec((step, rank), lambda i: (i, 0))
    tiles = (shape[0], 2 * RANK, rank)
    partial = call(
        projections,
        [tiles],
        *(pltpu.with_memory_space_constraint(x, pltpu.HBM) for x in (b, a, u_start, v_start)),
        grid=(4,),
        in_specs=[factor_block, factor_block, basis_block, basis_block],
        out_specs=pl.BlockSpec(tiles, lambda i: (0, 0, 0)),
    )
    pair = total(partial, "row", None, owner_coefficients)
    pair_other = from_sibling(pair)

    chips = lax.axis_size("tenant") // 2
    load_shape = (chips, width // 2 // chips, rank)
    load = call(load_sum, [load_shape], *b_halves, pair, pair_other)
    basis = tenant_total(load)
    basis_other = from_sibling(basis)
    mine, _ = gram_total(flag, b_halves, basis, rank)
    inverse, left, load = call(
        turn_over,
        [(rank, rank), shape, load_shape],
        flag,
        mine,
        from_sibling(mine),
        pair,
        pair_other,
        *a_halves,
        in_specs=with_core(6),
    )
    u_scaled = call(
        left_basis,
        [(width, rank)],
        flag,
        inverse,
        basis,
        basis_other,
        in_specs=with_core(3),
        cost_estimate=pl.CostEstimate(
            flops=6 * width * rank * rank, bytes_accessed=8 * width * rank, transcendentals=0
        ),
    )
    basis = tenant_total(load)
    basis_other = from_sibling(basis)
    mine, u_scaled = gram_total(flag, a_halves, basis, rank, u_scaled)
    v_scaled, right = call(
        finish,
        [(width, rank), shape],
        flag,
        mine,
        from_sibling(mine),
        basis,
        basis_other,
        in_specs=with_core(4),
        scratch_shapes=[pltpu.VMEM((rank, rank), jnp.float32)],
    )
    return u_scaled, v_scaled, left, right


def solution(mesh):
    in_specs = (P("tenant", None, "row"), P("tenant", None, "row"), P("row", None), P("row", None))
    out_specs = (P("row", None), P("row", None), P("tenant", None, None), P("tenant", None, None))
    return jax.shard_map(local, mesh=mesh, in_specs=in_specs, out_specs=out_specs, check_vma=False)
```

```python
import math

import jax
import jax.numpy as jnp
from jax import lax
from jax.experimental import pallas as pl
from jax.experimental.pallas import tpu as pltpu
from jax.sharding import PartitionSpec as P

D = 8192
RANK = 16
LANES = 128
SUBLANES = 8
PANEL = 32
STEPS = 4


def pieces(x):
    high = x.astype(jnp.bfloat16)
    rest = x - high.astype(jnp.float32)
    middle = rest.astype(jnp.bfloat16)
    return high, middle, (rest - middle.astype(jnp.float32)).astype(jnp.bfloat16)


def float32_product(x, y):
    xh, xm, xl = pieces(x)
    yh, ym, yl = pieces(y)
    xs = jnp.concatenate([xh, xh, xm, xh, xl, xm])
    ys = jnp.concatenate([yh, ym, yh, yl, yh, ym])
    return lax.dot_general(xs, ys, (((0,), (0,)), ((), ())), preferred_element_type=jnp.float32)


def column(x, lane):
    return jnp.broadcast_to(x[:, lane : lane + 1], (SUBLANES, LANES))


def spread(ref, row):
    return ref[pl.ds(row, SUBLANES, stride=0), :]


def eliminate(rows, units, start, rows_ref, columns_ref, factors_ref):
    sub = lax.broadcasted_iota(jnp.int32, (SUBLANES, LANES), 0)
    tile = start // LANES
    for m, first in enumerate(range(start % LANES, start % LANES + PANEL, SUBLANES)):
        slot = m % 4
        tiles = [*rows[m], units[m]]
        if m == 0:
            pivots = [column(rows[m][tile], first + j) for j in range(SUBLANES)]
        for j in range(SUBLANES):
            columns_ref[slot, pl.ds(j * SUBLANES, SUBLANES), :] = pivots[j]
        for t, x in enumerate(tiles):
            rows_ref[slot, pl.ds(t * SUBLANES, SUBLANES), :] = x
        r = [
            [spread(rows_ref.at[slot], t * SUBLANES + i) for t in range(len(tiles))]
            for i in range(SUBLANES)
        ]
        d = [
            [spread(columns_ref.at[slot], j * SUBLANES + i) for j in range(SUBLANES)]
            for i in range(SUBLANES)
        ]
        later = range(m + 1, len(rows))
        c = {g: [column(rows[g][tile], first + j) for j in range(SUBLANES)] for g in later}
        if later:
            ahead = first + SUBLANES
            pivots = [column(rows[m + 1][tile], ahead + j) for j in range(SUBLANES)]
        done = tiles
        for j in range(SUBLANES):
            inverse = lax.rsqrt(d[j][j])
            p = [x * inverse for x in r[j]]
            done = [jnp.where(sub == j, x, y) for x, y in zip(p, done)]
            below = range(j + 1, SUBLANES)
            factor = {i: d[j][i] * inverse for i in below}
            for i in below:
                for other in range(i, SUBLANES):
                    d[i][other] -= factor[i] * factor[other]
                r[i] = [x - factor[i] * y for x, y in zip(r[i], p)]
            for g in later:
                scale = c[g][j] * inverse
                if g == m + 1:
                    place = pl.ds(j * SUBLANES, SUBLANES)
                    factors_ref[slot, place, :] = scale
                    for k in range(SUBLANES):
                        pivots[k] -= scale * spread(factors_ref.at[slot], j * SUBLANES + k)
                for i in below:
                    c[g][i] -= scale * factor[i]
                rows[g] = [x - scale * y for x, y in zip(rows[g], p)]
                units[g] -= scale * p[-1]
        rows[m], units[m] = done[:-1], done[-1]
    rows = [jnp.concatenate(tiles, axis=1) for tiles in rows]
    return jnp.concatenate(rows), jnp.concatenate(units)


def split(x):
    high = x.astype(jnp.bfloat16)
    return high, (x - high.astype(jnp.float32)).astype(jnp.bfloat16)


def product(x, y, x_dim=1, y_dim=0):
    dims = (((x_dim,), (y_dim,)), ((), ()))
    xh, xl = split(x)
    yh, yl = split(y)

    def part(p, q):
        return lax.dot_general(p, q, dims, preferred_element_type=jnp.float32)

    return part(xh, yh) + (part(xh, yl) + part(xl, yh))


def matrix(x):
    return x.reshape(-1, x.shape[-1])


def factor_in_place(out_ref, *scratch):
    n = out_ref.shape[0]
    sub = lax.broadcasted_iota(jnp.int32, (SUBLANES, LANES), 0)
    lane = lax.broadcasted_iota(jnp.int32, (SUBLANES, LANES), 1)
    column = lax.broadcasted_iota(jnp.int32, (n, n), 1)
    for start in range(0, n, PANEL):
        end = start + PANEL
        tile = start // LANES
        rows, units = [], []
        for g in range(0, PANEL, SUBLANES):
            place = pl.ds(start + g, SUBLANES)
            rows.append([out_ref[place, pl.ds(t, LANES)] for t in range(0, n, LANES)])
            units.append(jnp.where(lane == sub + (start % LANES + g), 1.0, 0.0))
        rows, units = eliminate(rows, units, start, *scratch)
        blank = jnp.zeros_like(units)
        units = jnp.concatenate([units if t == tile else blank for t in range(n // LANES)], axis=1)
        inside = (column >= start) & (column < end)
        solved = jnp.where(inside[:PANEL], units, rows)
        out_ref[pl.ds(start, PANEL), :] = jnp.where(column[:PANEL] < end, solved, 0.0)
        if end < n:
            aligned = end // LANES * LANES
            update = float32_product(rows[:, aligned:], solved)[end - aligned :]
            rest = out_ref[pl.ds(end, n - end), :]
            out_ref[pl.ds(end, n - end), :] = jnp.where(inside[end:], 0.0, rest) - update


def factor_scratch(n):
    tiles = n // LANES + 1
    return [
        pltpu.VMEM((4, tiles * SUBLANES, LANES), jnp.float32),
        pltpu.VMEM((4, SUBLANES * SUBLANES, LANES), jnp.float32),
        pltpu.VMEM((4, SUBLANES * SUBLANES, LANES), jnp.float32),
    ]


def call(kernel, shapes, *operands, **options):
    shapes = [jax.ShapeDtypeStruct(shape, jnp.float32) for shape in shapes]
    return pl.pallas_call(
        kernel,
        out_shape=shapes if len(shapes) > 1 else shapes[0],
        compiler_params=pltpu.CompilerParams(vmem_limit_bytes=32 << 20),
        name=kernel.__name__,
        **options,
    )(*operands)


def projections(b_hbm, a_hbm, u_hbm, v_hbm, out_ref, b_ref, a_ref, u_ref, v_ref, sems):
    step = b_ref.shape[1] // STEPS
    copies = []
    for i in range(STEPS):
        part = pl.ds(i * step, step)
        pairs = (
            (u_hbm.at[part], u_ref.at[part]),
            (b_hbm.at[:, part], b_ref.at[:, part]),
            (v_hbm.at[part], v_ref.at[part]),
            (a_hbm.at[:, part], a_ref.at[:, part]),
        )
        copies.append([pltpu.make_async_copy(*p, sems.at[i, k]) for k, p in enumerate(pairs)])
    for group in copies:
        for copy in group:
            copy.start()
    left = right = 0.0
    for i, group in enumerate(copies):
        part = pl.ds(i * step, step)
        group[0].wait()
        group[1].wait()
        left += product(b_ref[:, part], u_ref[part])
        group[2].wait()
        group[3].wait()
        right += product(a_ref[:, part], v_ref[part])
    out_ref[:, :RANK] = left.reshape(-1, RANK, left.shape[1])
    out_ref[:, RANK:] = right.reshape(-1, RANK, right.shape[1])


def owner_coefficients(tiles_ref, out_ref):
    total = jnp.sum(tiles_ref[...], axis=0)
    left, right = total[:RANK], total[RANK:]
    coeffs = product(product(right, right, 1, 1), left)
    out_ref[:, :RANK] = jnp.broadcast_to(coeffs, (len(out_ref), *coeffs.shape))
    out_ref[:, RANK:] = jnp.broadcast_to(right, (len(out_ref), *right.shape))


def owner_sum(tiles_ref, out_ref):
    out_ref[...] = jnp.broadcast_to(jnp.sum(tiles_ref[...], axis=0), out_ref.shape)


def both(x_ref, y_ref):
    return jnp.concatenate([matrix(x_ref[...]), matrix(y_ref[...])])


def both_upper(x_ref, y_ref):
    return jnp.concatenate([matrix(x_ref[:, :RANK]), matrix(y_ref[:, :RANK])])


def both_lower(x_ref, y_ref):
    return jnp.concatenate([matrix(x_ref[:, RANK:]), matrix(y_ref[:, RANK:])])


def load_sum(keep_ref, swap_ref, mine_ref, other_ref, out_ref):
    load = product(both(keep_ref, swap_ref), both_upper(mine_ref, other_ref), 0, 0)
    out_ref[...] = load.reshape(out_ref.shape)


def gram_and_cores(core_ref, keep_ref, swap_ref, basis_ref, mine_ref, other_ref, gram_ref):
    basis = matrix(basis_ref[...])
    cores = product(both(keep_ref, swap_ref), basis)
    gram_ref[...] = product(basis, basis, 0, 0)
    count, half = len(mine_ref), len(gram_ref) // 2
    mine_ref[:, :RANK] = cores[:half].reshape(count, RANK, -1)
    other_ref[:, :RANK] = cores[half:].reshape(count, RANK, -1)
    core = core_ref[0]
    mine_ref[:, RANK:] = gram_ref[pl.ds(core * half, half), :].reshape(count, RANK, -1)
    other_ref[:, RANK:] = gram_ref[pl.ds((1 - core) * half, half), :].reshape(count, RANK, -1)


def inverse_factor(core, mine_ref, other_ref, inverse_ref, *scratch):
    half = len(inverse_ref) // 2
    inverse_ref[pl.ds(core * half, half), :] = matrix(mine_ref[:, RANK:])
    inverse_ref[pl.ds((1 - core) * half, half), :] = matrix(other_ref[:, RANK:])
    factor_in_place(inverse_ref, *scratch)


def turn_over(
    core_ref, mine_ref, other_ref, pair_ref, pair_other_ref, keep_ref, swap_ref,
    inverse_ref, left_ref, load_ref, *scratch,
):
    inverse_factor(core_ref[0], mine_ref, other_ref, inverse_ref, *scratch)
    left = product(both_upper(mine_ref, other_ref), inverse_ref[...], 1, 1)
    left_ref[...] = left[: len(left) // 2].reshape(left_ref.shape)
    weight = product(left, left, 1, 1)
    tenant = [lax.broadcasted_iota(jnp.int32, weight.shape, d) // RANK for d in range(2)]
    weight = jnp.where(tenant[0] == tenant[1], weight, 0.0)
    coeffs = product(weight, both_lower(pair_ref, pair_other_ref))
    load = product(both(keep_ref, swap_ref), coeffs, 0, 0)
    load_ref[...] = load.reshape(load_ref.shape)


def scaled_basis(core, inverse, mine_ref, other_ref, out_ref):
    half = len(out_ref) // 2
    scale = math.sqrt(D)
    for place, ref in ((core, mine_ref), (1 - core, other_ref)):
        out_ref[pl.ds(place * half, half), :] = product(matrix(ref[...]), inverse, 1, 1) * scale


def left_basis(core_ref, inverse_ref, mine_ref, other_ref, out_ref):
    scaled_basis(core_ref[0], inverse_ref[...], mine_ref, other_ref, out_ref)


def finish(
    core_ref, mine_ref, other_ref, basis_ref, basis_other_ref,
    out_ref, right_ref, inverse_ref, *scratch,
):
    inverse_factor(core_ref[0], mine_ref, other_ref, inverse_ref, *scratch)
    inverse = inverse_ref[...]
    right = product(matrix(mine_ref[:, :RANK]), inverse, 1, 1)
    right_ref[...] = right.reshape(right_ref.shape)
    scaled_basis(core_ref[0], inverse, basis_ref, basis_other_ref, out_ref)


def exchanged(tiles, axis, groups=None):
    return lax.all_to_all(tiles, axis, 0, 0, axis_index_groups=groups, tiled=True)


def total(tiles, axis, groups=None, at_owner=owner_sum):
    copies = call(at_owner, [tiles.shape], exchanged(tiles, axis, groups))
    return exchanged(copies, axis, groups)


def from_sibling(x):
    count = lax.axis_size("tenant")
    return lax.ppermute(x, "tenant", [(i, i ^ 1) for i in range(count)])


def tenant_total(load):
    chips = lax.axis_size("tenant") // 2
    groups = [[2 * chip + core for chip in range(chips)] for core in range(2)]
    return total(load, "tenant", groups)


def gram_total(core, halves, basis, rank, beside=()):
    count = lax.axis_size("row")
    tiles = (count, 2 * RANK, rank)
    mine, other = call(
        gram_and_cores,
        [tiles, tiles],
        core,
        *halves,
        basis,
        in_specs=with_core(3),
        scratch_shapes=[pltpu.VMEM((rank, rank), jnp.float32)],
    )
    other, beside = lax.optimization_barrier((from_sibling(other), beside))
    return total(mine + other, "row"), beside


def column_halves(factors, core):
    half = factors.shape[1] // 2
    keep = lax.dynamic_slice_in_dim(factors, core * half, half, 1)
    return keep, from_sibling(lax.dynamic_slice_in_dim(factors, (1 - core) * half, half, 1))


def with_core(count):
    return [pl.BlockSpec(memory_space=m) for m in (pltpu.SMEM, *[pltpu.VMEM] * count)]


def local(b_factors, a_factors, u_start, v_start):
    shape = (*b_factors.shape[:2], u_start.shape[1])
    width, rank = u_start.shape
    core = lax.axis_index("tenant") % 2
    flag = jnp.reshape(core, (1,)).astype(jnp.int32)
    b = b_factors.reshape(-1, width)
    a = a_factors.reshape(-1, width)
    b_halves, a_halves = column_halves(b, core), column_halves(a, core)

    partial = call(
        projections,
        [(shape[0], 2 * RANK, rank)],
        b,
        a,
        u_start,
        v_start,
        in_specs=[pl.BlockSpec(memory_space=pltpu.HBM)] * 4,
        scratch_shapes=[
            *(pltpu.VMEM(x.shape, x.dtype) for x in (b, a, u_start, v_start)),
            pltpu.SemaphoreType.DMA((STEPS, 4)),
        ],
    )
    pair = total(partial, "row", None, owner_coefficients)
    pair_other = from_sibling(pair)

    chips = lax.axis_size("tenant") // 2
    load_shape = (chips, width // 2 // chips, rank)
    load = call(load_sum, [load_shape], *b_halves, pair, pair_other)
    basis = tenant_total(load)
    basis_other = from_sibling(basis)
    mine, _ = gram_total(flag, b_halves, basis, rank)
    inverse, left, load = call(
        turn_over,
        [(rank, rank), shape, load_shape],
        flag,
        mine,
        from_sibling(mine),
        pair,
        pair_other,
        *a_halves,
        in_specs=with_core(6),
        scratch_shapes=factor_scratch(rank),
    )
    u_scaled = call(
        left_basis,
        [(width, rank)],
        flag,
        inverse,
        basis,
        basis_other,
        in_specs=with_core(3),
        cost_estimate=pl.CostEstimate(
            flops=6 * width * rank * rank, bytes_accessed=8 * width * rank, transcendentals=0
        ),
    )
    basis = tenant_total(load)
    basis_other = from_sibling(basis)
    mine, u_scaled = gram_total(flag, a_halves, basis, rank, u_scaled)
    v_scaled, right = call(
        finish,
        [(width, rank), shape],
        flag,
        mine,
        from_sibling(mine),
        basis,
        basis_other,
        in_specs=with_core(4),
        scratch_shapes=[pltpu.VMEM((rank, rank), jnp.float32), *factor_scratch(rank)],
    )
    return u_scaled, v_scaled, left, right


def solution(mesh):
    in_specs = (P("tenant", None, "row"), P("tenant", None, "row"), P("row", None), P("row", None))
    out_specs = (P("row", None), P("row", None), P("tenant", None, None), P("tenant", None, None))
    return jax.shard_map(local, mesh=mesh, in_specs=in_specs, out_specs=out_specs, check_vma=False)
```

```python
import math

import jax
import jax.numpy as jnp
from jax import lax
from jax.experimental import pallas as pl
from jax.experimental.pallas import tpu as pltpu
from jax.sharding import PartitionSpec as P

D = 8192
RANK = 16
LANES = 128
SUBLANES = 8
PANEL = 32
STEPS = 4


def pieces(x):
    high = x.astype(jnp.bfloat16)
    rest = x - high.astype(jnp.float32)
    middle = rest.astype(jnp.bfloat16)
    return high, middle, (rest - middle.astype(jnp.float32)).astype(jnp.bfloat16)


def float32_product(x, y):
    xh, xm, xl = pieces(x)
    yh, ym, yl = pieces(y)
    xs = jnp.concatenate([xh, xh, xm, xh, xl, xm])
    ys = jnp.concatenate([yh, ym, yh, yl, yh, ym])
    return lax.dot_general(xs, ys, (((0,), (0,)), ((), ())), preferred_element_type=jnp.float32)


def column(x, lane):
    return jnp.broadcast_to(x[:, lane : lane + 1], (SUBLANES, LANES))


def spread(ref, row):
    return ref[pl.ds(row, SUBLANES, stride=0), :]


def eliminate(rows, units, start, rows_ref, columns_ref, factors_ref):
    sub = lax.broadcasted_iota(jnp.int32, (SUBLANES, LANES), 0)
    tile = start // LANES
    for m, first in enumerate(range(start % LANES, start % LANES + PANEL, SUBLANES)):
        slot = m % 4
        tiles = [*rows[m], units[m]]
        if m == 0:
            pivots = [column(rows[m][tile], first + j) for j in range(SUBLANES)]
        for j in range(SUBLANES):
            columns_ref[slot, pl.ds(j * SUBLANES, SUBLANES), :] = pivots[j]
        for t, x in enumerate(tiles):
            rows_ref[slot, pl.ds(t * SUBLANES, SUBLANES), :] = x
        r = [
            [spread(rows_ref.at[slot], t * SUBLANES + i) for t in range(len(tiles))]
            for i in range(SUBLANES)
        ]
        d = [
            [spread(columns_ref.at[slot], j * SUBLANES + i) for j in range(SUBLANES)]
            for i in range(SUBLANES)
        ]
        later = range(m + 1, len(rows))
        c = {g: [column(rows[g][tile], first + j) for j in range(SUBLANES)] for g in later}
        if later:
            ahead = first + SUBLANES
            pivots = [column(rows[m + 1][tile], ahead + j) for j in range(SUBLANES)]
        done = tiles
        for j in range(SUBLANES):
            inverse = lax.rsqrt(d[j][j])
            p = [x * inverse for x in r[j]]
            done = [jnp.where(sub == j, x, y) for x, y in zip(p, done)]
            below = range(j + 1, SUBLANES)
            factor = {i: d[j][i] * inverse for i in below}
            for i in below:
                for other in range(i, SUBLANES):
                    d[i][other] -= factor[i] * factor[other]
                r[i] = [x - factor[i] * y for x, y in zip(r[i], p)]
            for g in later:
                scale = c[g][j] * inverse
                if g == m + 1:
                    place = pl.ds(j * SUBLANES, SUBLANES)
                    factors_ref[slot, place, :] = scale
                    for k in range(SUBLANES):
                        pivots[k] -= scale * spread(factors_ref.at[slot], j * SUBLANES + k)
                for i in below:
                    c[g][i] -= scale * factor[i]
                rows[g] = [x - scale * y for x, y in zip(rows[g], p)]
                units[g] -= scale * p[-1]
        rows[m], units[m] = done[:-1], done[-1]
    rows = [jnp.concatenate(tiles, axis=1) for tiles in rows]
    return jnp.concatenate(rows), jnp.concatenate(units)


def split(x):
    high = x.astype(jnp.bfloat16)
    return high, (x - high.astype(jnp.float32)).astype(jnp.bfloat16)


def product(x, y, x_dim=1, y_dim=0):
    dims = (((x_dim,), (y_dim,)), ((), ()))
    xh, xl = split(x)
    yh, yl = split(y)

    def part(p, q):
        return lax.dot_general(p, q, dims, preferred_element_type=jnp.float32)

    return part(xh, yh) + (part(xh, yl) + part(xl, yh))


def matrix(x):
    return x.reshape(-1, x.shape[-1])


def factor_in_place(out_ref, *scratch):
    n = out_ref.shape[0]
    sub = lax.broadcasted_iota(jnp.int32, (SUBLANES, LANES), 0)
    lane = lax.broadcasted_iota(jnp.int32, (SUBLANES, LANES), 1)
    column = lax.broadcasted_iota(jnp.int32, (n, n), 1)
    for start in range(0, n, PANEL):
        end = start + PANEL
        tile = start // LANES
        rows, units = [], []
        for g in range(0, PANEL, SUBLANES):
            place = pl.ds(start + g, SUBLANES)
            rows.append([out_ref[place, pl.ds(t, LANES)] for t in range(0, n, LANES)])
            units.append(jnp.where(lane == sub + (start % LANES + g), 1.0, 0.0))
        rows, units = eliminate(rows, units, start, *scratch)
        blank = jnp.zeros_like(units)
        units = jnp.concatenate([units if t == tile else blank for t in range(n // LANES)], axis=1)
        inside = (column >= start) & (column < end)
        solved = jnp.where(inside[:PANEL], units, rows)
        out_ref[pl.ds(start, PANEL), :] = jnp.where(column[:PANEL] < end, solved, 0.0)
        if end < n:
            aligned = end // LANES * LANES
            update = float32_product(rows[:, aligned:], solved)[end - aligned :]
            rest = out_ref[pl.ds(end, n - end), :]
            out_ref[pl.ds(end, n - end), :] = jnp.where(inside[end:], 0.0, rest) - update


def factor_scratch(n):
    tiles = n // LANES + 1
    return [
        pltpu.VMEM((4, tiles * SUBLANES, LANES), jnp.float32),
        pltpu.VMEM((4, SUBLANES * SUBLANES, LANES), jnp.float32),
        pltpu.VMEM((4, SUBLANES * SUBLANES, LANES), jnp.float32),
    ]


def call(kernel, shapes, *operands, **options):
    shapes = [jax.ShapeDtypeStruct(shape, jnp.float32) for shape in shapes]
    return pl.pallas_call(
        kernel,
        out_shape=shapes if len(shapes) > 1 else shapes[0],
        compiler_params=pltpu.CompilerParams(vmem_limit_bytes=32 << 20),
        name=kernel.__name__,
        **options,
    )(*operands)


def projections(b_hbm, a_hbm, u_hbm, v_hbm, out_ref, b_ref, a_ref, u_ref, v_ref, sems):
    step = b_ref.shape[1] // STEPS
    copies = []
    for i in range(STEPS):
        part = pl.ds(i * step, step)
        pairs = (
            (u_hbm.at[part], u_ref.at[part]),
            (b_hbm.at[:, part], b_ref.at[:, part]),
            (v_hbm.at[part], v_ref.at[part]),
            (a_hbm.at[:, part], a_ref.at[:, part]),
        )
        copies.append([pltpu.make_async_copy(*p, sems.at[i, k]) for k, p in enumerate(pairs)])
    for group in copies:
        for copy in group:
            copy.start()
    left = right = 0.0
    for i, group in enumerate(copies):
        part = pl.ds(i * step, step)
        group[0].wait()
        group[1].wait()
        left += product(b_ref[:, part], u_ref[part])
        group[2].wait()
        group[3].wait()
        right += product(a_ref[:, part], v_ref[part])
    out_ref[:, :RANK] = left.reshape(-1, RANK, left.shape[1])
    out_ref[:, RANK:] = right.reshape(-1, RANK, right.shape[1])


def owner_coefficients(tiles_ref, out_ref):
    total = jnp.sum(tiles_ref[...], axis=0)
    left, right = total[:RANK], total[RANK:]
    coeffs = product(product(right, right, 1, 1), left)
    out_ref[:, :RANK] = jnp.broadcast_to(coeffs, (len(out_ref), *coeffs.shape))
    out_ref[:, RANK:] = jnp.broadcast_to(right, (len(out_ref), *right.shape))


def owner_sum(tiles_ref, out_ref):
    out_ref[...] = jnp.broadcast_to(jnp.sum(tiles_ref[...], axis=0), out_ref.shape)


def both(x_ref, y_ref):
    return jnp.concatenate([matrix(x_ref[...]), matrix(y_ref[...])])


def both_upper(x_ref, y_ref):
    return jnp.concatenate([matrix(x_ref[:, :RANK]), matrix(y_ref[:, :RANK])])


def both_lower(x_ref, y_ref):
    return jnp.concatenate([matrix(x_ref[:, RANK:]), matrix(y_ref[:, RANK:])])


def load_sum(keep_ref, swap_ref, mine_ref, other_ref, out_ref):
    load = product(both(keep_ref, swap_ref), both_upper(mine_ref, other_ref), 0, 0)
    out_ref[...] = load.reshape(out_ref.shape)


def gram_and_cores(core_ref, keep_ref, swap_ref, basis_ref, mine_ref, other_ref, gram_ref):
    basis = matrix(basis_ref[...])
    cores = product(both(keep_ref, swap_ref), basis)
    gram_ref[...] = product(basis, basis, 0, 0)
    count, half = len(mine_ref), len(gram_ref) // 2
    mine_ref[:, :RANK] = cores[:half].reshape(count, RANK, -1)
    other_ref[:, :RANK] = cores[half:].reshape(count, RANK, -1)
    core = core_ref[0]
    mine_ref[:, RANK:] = gram_ref[pl.ds(core * half, half), :].reshape(count, RANK, -1)
    other_ref[:, RANK:] = gram_ref[pl.ds((1 - core) * half, half), :].reshape(count, RANK, -1)


def inverse_factor(core, mine_ref, other_ref, inverse_ref, *scratch):
    half = len(inverse_ref) // 2
    inverse_ref[pl.ds(core * half, half), :] = matrix(mine_ref[:, RANK:])
    inverse_ref[pl.ds((1 - core) * half, half), :] = matrix(other_ref[:, RANK:])
    factor_in_place(inverse_ref, *scratch)


def turn_over(
    core_ref, mine_ref, other_ref, pair_ref, pair_other_ref, keep_ref, swap_ref,
    inverse_ref, left_ref, load_ref, *scratch,
):
    inverse_factor(core_ref[0], mine_ref, other_ref, inverse_ref, *scratch)
    left = product(both_upper(mine_ref, other_ref), inverse_ref[...], 1, 1)
    left_ref[...] = left[: len(left) // 2].reshape(left_ref.shape)
    weight = product(left, left, 1, 1)
    tenant = [lax.broadcasted_iota(jnp.int32, weight.shape, d) // RANK for d in range(2)]
    weight = jnp.where(tenant[0] == tenant[1], weight, 0.0)
    coeffs = product(weight, both_lower(pair_ref, pair_other_ref))
    load = product(both(keep_ref, swap_ref), coeffs, 0, 0)
    load_ref[...] = load.reshape(load_ref.shape)


def scaled_basis(core, inverse, mine_ref, other_ref, out_ref):
    half = len(out_ref) // 2
    scale = math.sqrt(D)
    for place, ref in ((core, mine_ref), (1 - core, other_ref)):
        out_ref[pl.ds(place * half, half), :] = product(matrix(ref[...]), inverse, 1, 1) * scale


def left_basis(core_ref, inverse_ref, mine_ref, other_ref, out_ref):
    scaled_basis(core_ref[0], inverse_ref[...], mine_ref, other_ref, out_ref)


def finish(
    core_ref, mine_ref, other_ref, basis_ref, basis_other_ref,
    out_ref, right_ref, inverse_ref, *scratch,
):
    inverse_factor(core_ref[0], mine_ref, other_ref, inverse_ref, *scratch)
    inverse = inverse_ref[...]
    right = product(matrix(mine_ref[:, :RANK]), inverse, 1, 1)
    right_ref[...] = right.reshape(right_ref.shape)
    scaled_basis(core_ref[0], inverse, basis_ref, basis_other_ref, out_ref)


def exchanged(tiles, axis, groups=None):
    return lax.all_to_all(tiles, axis, 0, 0, axis_index_groups=groups, tiled=True)


def total(tiles, axis, groups=None, at_owner=owner_sum):
    copies = call(at_owner, [tiles.shape], exchanged(tiles, axis, groups))
    return exchanged(copies, axis, groups)


def from_sibling(x):
    count = lax.axis_size("tenant")
    return lax.ppermute(x, "tenant", [(i, i ^ 1) for i in range(count)])


def tenant_total(load):
    chips = lax.axis_size("tenant") // 2
    groups = [[2 * chip + core for chip in range(chips)] for core in range(2)]
    return total(load, "tenant", groups)


def gram_total(core, halves, basis, rank, beside=()):
    count = lax.axis_size("row")
    tiles = (count, 2 * RANK, rank)
    mine, other = call(
        gram_and_cores,
        [tiles, tiles],
        core,
        *halves,
        basis,
        in_specs=with_core(3),
        scratch_shapes=[pltpu.VMEM((rank, rank), jnp.float32)],
    )
    other, beside = lax.optimization_barrier((from_sibling(other), beside))
    return total(mine + other, "row"), beside


def column_halves(factors, core):
    half = factors.shape[1] // 2
    keep = lax.dynamic_slice_in_dim(factors, core * half, half, 1)
    return keep, from_sibling(lax.dynamic_slice_in_dim(factors, (1 - core) * half, half, 1))


def with_core(count):
    return [pl.BlockSpec(memory_space=m) for m in (pltpu.SMEM, *[pltpu.VMEM] * count)]


def local(b_factors, a_factors, u_start, v_start):
    shape = (*b_factors.shape[:2], u_start.shape[1])
    width, rank = u_start.shape
    core = lax.axis_index("tenant") % 2
    flag = jnp.reshape(core, (1,)).astype(jnp.int32)
    b = b_factors.reshape(-1, width)
    a = a_factors.reshape(-1, width)
    b_halves, a_halves = column_halves(b, core), column_halves(a, core)

    partial = call(
        projections,
        [(shape[0], 2 * RANK, rank)],
        *(pltpu.with_memory_space_constraint(x, pltpu.HBM) for x in (b, a, u_start, v_start)),
        in_specs=[pl.BlockSpec(memory_space=pltpu.HBM)] * 4,
        scratch_shapes=[
            *(pltpu.VMEM(x.shape, x.dtype) for x in (b, a, u_start, v_start)),
            pltpu.SemaphoreType.DMA((STEPS, 4)),
        ],
    )
    pair = total(partial, "row", None, owner_coefficients)
    pair_other = from_sibling(pair)

    chips = lax.axis_size("tenant") // 2
    load_shape = (chips, width // 2 // chips, rank)
    load = call(load_sum, [load_shape], *b_halves, pair, pair_other)
    basis = tenant_total(load)
    basis_other = from_sibling(basis)
    mine, _ = gram_total(flag, b_halves, basis, rank)
    mine_other, basis_other = lax.optimization_barrier((from_sibling(mine), basis_other))
    inverse, left, load = call(
        turn_over,
        [(rank, rank), shape, load_shape],
        flag,
        mine,
        mine_other,
        pair,
        pair_other,
        *a_halves,
        in_specs=with_core(6),
        scratch_shapes=factor_scratch(rank),
    )
    u_scaled = call(
        left_basis,
        [(width, rank)],
        flag,
        inverse,
        basis,
        basis_other,
        in_specs=with_core(3),
        cost_estimate=pl.CostEstimate(
            flops=6 * width * rank * rank, bytes_accessed=8 * width * rank, transcendentals=0
        ),
    )
    basis = tenant_total(load)
    basis_other = from_sibling(basis)
    mine, u_scaled = gram_total(flag, a_halves, basis, rank, u_scaled)
    v_scaled, right = call(
        finish,
        [(width, rank), shape],
        flag,
        mine,
        from_sibling(mine),
        basis,
        basis_other,
        in_specs=with_core(4),
        scratch_shapes=[pltpu.VMEM((rank, rank), jnp.float32), *factor_scratch(rank)],
    )
    return u_scaled, v_scaled, left, right


def solution(mesh):
    in_specs = (P("tenant", None, "row"), P("tenant", None, "row"), P("row", None), P("row", None))
    out_specs = (P("row", None), P("row", None), P("tenant", None, None), P("tenant", None, None))
    return jax.shard_map(local, mesh=mesh, in_specs=in_specs, out_specs=out_specs, check_vma=False)
```

```python
import math

import jax
import jax.numpy as jnp
from jax import lax
from jax.experimental import pallas as pl
from jax.experimental.pallas import tpu as pltpu
from jax.sharding import Mesh
from jax.sharding import PartitionSpec as P

D = 8192
RANK = 16
LANES = 128
SUBLANES = 8
PANEL = 32
STEPS = 4
ROW = ("y_lo", "row")
QUARTER = ("y_lo", "core")
STEPS_AWAY = (0, 2, 1, 3)


def pieces(x):
    high = x.astype(jnp.bfloat16)
    rest = x - high.astype(jnp.float32)
    middle = rest.astype(jnp.bfloat16)
    return high, middle, (rest - middle.astype(jnp.float32)).astype(jnp.bfloat16)


def float32_product(x, y):
    xh, xm, xl = pieces(x)
    yh, ym, yl = pieces(y)
    xs = jnp.concatenate([xh, xh, xm, xh, xl, xm])
    ys = jnp.concatenate([yh, ym, yh, yl, yh, ym])
    return lax.dot_general(xs, ys, (((0,), (0,)), ((), ())), preferred_element_type=jnp.float32)


def column(x, lane):
    return jnp.broadcast_to(x[:, lane : lane + 1], (SUBLANES, LANES))


def spread(ref, row):
    return ref[pl.ds(row, SUBLANES, stride=0), :]


def eliminate(rows, units, start, rows_ref, columns_ref, factors_ref):
    sub = lax.broadcasted_iota(jnp.int32, (SUBLANES, LANES), 0)
    tile = start // LANES
    for m, first in enumerate(range(start % LANES, start % LANES + PANEL, SUBLANES)):
        slot = m % 4
        tiles = [*rows[m], units[m]]
        if m == 0:
            pivots = [column(rows[m][tile], first + j) for j in range(SUBLANES)]
        for j in range(SUBLANES):
            columns_ref[slot, pl.ds(j * SUBLANES, SUBLANES), :] = pivots[j]
        for t, x in enumerate(tiles):
            rows_ref[slot, pl.ds(t * SUBLANES, SUBLANES), :] = x
        r = [
            [spread(rows_ref.at[slot], t * SUBLANES + i) for t in range(len(tiles))]
            for i in range(SUBLANES)
        ]
        d = [
            [spread(columns_ref.at[slot], j * SUBLANES + i) for j in range(SUBLANES)]
            for i in range(SUBLANES)
        ]
        later = range(m + 1, len(rows))
        c = {g: [column(rows[g][tile], first + j) for j in range(SUBLANES)] for g in later}
        if later:
            ahead = first + SUBLANES
            pivots = [column(rows[m + 1][tile], ahead + j) for j in range(SUBLANES)]
        done = tiles
        for j in range(SUBLANES):
            inverse = lax.rsqrt(d[j][j])
            p = [x * inverse for x in r[j]]
            done = [jnp.where(sub == j, x, y) for x, y in zip(p, done)]
            below = range(j + 1, SUBLANES)
            factor = {i: d[j][i] * inverse for i in below}
            for i in below:
                for other in range(i, SUBLANES):
                    d[i][other] -= factor[i] * factor[other]
                r[i] = [x - factor[i] * y for x, y in zip(r[i], p)]
            for g in later:
                scale = c[g][j] * inverse
                if g == m + 1:
                    place = pl.ds(j * SUBLANES, SUBLANES)
                    factors_ref[slot, place, :] = scale
                    for k in range(SUBLANES):
                        pivots[k] -= scale * spread(factors_ref.at[slot], j * SUBLANES + k)
                for i in below:
                    c[g][i] -= scale * factor[i]
                rows[g] = [x - scale * y for x, y in zip(rows[g], p)]
                units[g] -= scale * p[-1]
        rows[m], units[m] = done[:-1], done[-1]
    rows = [jnp.concatenate(tiles, axis=1) for tiles in rows]
    return jnp.concatenate(rows), jnp.concatenate(units)


def split(x):
    high = x.astype(jnp.bfloat16)
    return high, (x - high.astype(jnp.float32)).astype(jnp.bfloat16)


def product(x, y, x_dim=1, y_dim=0):
    dims = (((x_dim,), (y_dim,)), ((), ()))
    xh, xl = split(x)
    yh, yl = split(y)

    def part(p, q):
        return lax.dot_general(p, q, dims, preferred_element_type=jnp.float32)

    return part(xh, yh) + (part(xh, yl) + part(xl, yh))


def matrix(x):
    return x.reshape(-1, x.shape[-1])


def factor_in_place(out_ref, *scratch):
    n = out_ref.shape[0]
    sub = lax.broadcasted_iota(jnp.int32, (SUBLANES, LANES), 0)
    lane = lax.broadcasted_iota(jnp.int32, (SUBLANES, LANES), 1)
    column = lax.broadcasted_iota(jnp.int32, (n, n), 1)
    for start in range(0, n, PANEL):
        end = start + PANEL
        tile = start // LANES
        rows, units = [], []
        for g in range(0, PANEL, SUBLANES):
            place = pl.ds(start + g, SUBLANES)
            rows.append([out_ref[place, pl.ds(t, LANES)] for t in range(0, n, LANES)])
            units.append(jnp.where(lane == sub + (start % LANES + g), 1.0, 0.0))
        rows, units = eliminate(rows, units, start, *scratch)
        blank = jnp.zeros_like(units)
        units = jnp.concatenate([units if t == tile else blank for t in range(n // LANES)], axis=1)
        inside = (column >= start) & (column < end)
        solved = jnp.where(inside[:PANEL], units, rows)
        out_ref[pl.ds(start, PANEL), :] = jnp.where(column[:PANEL] < end, solved, 0.0)
        if end < n:
            aligned = end // LANES * LANES
            update = float32_product(rows[:, aligned:], solved)[end - aligned :]
            rest = out_ref[pl.ds(end, n - end), :]
            out_ref[pl.ds(end, n - end), :] = jnp.where(inside[end:], 0.0, rest) - update


def factor_scratch(n):
    tiles = n // LANES + 1
    return [
        pltpu.VMEM((4, tiles * SUBLANES, LANES), jnp.float32),
        pltpu.VMEM((4, SUBLANES * SUBLANES, LANES), jnp.float32),
        pltpu.VMEM((4, SUBLANES * SUBLANES, LANES), jnp.float32),
    ]


def call(kernel, shapes, *operands, **options):
    shapes = [jax.ShapeDtypeStruct(shape, jnp.float32) for shape in shapes]
    return pl.pallas_call(
        kernel,
        out_shape=shapes if len(shapes) > 1 else shapes[0],
        compiler_params=pltpu.CompilerParams(vmem_limit_bytes=32 << 20),
        name=kernel.__name__,
        **options,
    )(*operands)


def projections(b_hbm, a_hbm, u_hbm, v_hbm, out_ref, b_ref, a_ref, u_ref, v_ref, sems):
    step = b_ref.shape[1] // STEPS
    copies = []
    for i in range(STEPS):
        part = pl.ds(i * step, step)
        pairs = (
            (u_hbm.at[part], u_ref.at[part]),
            (b_hbm.at[:, part], b_ref.at[:, part]),
            (v_hbm.at[part], v_ref.at[part]),
            (a_hbm.at[:, part], a_ref.at[:, part]),
        )
        copies.append([pltpu.make_async_copy(*p, sems.at[i, k]) for k, p in enumerate(pairs)])
    for group in copies:
        for copy in group:
            copy.start()
    left = right = 0.0
    for i, group in enumerate(copies):
        part = pl.ds(i * step, step)
        group[0].wait()
        group[1].wait()
        left += product(b_ref[:, part], u_ref[part])
        group[2].wait()
        group[3].wait()
        right += product(a_ref[:, part], v_ref[part])
    out_ref[:, :RANK] = left.reshape(-1, RANK, left.shape[1])
    out_ref[:, RANK:] = right.reshape(-1, RANK, right.shape[1])


def owner_coefficients(tiles_ref, out_ref):
    total = jnp.sum(tiles_ref[...], axis=0)
    left, right = total[:RANK], total[RANK:]
    coeffs = product(product(right, right, 1, 1), left)
    out_ref[:, :RANK] = jnp.broadcast_to(coeffs, (len(out_ref), *coeffs.shape))
    out_ref[:, RANK:] = jnp.broadcast_to(right, (len(out_ref), *right.shape))


def owner_sum(tiles_ref, out_ref):
    out_ref[...] = jnp.broadcast_to(jnp.sum(tiles_ref[...], axis=0), out_ref.shape)


def stacked(refs):
    return jnp.concatenate([ref[...] for ref in refs])


def by_distance(quarter, ref):
    count = len(ref) // 2
    half = quarter // 2
    return [pl.ds(place * count, count) for place in (half, 1 - half)]


def tenants(quarter, refs, first):
    rows = pl.ds(first, RANK)
    tiles = [ref[place, rows] for ref in refs for place in by_distance(quarter, ref)]
    return jnp.concatenate([matrix(x) for x in tiles])


def load_sum(quarter_ref, f0, f1, f2, f3, mine_ref, other_ref, *out_refs):
    coeffs = tenants(quarter_ref[0], (mine_ref, other_ref), 0)
    store_load(product(stacked((f0, f1, f2, f3)), coeffs, 0, 0), out_refs)


def store_load(load, out_refs):
    count = len(out_refs[0])
    for i, ref in enumerate(out_refs):
        ref[...] = load[i * count : (i + 1) * count]


def gram_and_cores(quarter_ref, f0, f1, f2, f3, x_ref, y_ref, mine_ref, other_ref, gram_ref):
    basis = stacked((x_ref, y_ref))
    cores = product(stacked((f0, f1, f2, f3)), basis)
    gram_ref[...] = product(basis, basis, 0, 0)
    quarter = quarter_ref[0]
    core, half = quarter % 2, len(gram_ref) // 2
    block = len(cores) // 4
    for i, (ref, which) in enumerate(((mine_ref, core), (other_ref, 1 - core))):
        for j, place in enumerate(by_distance(quarter, ref)):
            rows = cores[(2 * i + j) * block : (2 * i + j + 1) * block]
            ref[place, :RANK] = rows.reshape(-1, RANK, rows.shape[1])
        rows = gram_ref[pl.ds(which * half, half), :]
        ref[:, RANK:] = rows.reshape(len(ref), -1, rows.shape[1])


def inverse_factor(core, mine_ref, other_ref, inverse_ref, *scratch):
    half = len(inverse_ref) // 2
    inverse_ref[pl.ds(core * half, half), :] = matrix(mine_ref[:, RANK:])
    inverse_ref[pl.ds((1 - core) * half, half), :] = matrix(other_ref[:, RANK:])
    factor_in_place(inverse_ref, *scratch)


def turn_over(
    quarter_ref, mine_ref, other_ref, pair_ref, pair_other_ref, f0, f1, f2, f3,
    inverse_ref, left_ref, x_ref, y_ref, *scratch,
):
    quarter = quarter_ref[0]
    inverse_factor(quarter % 2, mine_ref, other_ref, inverse_ref, *scratch)
    left = product(tenants(quarter, (mine_ref, other_ref), 0), inverse_ref[...], 1, 1)
    right = tenants(quarter, (pair_ref, pair_other_ref), RANK)
    own = left[: len(left) // 4]
    left_ref[...] = own.reshape(left_ref.shape)
    half = len(left) // 2
    tenant = [lax.broadcasted_iota(jnp.int32, (half, half), d) // RANK for d in range(2)]
    coeffs = []
    for part in (slice(0, half), slice(half, None)):
        weight = jnp.where(tenant[0] == tenant[1], product(left[part], left[part], 1, 1), 0.0)
        coeffs.append(product(weight, right[part]))
    load = product(stacked((f0, f1, f2, f3)), jnp.concatenate(coeffs), 0, 0)
    store_load(load, (x_ref, y_ref))


def scaled_basis(quarter, inverse, refs, out_ref):
    scale = math.sqrt(D)
    for step, ref in zip(STEPS_AWAY, refs):
        rows = pl.ds((quarter ^ step) * len(ref), len(ref))
        out_ref[rows, :] = product(ref[...], inverse, 1, 1) * scale


def left_basis(quarter_ref, inverse_ref, q0, q1, q2, q3, out_ref):
    scaled_basis(quarter_ref[0], inverse_ref[...], (q0, q1, q2, q3), out_ref)


def finish(
    quarter_ref, mine_ref, other_ref, q0, q1, q2, q3, out_ref, right_ref, inverse_ref, *scratch
):
    quarter = quarter_ref[0]
    inverse_factor(quarter % 2, mine_ref, other_ref, inverse_ref, *scratch)
    inverse = inverse_ref[...]
    own = matrix(mine_ref[by_distance(quarter, mine_ref)[0], :RANK])
    right_ref[...] = product(own, inverse, 1, 1).reshape(right_ref.shape)
    scaled_basis(quarter, inverse, (q0, q1, q2, q3), out_ref)


def exchanged(tiles, axis):
    return lax.all_to_all(tiles, axis, 0, 0, tiled=True)


def from_peer(x, axis, step):
    count = lax.axis_size(axis)
    return lax.ppermute(x, axis, [(i, i ^ step) for i in range(count)])


def row_total(tiles):
    tiles = exchanged(tiles, ROW)
    return exchanged(call(owner_sum, [tiles.shape], tiles), ROW)


def plane_total(x, y):
    for x_step, y_step in ((1, 3), (3, 1)):
        x, y = x + from_peer(x, "z", x_step), y + from_peer(y, "z", y_step)
    return x, y


def from_sibling(x):
    return from_peer(x, "core", 1)


def column_quarters(factors, quarter):
    size = factors.shape[1] // 4

    def columns(step):
        return lax.dynamic_slice_in_dim(factors, (quarter ^ step) * size, size, 1)

    moved = [from_peer(columns(step), QUARTER, step) for step in STEPS_AWAY[1:]]
    return columns(0), *moved


def basis_quarters(x, y):
    mine = jnp.concatenate([x, y])
    across = from_peer(mine, "y_lo", 1)
    return mine, across, from_sibling(mine), from_sibling(across)


def with_quarter(count):
    return [pl.BlockSpec(memory_space=m) for m in (pltpu.SMEM, *[pltpu.VMEM] * count)]


def gram_total(quarter, factors, parts, rank, beside=()):
    tiles = (lax.axis_size(ROW), RANK + rank // 2 // lax.axis_size(ROW), rank)
    mine, other = call(
        gram_and_cores,
        [tiles, tiles],
        quarter,
        *factors,
        *parts,
        in_specs=with_quarter(6),
        scratch_shapes=[pltpu.VMEM((rank, rank), jnp.float32)],
    )
    other, beside = lax.optimization_barrier((from_sibling(other), beside))
    return row_total(mine + other), beside


def local(b_factors, a_factors, u_start, v_start):
    shape = (*b_factors.shape[:2], u_start.shape[1])
    width, rank = u_start.shape
    place = lax.axis_index(QUARTER)
    quarter = jnp.reshape(place, (1,)).astype(jnp.int32)
    b = b_factors.reshape(-1, width)
    a = a_factors.reshape(-1, width)
    b_quarters, a_quarters = column_quarters(b, place), column_quarters(a, place)

    partial = call(
        projections,
        [(shape[0], 2 * RANK, rank)],
        *(pltpu.with_memory_space_constraint(x, pltpu.HBM) for x in (b, a, u_start, v_start)),
        in_specs=[pl.BlockSpec(memory_space=pltpu.HBM)] * 4,
        scratch_shapes=[
            *(pltpu.VMEM(x.shape, x.dtype) for x in (b, a, u_start, v_start)),
            pltpu.SemaphoreType.DMA((STEPS, 4)),
        ],
    )
    copies = (lax.axis_size(ROW), 2 * RANK, rank)
    pair = exchanged(call(owner_coefficients, [copies], exchanged(partial, "row")), ROW)
    pair_other = from_sibling(pair)

    part = (width // 8, rank)
    parts = call(
        load_sum, [part, part], quarter, *b_quarters, pair, pair_other, in_specs=with_quarter(6)
    )
    parts = plane_total(*parts)
    basis = basis_quarters(*parts)
    mine, _ = gram_total(quarter, b_quarters, parts, rank)
    inverse, left, *parts = call(
        turn_over,
        [(rank, rank), shape, part, part],
        quarter,
        mine,
        from_sibling(mine),
        pair,
        pair_other,
        *a_quarters,
        in_specs=with_quarter(8),
        scratch_shapes=factor_scratch(rank),
    )
    u_scaled = call(
        left_basis,
        [(width, rank)],
        quarter,
        inverse,
        *basis,
        in_specs=with_quarter(5),
        cost_estimate=pl.CostEstimate(
            flops=6 * width * rank * rank, bytes_accessed=8 * width * rank, transcendentals=0
        ),
    )
    parts = plane_total(*parts)
    basis = basis_quarters(*parts)
    mine, u_scaled = gram_total(quarter, a_quarters, parts, rank, u_scaled)
    v_scaled, right = call(
        finish,
        [(width, rank), shape],
        quarter,
        mine,
        from_sibling(mine),
        *basis,
        in_specs=with_quarter(6),
        scratch_shapes=[pltpu.VMEM((rank, rank), jnp.float32), *factor_scratch(rank)],
    )
    return u_scaled, v_scaled, left, right


def solution(mesh):
    count, rows = mesh.devices.shape
    mesh = Mesh(mesh.devices.reshape(count // 4, 2, 2, rows), ("z", "y_lo", "core", "row"))
    tenant = ("z", "y_lo", "core")
    in_specs = (P(tenant, None, "row"), P(tenant, None, "row"), P("row", None), P("row", None))
    out_specs = (P("row", None), P("row", None), P(tenant, None, None), P(tenant, None, None))
    return jax.shard_map(local, mesh=mesh, in_specs=in_specs, out_specs=out_specs, check_vma=False)
```

```python
import math

import jax
import jax.numpy as jnp
from jax import lax
from jax.experimental import pallas as pl
from jax.experimental.pallas import tpu as pltpu
from jax.sharding import Mesh
from jax.sharding import PartitionSpec as P

D = 8192
RANK = 16
LANES = 128
SUBLANES = 8
PANEL = 32
STEPS = 4
ROW = ("y_lo", "row")
QUARTER = ("y_lo", "core")
STEPS_AWAY = (0, 2, 1, 3)


def pieces(x):
    high = x.astype(jnp.bfloat16)
    rest = x - high.astype(jnp.float32)
    middle = rest.astype(jnp.bfloat16)
    return high, middle, (rest - middle.astype(jnp.float32)).astype(jnp.bfloat16)


def float32_product(x, y):
    xh, xm, xl = pieces(x)
    yh, ym, yl = pieces(y)
    xs = jnp.concatenate([xh, xh, xm, xh, xl, xm])
    ys = jnp.concatenate([yh, ym, yh, yl, yh, ym])
    return lax.dot_general(xs, ys, (((0,), (0,)), ((), ())), preferred_element_type=jnp.float32)


def column(x, lane):
    return jnp.broadcast_to(x[:, lane : lane + 1], (SUBLANES, LANES))


def spread(ref, row):
    return ref[pl.ds(row, SUBLANES, stride=0), :]


def eliminate(rows, units, start, rows_ref, columns_ref, factors_ref):
    sub = lax.broadcasted_iota(jnp.int32, (SUBLANES, LANES), 0)
    tile = start // LANES
    for m, first in enumerate(range(start % LANES, start % LANES + PANEL, SUBLANES)):
        slot = m % 4
        tiles = [*rows[m], units[m]]
        if m == 0:
            pivots = [column(rows[m][tile], first + j) for j in range(SUBLANES)]
        for j in range(SUBLANES):
            columns_ref[slot, pl.ds(j * SUBLANES, SUBLANES), :] = pivots[j]
        for t, x in enumerate(tiles):
            rows_ref[slot, pl.ds(t * SUBLANES, SUBLANES), :] = x
        r = [
            [spread(rows_ref.at[slot], t * SUBLANES + i) for t in range(len(tiles))]
            for i in range(SUBLANES)
        ]
        d = [
            [spread(columns_ref.at[slot], j * SUBLANES + i) for j in range(SUBLANES)]
            for i in range(SUBLANES)
        ]
        later = range(m + 1, len(rows))
        c = {g: [column(rows[g][tile], first + j) for j in range(SUBLANES)] for g in later}
        if later:
            ahead = first + SUBLANES
            pivots = [column(rows[m + 1][tile], ahead + j) for j in range(SUBLANES)]
        done = tiles
        for j in range(SUBLANES):
            inverse = lax.rsqrt(d[j][j])
            p = [x * inverse for x in r[j]]
            done = [jnp.where(sub == j, x, y) for x, y in zip(p, done)]
            below = range(j + 1, SUBLANES)
            factor = {i: d[j][i] * inverse for i in below}
            for i in below:
                for other in range(i, SUBLANES):
                    d[i][other] -= factor[i] * factor[other]
                r[i] = [x - factor[i] * y for x, y in zip(r[i], p)]
            for g in later:
                scale = c[g][j] * inverse
                if g == m + 1:
                    place = pl.ds(j * SUBLANES, SUBLANES)
                    factors_ref[slot, place, :] = scale
                    for k in range(SUBLANES):
                        pivots[k] -= scale * spread(factors_ref.at[slot], j * SUBLANES + k)
                for i in below:
                    c[g][i] -= scale * factor[i]
                rows[g] = [x - scale * y for x, y in zip(rows[g], p)]
                units[g] -= scale * p[-1]
        rows[m], units[m] = done[:-1], done[-1]
    rows = [jnp.concatenate(tiles, axis=1) for tiles in rows]
    return jnp.concatenate(rows), jnp.concatenate(units)


def split(x):
    high = x.astype(jnp.bfloat16)
    return high, (x - high.astype(jnp.float32)).astype(jnp.bfloat16)


def product(x, y, x_dim=1, y_dim=0):
    dims = (((x_dim,), (y_dim,)), ((), ()))
    xh, xl = split(x)
    yh, yl = split(y)

    def part(p, q):
        return lax.dot_general(p, q, dims, preferred_element_type=jnp.float32)

    return part(xh, yh) + (part(xh, yl) + part(xl, yh))


def matrix(x):
    return x.reshape(-1, x.shape[-1])


def factor_in_place(out_ref, *scratch):
    n = out_ref.shape[0]
    sub = lax.broadcasted_iota(jnp.int32, (SUBLANES, LANES), 0)
    lane = lax.broadcasted_iota(jnp.int32, (SUBLANES, LANES), 1)
    column = lax.broadcasted_iota(jnp.int32, (n, n), 1)
    for start in range(0, n, PANEL):
        end = start + PANEL
        tile = start // LANES
        rows, units = [], []
        for g in range(0, PANEL, SUBLANES):
            place = pl.ds(start + g, SUBLANES)
            rows.append([out_ref[place, pl.ds(t, LANES)] for t in range(0, n, LANES)])
            units.append(jnp.where(lane == sub + (start % LANES + g), 1.0, 0.0))
        rows, units = eliminate(rows, units, start, *scratch)
        blank = jnp.zeros_like(units)
        units = jnp.concatenate([units if t == tile else blank for t in range(n // LANES)], axis=1)
        inside = (column >= start) & (column < end)
        solved = jnp.where(inside[:PANEL], units, rows)
        out_ref[pl.ds(start, PANEL), :] = jnp.where(column[:PANEL] < end, solved, 0.0)
        if end < n:
            aligned = end // LANES * LANES
            update = float32_product(rows[:, aligned:], solved)[end - aligned :]
            rest = out_ref[pl.ds(end, n - end), :]
            out_ref[pl.ds(end, n - end), :] = jnp.where(inside[end:], 0.0, rest) - update


def factor_scratch(n):
    tiles = n // LANES + 1
    return [
        pltpu.VMEM((4, tiles * SUBLANES, LANES), jnp.float32),
        pltpu.VMEM((4, SUBLANES * SUBLANES, LANES), jnp.float32),
        pltpu.VMEM((4, SUBLANES * SUBLANES, LANES), jnp.float32),
    ]


def call(kernel, shapes, *operands, **options):
    shapes = [jax.ShapeDtypeStruct(shape, jnp.float32) for shape in shapes]
    return pl.pallas_call(
        kernel,
        out_shape=shapes if len(shapes) > 1 else shapes[0],
        compiler_params=pltpu.CompilerParams(vmem_limit_bytes=32 << 20),
        name=kernel.__name__,
        **options,
    )(*operands)


def projections(b_hbm, a_hbm, u_hbm, v_hbm, out_ref, b_ref, a_ref, u_ref, v_ref, sems):
    step = b_ref.shape[1] // STEPS
    copies = []
    for i in range(STEPS):
        part = pl.ds(i * step, step)
        pairs = (
            (u_hbm.at[part], u_ref.at[part]),
            (b_hbm.at[:, part], b_ref.at[:, part]),
            (v_hbm.at[part], v_ref.at[part]),
            (a_hbm.at[:, part], a_ref.at[:, part]),
        )
        copies.append([pltpu.make_async_copy(*p, sems.at[i, k]) for k, p in enumerate(pairs)])
    for group in copies:
        for copy in group:
            copy.start()
    left = right = 0.0
    for i, group in enumerate(copies):
        part = pl.ds(i * step, step)
        group[0].wait()
        group[1].wait()
        left += product(b_ref[:, part], u_ref[part])
        group[2].wait()
        group[3].wait()
        right += product(a_ref[:, part], v_ref[part])
    out_ref[:, :RANK] = left.reshape(-1, RANK, left.shape[1])
    out_ref[:, RANK:] = right.reshape(-1, RANK, right.shape[1])


def owner_coefficients(tiles_ref, out_ref):
    total = jnp.sum(tiles_ref[...], axis=0)
    left, right = total[:RANK], total[RANK:]
    coeffs = product(product(right, right, 1, 1), left)
    out_ref[:, :RANK] = jnp.broadcast_to(coeffs, (len(out_ref), *coeffs.shape))
    out_ref[:, RANK:] = jnp.broadcast_to(right, (len(out_ref), *right.shape))


def owner_sum(tiles_ref, out_ref):
    out_ref[...] = jnp.broadcast_to(jnp.sum(tiles_ref[...], axis=0), out_ref.shape)


def stacked(refs):
    return jnp.concatenate([ref[...] for ref in refs])


def by_distance(quarter, ref):
    count = len(ref) // 2
    half = quarter // 2
    return [pl.ds(place * count, count) for place in (half, 1 - half)]


def tenants(quarter, refs, first):
    rows = pl.ds(first, RANK)
    tiles = [ref[place, rows] for ref in refs for place in by_distance(quarter, ref)]
    return jnp.concatenate([matrix(x) for x in tiles])


def load_sum(quarter_ref, f0, f1, f2, f3, mine_ref, other_ref, *out_refs):
    coeffs = tenants(quarter_ref[0], (mine_ref, other_ref), 0)
    store_load(product(stacked((f0, f1, f2, f3)), coeffs, 0, 0), out_refs)


def store_load(load, out_refs):
    count = len(out_refs[0])
    for i, ref in enumerate(out_refs):
        ref[...] = load[i * count : (i + 1) * count]


def gram_and_cores(quarter_ref, f0, f1, f2, f3, x_ref, y_ref, mine_ref, other_ref, gram_ref):
    basis = stacked((x_ref, y_ref))
    cores = product(stacked((f0, f1, f2, f3)), basis)
    gram_ref[...] = product(basis, basis, 0, 0)
    quarter = quarter_ref[0]
    core, half = quarter % 2, len(gram_ref) // 2
    block = len(cores) // 4
    for i, (ref, which) in enumerate(((mine_ref, core), (other_ref, 1 - core))):
        for j, place in enumerate(by_distance(quarter, ref)):
            rows = cores[(2 * i + j) * block : (2 * i + j + 1) * block]
            ref[place, :RANK] = rows.reshape(-1, RANK, rows.shape[1])
        rows = gram_ref[pl.ds(which * half, half), :]
        ref[:, RANK:] = rows.reshape(len(ref), -1, rows.shape[1])


def inverse_factor(core, mine_ref, other_ref, inverse_ref, *scratch):
    half = len(inverse_ref) // 2
    inverse_ref[pl.ds(core * half, half), :] = matrix(mine_ref[:, RANK:])
    inverse_ref[pl.ds((1 - core) * half, half), :] = matrix(other_ref[:, RANK:])
    factor_in_place(inverse_ref, *scratch)


def turn_over(
    quarter_ref, mine_ref, other_ref, pair_ref, pair_other_ref, f0, f1, f2, f3,
    inverse_ref, left_ref, x_ref, y_ref, *scratch,
):
    quarter = quarter_ref[0]
    inverse_factor(quarter % 2, mine_ref, other_ref, inverse_ref, *scratch)
    left = product(tenants(quarter, (mine_ref, other_ref), 0), inverse_ref[...], 1, 1)
    right = tenants(quarter, (pair_ref, pair_other_ref), RANK)
    own = left[: len(left) // 4]
    left_ref[...] = own.reshape(left_ref.shape)
    half = len(left) // 2
    tenant = [lax.broadcasted_iota(jnp.int32, (half, half), d) // RANK for d in range(2)]
    coeffs = []
    for part in (slice(0, half), slice(half, None)):
        weight = jnp.where(tenant[0] == tenant[1], product(left[part], left[part], 1, 1), 0.0)
        coeffs.append(product(weight, right[part]))
    load = product(stacked((f0, f1, f2, f3)), jnp.concatenate(coeffs), 0, 0)
    store_load(load, (x_ref, y_ref))


def scaled_basis(quarter, inverse, refs, out_ref):
    scale = math.sqrt(D)
    for step, ref in zip(STEPS_AWAY, refs):
        rows = pl.ds((quarter ^ step) * len(ref), len(ref))
        out_ref[rows, :] = product(ref[...], inverse, 1, 1) * scale


def left_basis(quarter_ref, inverse_ref, q0, q1, q2, q3, out_ref):
    scaled_basis(quarter_ref[0], inverse_ref[...], (q0, q1, q2, q3), out_ref)


def finish(
    quarter_ref, mine_ref, other_ref, q0, q1, q2, q3, out_ref, right_ref, inverse_ref, *scratch
):
    quarter = quarter_ref[0]
    inverse_factor(quarter % 2, mine_ref, other_ref, inverse_ref, *scratch)
    inverse = inverse_ref[...]
    own = matrix(mine_ref[by_distance(quarter, mine_ref)[0], :RANK])
    right_ref[...] = product(own, inverse, 1, 1).reshape(right_ref.shape)
    scaled_basis(quarter, inverse, (q0, q1, q2, q3), out_ref)


def exchanged(tiles, axis):
    return lax.all_to_all(tiles, axis, 0, 0, tiled=True)


def from_peer(x, axis, step):
    count = lax.axis_size(axis)
    return lax.ppermute(x, axis, [(i, i ^ step) for i in range(count)])


def together(x, others):
    return lax.optimization_barrier((x, others))


def row_total(tiles, parts, others):
    basis = jnp.concatenate(parts)
    tiles, across = together(exchanged(tiles, ROW), from_peer(basis, "y_lo", 1))
    whole = exchanged(call(owner_sum, [tiles.shape], tiles), ROW)
    quarters = (from_sibling(basis), from_sibling(across))
    whole, (quarters, others) = together(whole, (quarters, others))
    return whole, (basis, across, *quarters), others


def plane_total(x, y):
    for x_step, y_step in ((1, 3), (3, 1)):
        x, y = x + from_peer(x, "z", x_step), y + from_peer(y, "z", y_step)
    return x, y


def from_sibling(x):
    return from_peer(x, "core", 1)


def column_quarters(factors, quarter):
    size = factors.shape[1] // 4

    def columns(step):
        return lax.dynamic_slice_in_dim(factors, (quarter ^ step) * size, size, 1)

    moved = [from_peer(columns(step), QUARTER, step) for step in STEPS_AWAY[1:]]
    return columns(0), *moved


def with_quarter(count):
    return [pl.BlockSpec(memory_space=m) for m in (pltpu.SMEM, *[pltpu.VMEM] * count)]


def gram_total(quarter, factors, parts, rank, beside=(), others=()):
    tiles = (lax.axis_size(ROW), RANK + rank // 2 // lax.axis_size(ROW), rank)
    mine, other = call(
        gram_and_cores,
        [tiles, tiles],
        quarter,
        *factors,
        *parts,
        in_specs=with_quarter(6),
        scratch_shapes=[pltpu.VMEM((rank, rank), jnp.float32)],
    )
    other, beside = together(from_sibling(other), beside)
    return *row_total(mine + other, parts, others), beside


def local(b_factors, a_factors, u_start, v_start):
    shape = (*b_factors.shape[:2], u_start.shape[1])
    width, rank = u_start.shape
    place = lax.axis_index(QUARTER)
    quarter = jnp.reshape(place, (1,)).astype(jnp.int32)
    b = b_factors.reshape(-1, width)
    a = a_factors.reshape(-1, width)
    b_quarters, a_quarters = column_quarters(b, place), column_quarters(a, place)

    partial = call(
        projections,
        [(shape[0], 2 * RANK, rank)],
        *(pltpu.with_memory_space_constraint(x, pltpu.HBM) for x in (b, a, u_start, v_start)),
        in_specs=[pl.BlockSpec(memory_space=pltpu.HBM)] * 4,
        scratch_shapes=[
            *(pltpu.VMEM(x.shape, x.dtype) for x in (b, a, u_start, v_start)),
            pltpu.SemaphoreType.DMA((STEPS, 4)),
        ],
    )
    copies = (lax.axis_size(ROW), 2 * RANK, rank)
    pair = exchanged(call(owner_coefficients, [copies], exchanged(partial, "row")), ROW)
    pair, b_quarters = together(pair, b_quarters)
    pair_other = from_sibling(pair)

    part = (width // 8, rank)
    parts = call(
        load_sum, [part, part], quarter, *b_quarters, pair, pair_other, in_specs=with_quarter(6)
    )
    parts = plane_total(*parts)
    mine, basis, a_quarters, _ = gram_total(
        quarter, b_quarters, parts, rank, others=a_quarters
    )
    inverse, left, *parts = call(
        turn_over,
        [(rank, rank), shape, part, part],
        quarter,
        mine,
        from_sibling(mine),
        pair,
        pair_other,
        *a_quarters,
        in_specs=with_quarter(8),
        scratch_shapes=factor_scratch(rank),
    )
    u_scaled = call(
        left_basis,
        [(width, rank)],
        quarter,
        inverse,
        *basis,
        in_specs=with_quarter(5),
        cost_estimate=pl.CostEstimate(
            flops=6 * width * rank * rank, bytes_accessed=8 * width * rank, transcendentals=0
        ),
    )
    parts = plane_total(*parts)
    mine, basis, _, u_scaled = gram_total(quarter, a_quarters, parts, rank, u_scaled)
    v_scaled, right = call(
        finish,
        [(width, rank), shape],
        quarter,
        mine,
        from_sibling(mine),
        *basis,
        in_specs=with_quarter(6),
        scratch_shapes=[pltpu.VMEM((rank, rank), jnp.float32), *factor_scratch(rank)],
    )
    return u_scaled, v_scaled, left, right


def solution(mesh):
    count, rows = mesh.devices.shape
    mesh = Mesh(mesh.devices.reshape(count // 4, 2, 2, rows), ("z", "y_lo", "core", "row"))
    tenant = ("z", "y_lo", "core")
    in_specs = (P(tenant, None, "row"), P(tenant, None, "row"), P("row", None), P("row", None))
    out_specs = (P("row", None), P("row", None), P(tenant, None, None), P(tenant, None, None))
    return jax.shard_map(local, mesh=mesh, in_specs=in_specs, out_specs=out_specs, check_vma=False)
```

```python
import math

import jax
import jax.numpy as jnp
from jax import lax
from jax.experimental import pallas as pl
from jax.experimental.pallas import tpu as pltpu
from jax.sharding import Mesh
from jax.sharding import PartitionSpec as P

D = 8192
RANK = 16
LANES = 128
SUBLANES = 8
PANEL = 32
STEPS = 4
ROW = ("z_lo", "row")
STEPS_AWAY = (0, 2, 1, 3)


def pieces(x):
    high = x.astype(jnp.bfloat16)
    rest = x - high.astype(jnp.float32)
    middle = rest.astype(jnp.bfloat16)
    return high, middle, (rest - middle.astype(jnp.float32)).astype(jnp.bfloat16)


def float32_product(x, y):
    xh, xm, xl = pieces(x)
    yh, ym, yl = pieces(y)
    xs = jnp.concatenate([xh, xh, xm, xh, xl, xm])
    ys = jnp.concatenate([yh, ym, yh, yl, yh, ym])
    return lax.dot_general(xs, ys, (((0,), (0,)), ((), ())), preferred_element_type=jnp.float32)


def column(x, lane):
    return jnp.broadcast_to(x[:, lane : lane + 1], (SUBLANES, LANES))


def spread(ref, row):
    return ref[pl.ds(row, SUBLANES, stride=0), :]


def eliminate(rows, units, start, rows_ref, columns_ref, factors_ref):
    sub = lax.broadcasted_iota(jnp.int32, (SUBLANES, LANES), 0)
    tile = start // LANES
    for m, first in enumerate(range(start % LANES, start % LANES + PANEL, SUBLANES)):
        slot = m % 4
        tiles = [*rows[m], units[m]]
        if m == 0:
            pivots = [column(rows[m][tile], first + j) for j in range(SUBLANES)]
        for j in range(SUBLANES):
            columns_ref[slot, pl.ds(j * SUBLANES, SUBLANES), :] = pivots[j]
        for t, x in enumerate(tiles):
            rows_ref[slot, pl.ds(t * SUBLANES, SUBLANES), :] = x
        r = [
            [spread(rows_ref.at[slot], t * SUBLANES + i) for t in range(len(tiles))]
            for i in range(SUBLANES)
        ]
        d = [
            [spread(columns_ref.at[slot], j * SUBLANES + i) for j in range(SUBLANES)]
            for i in range(SUBLANES)
        ]
        later = range(m + 1, len(rows))
        c = {g: [column(rows[g][tile], first + j) for j in range(SUBLANES)] for g in later}
        if later:
            ahead = first + SUBLANES
            pivots = [column(rows[m + 1][tile], ahead + j) for j in range(SUBLANES)]
        done = tiles
        for j in range(SUBLANES):
            inverse = lax.rsqrt(d[j][j])
            p = [x * inverse for x in r[j]]
            done = [jnp.where(sub == j, x, y) for x, y in zip(p, done)]
            below = range(j + 1, SUBLANES)
            factor = {i: d[j][i] * inverse for i in below}
            for i in below:
                for other in range(i, SUBLANES):
                    d[i][other] -= factor[i] * factor[other]
                r[i] = [x - factor[i] * y for x, y in zip(r[i], p)]
            for g in later:
                scale = c[g][j] * inverse
                if g == m + 1:
                    place = pl.ds(j * SUBLANES, SUBLANES)
                    factors_ref[slot, place, :] = scale
                    for k in range(SUBLANES):
                        pivots[k] -= scale * spread(factors_ref.at[slot], j * SUBLANES + k)
                for i in below:
                    c[g][i] -= scale * factor[i]
                rows[g] = [x - scale * y for x, y in zip(rows[g], p)]
                units[g] -= scale * p[-1]
        rows[m], units[m] = done[:-1], done[-1]
    rows = [jnp.concatenate(tiles, axis=1) for tiles in rows]
    return jnp.concatenate(rows), jnp.concatenate(units)


def split(x):
    high = x.astype(jnp.bfloat16)
    return high, (x - high.astype(jnp.float32)).astype(jnp.bfloat16)


def product(x, y, x_dim=1, y_dim=0):
    dims = (((x_dim,), (y_dim,)), ((), ()))
    xh, xl = split(x)
    yh, yl = split(y)

    def part(p, q):
        return lax.dot_general(p, q, dims, preferred_element_type=jnp.float32)

    return part(xh, yh) + (part(xh, yl) + part(xl, yh))


def matrix(x):
    return x.reshape(-1, x.shape[-1])


def factor_in_place(out_ref, *scratch):
    n = out_ref.shape[0]
    sub = lax.broadcasted_iota(jnp.int32, (SUBLANES, LANES), 0)
    lane = lax.broadcasted_iota(jnp.int32, (SUBLANES, LANES), 1)
    column = lax.broadcasted_iota(jnp.int32, (n, n), 1)
    for start in range(0, n, PANEL):
        end = start + PANEL
        tile = start // LANES
        rows, units = [], []
        for g in range(0, PANEL, SUBLANES):
            place = pl.ds(start + g, SUBLANES)
            rows.append([out_ref[place, pl.ds(t, LANES)] for t in range(0, n, LANES)])
            units.append(jnp.where(lane == sub + (start % LANES + g), 1.0, 0.0))
        rows, units = eliminate(rows, units, start, *scratch)
        blank = jnp.zeros_like(units)
        units = jnp.concatenate([units if t == tile else blank for t in range(n // LANES)], axis=1)
        inside = (column >= start) & (column < end)
        solved = jnp.where(inside[:PANEL], units, rows)
        out_ref[pl.ds(start, PANEL), :] = jnp.where(column[:PANEL] < end, solved, 0.0)
        if end < n:
            aligned = end // LANES * LANES
            update = float32_product(rows[:, aligned:], solved)[end - aligned :]
            rest = out_ref[pl.ds(end, n - end), :]
            out_ref[pl.ds(end, n - end), :] = jnp.where(inside[end:], 0.0, rest) - update


def factor_scratch(n):
    tiles = n // LANES + 1
    return [
        pltpu.VMEM((4, tiles * SUBLANES, LANES), jnp.float32),
        pltpu.VMEM((4, SUBLANES * SUBLANES, LANES), jnp.float32),
        pltpu.VMEM((4, SUBLANES * SUBLANES, LANES), jnp.float32),
    ]


def call(kernel, shapes, *operands, **options):
    shapes = [jax.ShapeDtypeStruct(shape, jnp.float32) for shape in shapes]
    return pl.pallas_call(
        kernel,
        out_shape=shapes if len(shapes) > 1 else shapes[0],
        compiler_params=pltpu.CompilerParams(vmem_limit_bytes=32 << 20),
        name=kernel.__name__,
        **options,
    )(*operands)


def projections(b_hbm, a_hbm, u_hbm, v_hbm, out_ref, b_ref, a_ref, u_ref, v_ref, sems):
    step = b_ref.shape[1] // STEPS
    copies = []
    for i in range(STEPS):
        part = pl.ds(i * step, step)
        pairs = (
            (u_hbm.at[part], u_ref.at[part]),
            (b_hbm.at[:, part], b_ref.at[:, part]),
            (v_hbm.at[part], v_ref.at[part]),
            (a_hbm.at[:, part], a_ref.at[:, part]),
        )
        copies.append([pltpu.make_async_copy(*p, sems.at[i, k]) for k, p in enumerate(pairs)])
    for group in copies:
        for copy in group:
            copy.start()
    left = right = 0.0
    for i, group in enumerate(copies):
        part = pl.ds(i * step, step)
        group[0].wait()
        group[1].wait()
        left += product(b_ref[:, part], u_ref[part])
        group[2].wait()
        group[3].wait()
        right += product(a_ref[:, part], v_ref[part])
    out_ref[:, :RANK] = left.reshape(-1, RANK, left.shape[1])
    out_ref[:, RANK:] = right.reshape(-1, RANK, right.shape[1])


def owner_coefficients(tiles_ref, out_ref):
    total = jnp.sum(tiles_ref[...], axis=0)
    left, right = total[:RANK], total[RANK:]
    coeffs = product(product(right, right, 1, 1), left)
    out_ref[:, :RANK] = jnp.broadcast_to(coeffs, (len(out_ref), *coeffs.shape))
    out_ref[:, RANK:] = jnp.broadcast_to(right, (len(out_ref), *right.shape))


def owner_sum(tiles_ref, out_ref):
    out_ref[...] = jnp.broadcast_to(jnp.sum(tiles_ref[...], axis=0), out_ref.shape)


def stacked(refs):
    return jnp.concatenate([ref[...] for ref in refs])


def by_distance(pair, ref):
    count = len(ref) // 2
    return [pl.ds(place * count, count) for place in (pair, 1 - pair)]


def tenants(pair, refs, first):
    rows = pl.ds(first, RANK)
    tiles = [ref[place, rows] for ref in refs for place in by_distance(pair, ref)]
    return jnp.concatenate([matrix(x) for x in tiles])


def load_sum(place_ref, f0, f1, f2, mine_ref, other_ref, *out_refs):
    coeffs = tenants(place_ref[1], (mine_ref, other_ref), 0)
    store_load(product(stacked((f0, f1, f2)), coeffs, 0, 0), out_refs)


def store_load(load, out_refs):
    count = len(out_refs[0])
    for i, ref in enumerate(out_refs):
        ref[...] = load[i * count : (i + 1) * count]


def gram_and_cores(place_ref, f0, f1, f2, x_ref, y_ref, mine_ref, other_ref, gram_ref):
    basis = stacked((x_ref, y_ref))
    cores = product(stacked((f0, f1, f2)), basis)
    gram_ref[...] = product(basis, basis, 0, 0)
    core, half = place_ref[0] % 2, len(gram_ref) // 2
    block = len(cores) // 4
    for i, (ref, which) in enumerate(((mine_ref, core), (other_ref, 1 - core))):
        for j, place in enumerate(by_distance(place_ref[1], ref)):
            rows = cores[(2 * i + j) * block : (2 * i + j + 1) * block]
            ref[place, :RANK] = rows.reshape(-1, RANK, rows.shape[1])
        rows = gram_ref[pl.ds(which * half, half), :]
        ref[:, RANK:] = rows.reshape(len(ref), -1, rows.shape[1])


def inverse_factor(core, mine_ref, other_ref, inverse_ref, *scratch):
    half = len(inverse_ref) // 2
    inverse_ref[pl.ds(core * half, half), :] = matrix(mine_ref[:, RANK:])
    inverse_ref[pl.ds((1 - core) * half, half), :] = matrix(other_ref[:, RANK:])
    factor_in_place(inverse_ref, *scratch)


def turn_over(
    place_ref, mine_ref, other_ref, pair_ref, pair_other_ref, f0, f1, f2,
    inverse_ref, left_ref, x_ref, y_ref, *scratch,
):
    pair = place_ref[1]
    inverse_factor(place_ref[0] % 2, mine_ref, other_ref, inverse_ref, *scratch)
    left = product(tenants(pair, (mine_ref, other_ref), 0), inverse_ref[...], 1, 1)
    right = tenants(pair, (pair_ref, pair_other_ref), RANK)
    own = left[: len(left) // 4]
    left_ref[...] = own.reshape(left_ref.shape)
    half = len(left) // 2
    tenant = [lax.broadcasted_iota(jnp.int32, (half, half), d) // RANK for d in range(2)]
    coeffs = []
    for part in (slice(0, half), slice(half, None)):
        weight = jnp.where(tenant[0] == tenant[1], product(left[part], left[part], 1, 1), 0.0)
        coeffs.append(product(weight, right[part]))
    load = product(stacked((f0, f1, f2)), jnp.concatenate(coeffs), 0, 0)
    store_load(load, (x_ref, y_ref))


def scaled_basis(quarter, inverse, refs, out_ref):
    scale = math.sqrt(D)
    for step, ref in zip(STEPS_AWAY, refs):
        rows = pl.ds((quarter ^ step) * len(ref), len(ref))
        out_ref[rows, :] = product(ref[...], inverse, 1, 1) * scale


def left_basis(place_ref, inverse_ref, q0, q1, q2, q3, out_ref):
    scaled_basis(place_ref[0], inverse_ref[...], (q0, q1, q2, q3), out_ref)


def finish(
    place_ref, mine_ref, other_ref, q0, q1, q2, q3, out_ref, right_ref, inverse_ref, *scratch
):
    quarter = place_ref[0]
    inverse_factor(quarter % 2, mine_ref, other_ref, inverse_ref, *scratch)
    inverse = inverse_ref[...]
    own = matrix(mine_ref[by_distance(place_ref[1], mine_ref)[0], :RANK])
    right_ref[...] = product(own, inverse, 1, 1).reshape(right_ref.shape)
    scaled_basis(quarter, inverse, (q0, q1, q2, q3), out_ref)


def exchanged(tiles, axis):
    return lax.all_to_all(tiles, axis, 0, 0, tiled=True)


def from_peer(x, axis, step):
    count = lax.axis_size(axis)
    return lax.ppermute(x, axis, [(i, i ^ step) for i in range(count)])


def together(x, others):
    return lax.optimization_barrier((x, others))


def from_sibling(x):
    return from_peer(x, "core", 1)


def across(x):
    return from_peer(x, "z_lo", 1)


def plane_total(x, y):
    orders = (((("z_hi", "z_lo"), 3), ("y_lo", 1)), (("y_lo", 1), (("z_hi", "z_lo"), 3)))
    for x_step, y_step in zip(*orders):
        x, y = x + from_peer(x, *x_step), y + from_peer(y, *y_step)
    return x, y


def column_half(factors, bit):
    half = factors.shape[1] // 2
    mine, its = (
        lax.dynamic_slice_in_dim(factors, which * half, half, 1) for which in (bit, 1 - bit)
    )
    return mine, across(its)


def column_quarter(halves, core):
    size = halves[0].shape[1] // 2

    def columns(which):
        return [lax.dynamic_slice_in_dim(x, which * size, size, 1) for x in halves]

    return *columns(core), from_sibling(jnp.concatenate(columns(1 - core)))


def with_place(count):
    return [pl.BlockSpec(memory_space=m) for m in (pltpu.SMEM, *[pltpu.VMEM] * count)]


def work(products, size):
    return pl.CostEstimate(flops=6 * products * size**3, bytes_accessed=0, transcendentals=0)


def gram_tiles(place, factors, parts, rank, beside):
    tiles = (lax.axis_size(ROW), RANK + rank // 2 // lax.axis_size(ROW), rank)
    mine, other = call(
        gram_and_cores,
        [tiles, tiles],
        place,
        *factors,
        *parts,
        in_specs=with_place(5),
        scratch_shapes=[pltpu.VMEM((rank, rank), jnp.float32)],
    )
    other, beside = together(from_sibling(other), beside)
    return mine + other, beside


def row_total(tiles):
    tiles = exchanged(tiles, ROW)
    return exchanged(call(owner_sum, [tiles.shape], tiles), ROW)


def local(b_factors, a_factors, u_start, v_start):
    shape = (*b_factors.shape[:2], u_start.shape[1])
    width, rank = u_start.shape
    pair_index, core = lax.axis_index("z_lo"), lax.axis_index("core")
    bit = pair_index ^ lax.axis_index("z_hi")
    place = jnp.stack([2 * bit + core, pair_index]).astype(jnp.int32)
    b = b_factors.reshape(-1, width)
    a = a_factors.reshape(-1, width)
    b_half, a_half = column_half(b, bit), column_half(a, bit)

    partial = call(
        projections,
        [(shape[0], 2 * RANK, rank)],
        *(pltpu.with_memory_space_constraint(x, pltpu.HBM) for x in (b, a, u_start, v_start)),
        in_specs=[pl.BlockSpec(memory_space=pltpu.HBM)] * 4,
        scratch_shapes=[
            *(pltpu.VMEM(x.shape, x.dtype) for x in (b, a, u_start, v_start)),
            pltpu.SemaphoreType.DMA((STEPS, 4)),
        ],
    )
    copies = (lax.axis_size(ROW), 2 * RANK, rank)
    tiles, (b_half, a_half) = together(exchanged(partial, "row"), (b_half, a_half))
    b_quarter, a_quarter = column_quarter(b_half, core), column_quarter(a_half, core)
    pair = exchanged(call(owner_coefficients, [copies], tiles), ROW)
    pair, (b_quarter, a_quarter) = together(pair, (b_quarter, a_quarter))
    pair_other = from_sibling(pair)

    part = (width // 8, rank)
    parts = call(
        load_sum, [part, part], place, *b_quarter, pair, pair_other, in_specs=with_place(5)
    )
    parts = plane_total(*parts)
    basis = jnp.concatenate(parts)
    tiles, _ = gram_tiles(place, b_quarter, parts, rank, ())
    mine = row_total(tiles)
    inverse, left, *parts = call(
        turn_over,
        [(rank, rank), shape, part, part],
        place,
        mine,
        from_sibling(mine),
        pair,
        pair_other,
        *a_quarter,
        in_specs=with_place(7),
        scratch_shapes=factor_scratch(rank),
        cost_estimate=work(64, rank),
    )
    parts, moved = together(parts, across(basis))
    parts = plane_total(*parts)
    u_scaled = call(
        left_basis,
        [(width, rank)],
        place,
        inverse,
        basis,
        moved,
        from_sibling(basis),
        from_sibling(moved),
        in_specs=with_place(5),
        cost_estimate=work(4, rank),
    )
    basis = jnp.concatenate(parts)
    tiles, (u_scaled, moved) = gram_tiles(place, a_quarter, parts, rank, (u_scaled, across(basis)))
    mine = row_total(tiles)
    mine, siblings = together(mine, (from_sibling(basis), from_sibling(moved)))
    v_scaled, right = call(
        finish,
        [(width, rank), shape],
        place,
        mine,
        from_sibling(mine),
        basis,
        moved,
        *siblings,
        in_specs=with_place(6),
        scratch_shapes=[pltpu.VMEM((rank, rank), jnp.float32), *factor_scratch(rank)],
    )
    return u_scaled, v_scaled, left, right


def solution(mesh):
    count, rows = mesh.devices.shape
    mesh = Mesh(
        mesh.devices.reshape(count // 8, 2, 2, 2, rows), ("z_hi", "z_lo", "y_lo", "core", "row")
    )
    tenant = ("z_hi", "z_lo", "y_lo", "core")
    in_specs = (P(tenant, None, "row"), P(tenant, None, "row"), P("row", None), P("row", None))
    out_specs = (P("row", None), P("row", None), P(tenant, None, None), P(tenant, None, None))
    return jax.shard_map(local, mesh=mesh, in_specs=in_specs, out_specs=out_specs, check_vma=False)
```

```python
import math

import jax
import jax.numpy as jnp
from jax import lax
from jax.experimental import pallas as pl
from jax.experimental.pallas import tpu as pltpu
from jax.sharding import Mesh
from jax.sharding import PartitionSpec as P

D = 8192
RANK = 16
LANES = 128
SUBLANES = 8
PANEL = 32
STEPS = 4
ROW = ("z_lo", "row")
STEPS_AWAY = (0, 2, 1, 3)


def pieces(x):
    high = x.astype(jnp.bfloat16)
    rest = x - high.astype(jnp.float32)
    middle = rest.astype(jnp.bfloat16)
    return high, middle, (rest - middle.astype(jnp.float32)).astype(jnp.bfloat16)


def float32_product(x, y):
    xh, xm, xl = pieces(x)
    yh, ym, yl = pieces(y)
    xs = jnp.concatenate([xh, xh, xm, xh, xl, xm])
    ys = jnp.concatenate([yh, ym, yh, yl, yh, ym])
    return lax.dot_general(xs, ys, (((0,), (0,)), ((), ())), preferred_element_type=jnp.float32)


def column(x, lane):
    return jnp.broadcast_to(x[:, lane : lane + 1], (SUBLANES, LANES))


def spread(ref, row):
    return ref[pl.ds(row, SUBLANES, stride=0), :]


def eliminate(rows, units, start, rows_ref, columns_ref, factors_ref):
    sub = lax.broadcasted_iota(jnp.int32, (SUBLANES, LANES), 0)
    tile = start // LANES
    for m, first in enumerate(range(start % LANES, start % LANES + PANEL, SUBLANES)):
        slot = m % 4
        tiles = [*rows[m], units[m]]
        if m == 0:
            pivots = [column(rows[m][tile], first + j) for j in range(SUBLANES)]
        for j in range(SUBLANES):
            columns_ref[slot, pl.ds(j * SUBLANES, SUBLANES), :] = pivots[j]
        for t, x in enumerate(tiles):
            rows_ref[slot, pl.ds(t * SUBLANES, SUBLANES), :] = x
        r = [
            [spread(rows_ref.at[slot], t * SUBLANES + i) for t in range(len(tiles))]
            for i in range(SUBLANES)
        ]
        d = [
            [spread(columns_ref.at[slot], j * SUBLANES + i) for j in range(SUBLANES)]
            for i in range(SUBLANES)
        ]
        later = range(m + 1, len(rows))
        c = {g: [column(rows[g][tile], first + j) for j in range(SUBLANES)] for g in later}
        if later:
            ahead = first + SUBLANES
            pivots = [column(rows[m + 1][tile], ahead + j) for j in range(SUBLANES)]
        done = tiles
        for j in range(SUBLANES):
            inverse = lax.rsqrt(d[j][j])
            p = [x * inverse for x in r[j]]
            done = [jnp.where(sub == j, x, y) for x, y in zip(p, done)]
            below = range(j + 1, SUBLANES)
            factor = {i: d[j][i] * inverse for i in below}
            for i in below:
                for other in range(i, SUBLANES):
                    d[i][other] -= factor[i] * factor[other]
                r[i] = [x - factor[i] * y for x, y in zip(r[i], p)]
            for g in later:
                scale = c[g][j] * inverse
                if g == m + 1:
                    place = pl.ds(j * SUBLANES, SUBLANES)
                    factors_ref[slot, place, :] = scale
                    for k in range(SUBLANES):
                        pivots[k] -= scale * spread(factors_ref.at[slot], j * SUBLANES + k)
                for i in below:
                    c[g][i] -= scale * factor[i]
                rows[g] = [x - scale * y for x, y in zip(rows[g], p)]
                units[g] -= scale * p[-1]
        rows[m], units[m] = done[:-1], done[-1]
    rows = [jnp.concatenate(tiles, axis=1) for tiles in rows]
    return jnp.concatenate(rows), jnp.concatenate(units)


def split(x):
    high = x.astype(jnp.bfloat16)
    return high, (x - high.astype(jnp.float32)).astype(jnp.bfloat16)


def product(x, y, x_dim=1, y_dim=0):
    dims = (((x_dim,), (y_dim,)), ((), ()))
    xh, xl = split(x)
    yh, yl = split(y)

    def part(p, q):
        return lax.dot_general(p, q, dims, preferred_element_type=jnp.float32)

    return part(xh, yh) + (part(xh, yl) + part(xl, yh))


def matrix(x):
    return x.reshape(-1, x.shape[-1])


def factor_in_place(out_ref, *scratch):
    n = out_ref.shape[0]
    sub = lax.broadcasted_iota(jnp.int32, (SUBLANES, LANES), 0)
    lane = lax.broadcasted_iota(jnp.int32, (SUBLANES, LANES), 1)
    column = lax.broadcasted_iota(jnp.int32, (n, n), 1)
    for start in range(0, n, PANEL):
        end = start + PANEL
        tile = start // LANES
        rows, units = [], []
        for g in range(0, PANEL, SUBLANES):
            place = pl.ds(start + g, SUBLANES)
            rows.append([out_ref[place, pl.ds(t, LANES)] for t in range(0, n, LANES)])
            units.append(jnp.where(lane == sub + (start % LANES + g), 1.0, 0.0))
        rows, units = eliminate(rows, units, start, *scratch)
        blank = jnp.zeros_like(units)
        units = jnp.concatenate([units if t == tile else blank for t in range(n // LANES)], axis=1)
        inside = (column >= start) & (column < end)
        solved = jnp.where(inside[:PANEL], units, rows)
        out_ref[pl.ds(start, PANEL), :] = jnp.where(column[:PANEL] < end, solved, 0.0)
        if end < n:
            aligned = end // LANES * LANES
            update = float32_product(rows[:, aligned:], solved)[end - aligned :]
            rest = out_ref[pl.ds(end, n - end), :]
            out_ref[pl.ds(end, n - end), :] = jnp.where(inside[end:], 0.0, rest) - update


def factor_scratch(n):
    tiles = n // LANES + 1
    return [
        pltpu.VMEM((4, tiles * SUBLANES, LANES), jnp.float32),
        pltpu.VMEM((4, SUBLANES * SUBLANES, LANES), jnp.float32),
        pltpu.VMEM((4, SUBLANES * SUBLANES, LANES), jnp.float32),
    ]


def call(kernel, shapes, *operands, **options):
    shapes = [jax.ShapeDtypeStruct(shape, jnp.float32) for shape in shapes]
    return pl.pallas_call(
        kernel,
        out_shape=shapes if len(shapes) > 1 else shapes[0],
        compiler_params=pltpu.CompilerParams(vmem_limit_bytes=32 << 20),
        name=kernel.__name__,
        **options,
    )(*operands)


def projections(b_hbm, a_hbm, u_hbm, v_hbm, out_ref, b_ref, a_ref, u_ref, v_ref, sems):
    step = b_ref.shape[1] // STEPS
    copies = []
    for i in range(STEPS):
        part = pl.ds(i * step, step)
        pairs = (
            (u_hbm.at[part], u_ref.at[part]),
            (b_hbm.at[:, part], b_ref.at[:, part]),
            (v_hbm.at[part], v_ref.at[part]),
            (a_hbm.at[:, part], a_ref.at[:, part]),
        )
        copies.append([pltpu.make_async_copy(*p, sems.at[i, k]) for k, p in enumerate(pairs)])
    for group in copies:
        for copy in group:
            copy.start()
    left = right = 0.0
    for i, group in enumerate(copies):
        part = pl.ds(i * step, step)
        group[0].wait()
        group[1].wait()
        left += product(b_ref[:, part], u_ref[part])
        group[2].wait()
        group[3].wait()
        right += product(a_ref[:, part], v_ref[part])
    out_ref[:, :RANK] = left.reshape(-1, RANK, left.shape[1])
    out_ref[:, RANK:] = right.reshape(-1, RANK, right.shape[1])


def owner_coefficients(tiles_ref, out_ref):
    total = jnp.sum(tiles_ref[...], axis=0)
    left, right = total[:RANK], total[RANK:]
    coeffs = product(product(right, right, 1, 1), left)
    out_ref[:, :RANK] = jnp.broadcast_to(coeffs, (len(out_ref), *coeffs.shape))
    out_ref[:, RANK:] = jnp.broadcast_to(right, (len(out_ref), *right.shape))


def owner_sum(tiles_ref, out_ref):
    out_ref[...] = jnp.broadcast_to(jnp.sum(tiles_ref[...], axis=0), out_ref.shape)


def stacked(refs):
    return jnp.concatenate([ref[...] for ref in refs])


def quarter_of(place_ref):
    return place_ref[0] // 2


def core_of(place_ref):
    return place_ref[0] // 2 % 2


def pair_of(place_ref):
    return place_ref[0] % 2


def by_distance(pair, ref):
    count = len(ref) // 2
    return [pl.ds(place * count, count) for place in (pair, 1 - pair)]


def tenants(pair, refs, first):
    rows = pl.ds(first, RANK)
    tiles = [ref[place, rows] for ref in refs for place in by_distance(pair, ref)]
    return jnp.concatenate([matrix(x) for x in tiles])


def load_sum(place_ref, f0, f1, f2, mine_ref, other_ref, *out_refs):
    coeffs = tenants(pair_of(place_ref), (mine_ref, other_ref), 0)
    store_load(product(stacked((f0, f1, f2)), coeffs, 0, 0), out_refs)


def store_load(load, out_refs):
    count = len(out_refs[0])
    for i, ref in enumerate(out_refs):
        ref[...] = load[i * count : (i + 1) * count]


def gram_and_cores(place_ref, f0, f1, f2, x_ref, y_ref, mine_ref, other_ref, gram_ref):
    basis = stacked((x_ref, y_ref))
    cores = product(stacked((f0, f1, f2)), basis)
    gram_ref[...] = product(basis, basis, 0, 0)
    core, half = core_of(place_ref), len(gram_ref) // 2
    block = len(cores) // 4
    for i, (ref, which) in enumerate(((mine_ref, core), (other_ref, 1 - core))):
        for j, place in enumerate(by_distance(pair_of(place_ref), ref)):
            rows = cores[(2 * i + j) * block : (2 * i + j + 1) * block]
            ref[place, :RANK] = rows.reshape(-1, RANK, rows.shape[1])
        rows = gram_ref[pl.ds(which * half, half), :]
        ref[:, RANK:] = rows.reshape(len(ref), -1, rows.shape[1])


def inverse_factor(core, mine_ref, other_ref, inverse_ref, *scratch):
    half = len(inverse_ref) // 2
    inverse_ref[pl.ds(core * half, half), :] = matrix(mine_ref[:, RANK:])
    inverse_ref[pl.ds((1 - core) * half, half), :] = matrix(other_ref[:, RANK:])
    factor_in_place(inverse_ref, *scratch)


def turn_over(
    place_ref, mine_ref, other_ref, pair_ref, pair_other_ref, f0, f1, f2,
    inverse_ref, left_ref, x_ref, y_ref, *scratch,
):
    pair = pair_of(place_ref)
    inverse_factor(core_of(place_ref), mine_ref, other_ref, inverse_ref, *scratch)
    left = product(tenants(pair, (mine_ref, other_ref), 0), inverse_ref[...], 1, 1)
    right = tenants(pair, (pair_ref, pair_other_ref), RANK)
    own = left[: len(left) // 4]
    left_ref[...] = own.reshape(left_ref.shape)
    half = len(left) // 2
    tenant = [lax.broadcasted_iota(jnp.int32, (half, half), d) // RANK for d in range(2)]
    coeffs = []
    for part in (slice(0, half), slice(half, None)):
        weight = jnp.where(tenant[0] == tenant[1], product(left[part], left[part], 1, 1), 0.0)
        coeffs.append(product(weight, right[part]))
    load = product(stacked((f0, f1, f2)), jnp.concatenate(coeffs), 0, 0)
    store_load(load, (x_ref, y_ref))


def scaled_basis(quarter, inverse, refs, out_ref):
    scale = math.sqrt(D)
    for step, ref in zip(STEPS_AWAY, refs):
        rows = pl.ds((quarter ^ step) * len(ref), len(ref))
        out_ref[rows, :] = product(ref[...], inverse, 1, 1) * scale


def left_basis(place_ref, inverse_ref, q0, q1, q2, q3, out_ref):
    scaled_basis(quarter_of(place_ref), inverse_ref[...], (q0, q1, q2, q3), out_ref)


def finish(
    place_ref, mine_ref, other_ref, q0, q1, q2, q3, out_ref, right_ref, inverse_ref, *scratch
):
    quarter = quarter_of(place_ref)
    inverse_factor(core_of(place_ref), mine_ref, other_ref, inverse_ref, *scratch)
    inverse = inverse_ref[...]
    own = matrix(mine_ref[by_distance(pair_of(place_ref), mine_ref)[0], :RANK])
    right_ref[...] = product(own, inverse, 1, 1).reshape(right_ref.shape)
    scaled_basis(quarter, inverse, (q0, q1, q2, q3), out_ref)


def exchanged(tiles, axis):
    return lax.all_to_all(tiles, axis, 0, 0, tiled=True)


def from_peer(x, axis, step):
    count = lax.axis_size(axis)
    return lax.ppermute(x, axis, [(i, i ^ step) for i in range(count)])


def together(x, others):
    return lax.optimization_barrier((x, others))


def from_sibling(x):
    return from_peer(x, "core", 1)


def across(x):
    return from_peer(x, "z_lo", 1)


def plane_total(x, y, besides):
    z, y_lo = (("z_hi", "z_lo"), 3), ("y_lo", 1)
    done = []
    for x_step, y_step, beside in zip((z, y_lo), (y_lo, z), besides):
        moved, beside = together((from_peer(x, *x_step), from_peer(y, *y_step)), beside)
        x, y = x + moved[0], y + moved[1]
        done.append(beside)
    return (x, y), done


def column_half(factors, bit):
    half = factors.shape[1] // 2
    mine, its = (
        lax.dynamic_slice_in_dim(factors, which * half, half, 1) for which in (bit, 1 - bit)
    )
    return mine, across(its)


def column_quarter(halves, core):
    size = halves[0].shape[1] // 2

    def columns(which):
        return [lax.dynamic_slice_in_dim(x, which * size, size, 1) for x in halves]

    return *columns(core), from_sibling(jnp.concatenate(columns(1 - core)))


def with_place(count):
    return [pl.BlockSpec(memory_space=m) for m in (pltpu.SMEM, *[pltpu.VMEM] * count)]


def work(products, size):
    return pl.CostEstimate(flops=6 * products * size**3, bytes_accessed=0, transcendentals=0)


def gram_tiles(place, factors, parts, rank, beside):
    tiles = (lax.axis_size(ROW), RANK + rank // 2 // lax.axis_size(ROW), rank)
    mine, other = call(
        gram_and_cores,
        [tiles, tiles],
        place,
        *factors,
        *parts,
        in_specs=with_place(5),
        scratch_shapes=[pltpu.VMEM((rank, rank), jnp.float32)],
    )
    other, beside = together(from_sibling(other), beside)
    return mine + other, beside


def row_total(tiles):
    tiles = exchanged(tiles, ROW)
    return exchanged(call(owner_sum, [tiles.shape], tiles), ROW)


def local(b_factors, a_factors, u_start, v_start):
    shape = (*b_factors.shape[:2], u_start.shape[1])
    width, rank = u_start.shape
    pair_index, core = lax.axis_index("z_lo"), lax.axis_index("core")
    bit = pair_index ^ lax.axis_index("z_hi")
    place = jnp.reshape(4 * bit + 2 * core + pair_index, (1,)).astype(jnp.int32)
    b = b_factors.reshape(-1, width)
    a = a_factors.reshape(-1, width)
    b_half = column_half(b, bit)

    partial = call(
        projections,
        [(shape[0], 2 * RANK, rank)],
        *(pltpu.with_memory_space_constraint(x, pltpu.HBM) for x in (b, a, u_start, v_start)),
        in_specs=[pl.BlockSpec(memory_space=pltpu.HBM)] * 4,
        scratch_shapes=[
            *(pltpu.VMEM(x.shape, x.dtype) for x in (b, a, u_start, v_start)),
            pltpu.SemaphoreType.DMA((STEPS, 4)),
        ],
    )
    copies = (lax.axis_size(ROW), 2 * RANK, rank)
    tiles, b_half = together(exchanged(partial, "row"), b_half)
    b_quarter = column_quarter(b_half, core)
    pair = exchanged(call(owner_coefficients, [copies], tiles), ROW)
    pair, b_quarter = together(pair, b_quarter)
    pair_other = from_sibling(pair)

    part = (width // 8, rank)
    parts = call(
        load_sum, [part, part], place, *b_quarter, pair, pair_other, in_specs=with_place(5)
    )
    parts, (_, a_half) = plane_total(*parts, ((), column_half(a, bit)))
    a_quarter = column_quarter(a_half, core)
    basis = jnp.concatenate(parts)
    tiles, _ = gram_tiles(place, b_quarter, parts, rank, ())
    mine, a_quarter = together(row_total(tiles), a_quarter)
    inverse, left, *parts = call(
        turn_over,
        [(rank, rank), shape, part, part],
        place,
        mine,
        from_sibling(mine),
        pair,
        pair_other,
        *a_quarter,
        in_specs=with_place(7),
        scratch_shapes=factor_scratch(rank),
        cost_estimate=work(64, rank),
    )
    parts, moved = together(parts, across(basis))
    u_scaled = call(
        left_basis,
        [(width, rank)],
        place,
        inverse,
        basis,
        moved,
        from_sibling(basis),
        from_sibling(moved),
        in_specs=with_place(5),
        cost_estimate=work(4, rank),
    )
    parts, (u_scaled, _) = plane_total(*parts, (u_scaled, ()))
    basis = jnp.concatenate(parts)
    tiles, moved = gram_tiles(place, a_quarter, parts, rank, across(basis))
    mine = row_total(tiles)
    mine, siblings = together(mine, (from_sibling(basis), from_sibling(moved)))
    v_scaled, right = call(
        finish,
        [(width, rank), shape],
        place,
        mine,
        from_sibling(mine),
        basis,
        moved,
        *siblings,
        in_specs=with_place(6),
        scratch_shapes=[pltpu.VMEM((rank, rank), jnp.float32), *factor_scratch(rank)],
    )
    return u_scaled, v_scaled, left, right


def solution(mesh):
    count, rows = mesh.devices.shape
    mesh = Mesh(
        mesh.devices.reshape(count // 8, 2, 2, 2, rows), ("z_hi", "z_lo", "y_lo", "core", "row")
    )
    tenant = ("z_hi", "z_lo", "y_lo", "core")
    in_specs = (P(tenant, None, "row"), P(tenant, None, "row"), P("row", None), P("row", None))
    out_specs = (P("row", None), P("row", None), P(tenant, None, None), P(tenant, None, None))
    return jax.shard_map(local, mesh=mesh, in_specs=in_specs, out_specs=out_specs, check_vma=False)
```

```python
import math

import jax
import jax.numpy as jnp
from jax import lax
from jax.experimental import pallas as pl
from jax.experimental.pallas import tpu as pltpu
from jax.sharding import Mesh
from jax.sharding import PartitionSpec as P

D = 8192
RANK = 16
LANES = 128
SUBLANES = 8
PANEL = 32
STEPS = 4
ROW = ("y_lo", "row")
STEPS_AWAY = (0, 2, 1, 3)


def pieces(x):
    high = x.astype(jnp.bfloat16)
    rest = x - high.astype(jnp.float32)
    middle = rest.astype(jnp.bfloat16)
    return high, middle, (rest - middle.astype(jnp.float32)).astype(jnp.bfloat16)


def float32_product(x, y):
    xh, xm, xl = pieces(x)
    yh, ym, yl = pieces(y)
    xs = jnp.concatenate([xh, xh, xm, xh, xl, xm])
    ys = jnp.concatenate([yh, ym, yh, yl, yh, ym])
    return lax.dot_general(xs, ys, (((0,), (0,)), ((), ())), preferred_element_type=jnp.float32)


def column(x, lane):
    return jnp.broadcast_to(x[:, lane : lane + 1], (SUBLANES, LANES))


def spread(ref, row):
    return ref[pl.ds(row, SUBLANES, stride=0), :]


def eliminate(rows, units, start, rows_ref, columns_ref, factors_ref):
    sub = lax.broadcasted_iota(jnp.int32, (SUBLANES, LANES), 0)
    tile = start // LANES
    for m, first in enumerate(range(start % LANES, start % LANES + PANEL, SUBLANES)):
        slot = m % 4
        tiles = [*rows[m], units[m]]
        if m == 0:
            pivots = [column(rows[m][tile], first + j) for j in range(SUBLANES)]
        for j in range(SUBLANES):
            columns_ref[slot, pl.ds(j * SUBLANES, SUBLANES), :] = pivots[j]
        for t, x in enumerate(tiles):
            rows_ref[slot, pl.ds(t * SUBLANES, SUBLANES), :] = x
        r = [
            [spread(rows_ref.at[slot], t * SUBLANES + i) for t in range(len(tiles))]
            for i in range(SUBLANES)
        ]
        d = [
            [spread(columns_ref.at[slot], j * SUBLANES + i) for j in range(SUBLANES)]
            for i in range(SUBLANES)
        ]
        later = range(m + 1, len(rows))
        c = {g: [column(rows[g][tile], first + j) for j in range(SUBLANES)] for g in later}
        if later:
            ahead = first + SUBLANES
            pivots = [column(rows[m + 1][tile], ahead + j) for j in range(SUBLANES)]
        done = tiles
        for j in range(SUBLANES):
            inverse = lax.rsqrt(d[j][j])
            p = [x * inverse for x in r[j]]
            done = [jnp.where(sub == j, x, y) for x, y in zip(p, done)]
            below = range(j + 1, SUBLANES)
            factor = {i: d[j][i] * inverse for i in below}
            for i in below:
                for other in range(i, SUBLANES):
                    d[i][other] -= factor[i] * factor[other]
                r[i] = [x - factor[i] * y for x, y in zip(r[i], p)]
            for g in later:
                scale = c[g][j] * inverse
                if g == m + 1:
                    place = pl.ds(j * SUBLANES, SUBLANES)
                    factors_ref[slot, place, :] = scale
                    for k in range(SUBLANES):
                        pivots[k] -= scale * spread(factors_ref.at[slot], j * SUBLANES + k)
                for i in below:
                    c[g][i] -= scale * factor[i]
                rows[g] = [x - scale * y for x, y in zip(rows[g], p)]
                units[g] -= scale * p[-1]
        rows[m], units[m] = done[:-1], done[-1]
    rows = [jnp.concatenate(tiles, axis=1) for tiles in rows]
    return jnp.concatenate(rows), jnp.concatenate(units)


def split(x):
    high = x.astype(jnp.bfloat16)
    return high, (x - high.astype(jnp.float32)).astype(jnp.bfloat16)


def product(x, y, x_dim=1, y_dim=0):
    dims = (((x_dim,), (y_dim,)), ((), ()))
    xh, xl = split(x)
    yh, yl = split(y)

    def part(p, q):
        return lax.dot_general(p, q, dims, preferred_element_type=jnp.float32)

    return part(xh, yh) + (part(xh, yl) + part(xl, yh))


def matrix(x):
    return x.reshape(-1, x.shape[-1])


def factor_in_place(out_ref, *scratch):
    n = out_ref.shape[0]
    sub = lax.broadcasted_iota(jnp.int32, (SUBLANES, LANES), 0)
    lane = lax.broadcasted_iota(jnp.int32, (SUBLANES, LANES), 1)
    column = lax.broadcasted_iota(jnp.int32, (n, n), 1)
    for start in range(0, n, PANEL):
        end = start + PANEL
        tile = start // LANES
        rows, units = [], []
        for g in range(0, PANEL, SUBLANES):
            place = pl.ds(start + g, SUBLANES)
            rows.append([out_ref[place, pl.ds(t, LANES)] for t in range(0, n, LANES)])
            units.append(jnp.where(lane == sub + (start % LANES + g), 1.0, 0.0))
        rows, units = eliminate(rows, units, start, *scratch)
        blank = jnp.zeros_like(units)
        units = jnp.concatenate([units if t == tile else blank for t in range(n // LANES)], axis=1)
        inside = (column >= start) & (column < end)
        solved = jnp.where(inside[:PANEL], units, rows)
        out_ref[pl.ds(start, PANEL), :] = jnp.where(column[:PANEL] < end, solved, 0.0)
        if end < n:
            aligned = end // LANES * LANES
            update = float32_product(rows[:, aligned:], solved)[end - aligned :]
            rest = out_ref[pl.ds(end, n - end), :]
            out_ref[pl.ds(end, n - end), :] = jnp.where(inside[end:], 0.0, rest) - update


def factor_scratch(n):
    tiles = n // LANES + 1
    return [
        pltpu.VMEM((4, tiles * SUBLANES, LANES), jnp.float32),
        pltpu.VMEM((4, SUBLANES * SUBLANES, LANES), jnp.float32),
        pltpu.VMEM((4, SUBLANES * SUBLANES, LANES), jnp.float32),
    ]


def call(kernel, shapes, *operands, **options):
    shapes = [jax.ShapeDtypeStruct(shape, jnp.float32) for shape in shapes]
    return pl.pallas_call(
        kernel,
        out_shape=shapes if len(shapes) > 1 else shapes[0],
        compiler_params=pltpu.CompilerParams(vmem_limit_bytes=32 << 20),
        name=kernel.__name__,
        **options,
    )(*operands)


def projections(b_hbm, a_hbm, u_hbm, v_hbm, out_ref, b_ref, a_ref, u_ref, v_ref, sems):
    step = b_ref.shape[1] // STEPS
    copies = []
    for i in range(STEPS):
        part = pl.ds(i * step, step)
        pairs = (
            (u_hbm.at[part], u_ref.at[part]),
            (b_hbm.at[:, part], b_ref.at[:, part]),
            (v_hbm.at[part], v_ref.at[part]),
            (a_hbm.at[:, part], a_ref.at[:, part]),
        )
        copies.append([pltpu.make_async_copy(*p, sems.at[i, k]) for k, p in enumerate(pairs)])
    for group in copies:
        for copy in group:
            copy.start()
    left = right = 0.0
    for i, group in enumerate(copies):
        part = pl.ds(i * step, step)
        group[0].wait()
        group[1].wait()
        left += product(b_ref[:, part], u_ref[part])
        group[2].wait()
        group[3].wait()
        right += product(a_ref[:, part], v_ref[part])
    out_ref[:, :RANK] = left.reshape(-1, RANK, left.shape[1])
    out_ref[:, RANK:] = right.reshape(-1, RANK, right.shape[1])


def owner_coefficients(tiles_ref, out_ref):
    total = jnp.sum(tiles_ref[...], axis=0)
    left, right = total[:RANK], total[RANK:]
    coeffs = product(product(right, right, 1, 1), left)
    out_ref[:, :RANK] = jnp.broadcast_to(coeffs, (len(out_ref), *coeffs.shape))
    out_ref[:, RANK:] = jnp.broadcast_to(right, (len(out_ref), *right.shape))


def owner_sum(tiles_ref, out_ref):
    out_ref[...] = jnp.broadcast_to(jnp.sum(tiles_ref[...], axis=0), out_ref.shape)


def stacked(refs):
    return jnp.concatenate([ref[...] for ref in refs])


def quarter_of(place_ref):
    return place_ref[0]


def core_of(place_ref):
    return place_ref[0] % 2


def pair_of(place_ref):
    return place_ref[0] // 2


def by_distance(pair, ref):
    count = len(ref) // 2
    return [pl.ds(place * count, count) for place in (pair, 1 - pair)]


def tenants(pair, refs, first):
    rows = pl.ds(first, RANK)
    tiles = [ref[place, rows] for ref in refs for place in by_distance(pair, ref)]
    return jnp.concatenate([matrix(x) for x in tiles])


def load_sum(place_ref, f0, f1, f2, mine_ref, other_ref, *out_refs):
    coeffs = tenants(pair_of(place_ref), (mine_ref, other_ref), 0)
    store_load(product(stacked((f0, f1, f2)), coeffs, 0, 0), out_refs)


def store_load(load, out_refs):
    count = len(out_refs[0])
    for i, ref in enumerate(out_refs):
        ref[...] = load[i * count : (i + 1) * count]


def gram_and_cores(place_ref, f0, f1, f2, x_ref, y_ref, mine_ref, other_ref, gram_ref):
    basis = stacked((x_ref, y_ref))
    cores = product(stacked((f0, f1, f2)), basis)
    gram_ref[...] = product(basis, basis, 0, 0)
    core, half = core_of(place_ref), len(gram_ref) // 2
    block = len(cores) // 4
    for i, (ref, which) in enumerate(((mine_ref, core), (other_ref, 1 - core))):
        for j, place in enumerate(by_distance(pair_of(place_ref), ref)):
            rows = cores[(2 * i + j) * block : (2 * i + j + 1) * block]
            ref[place, :RANK] = rows.reshape(-1, RANK, rows.shape[1])
        rows = gram_ref[pl.ds(which * half, half), :]
        ref[:, RANK:] = rows.reshape(len(ref), -1, rows.shape[1])


def inverse_factor(core, mine_ref, other_ref, inverse_ref, *scratch):
    half = len(inverse_ref) // 2
    inverse_ref[pl.ds(core * half, half), :] = matrix(mine_ref[:, RANK:])
    inverse_ref[pl.ds((1 - core) * half, half), :] = matrix(other_ref[:, RANK:])
    factor_in_place(inverse_ref, *scratch)


def turn_over(
    place_ref, mine_ref, other_ref, pair_ref, pair_other_ref, f0, f1, f2,
    inverse_ref, left_ref, x_ref, y_ref, *scratch,
):
    pair = pair_of(place_ref)
    inverse_factor(core_of(place_ref), mine_ref, other_ref, inverse_ref, *scratch)
    left = product(tenants(pair, (mine_ref, other_ref), 0), inverse_ref[...], 1, 1)
    right = tenants(pair, (pair_ref, pair_other_ref), RANK)
    own = left[: len(left) // 4]
    left_ref[...] = own.reshape(left_ref.shape)
    half = len(left) // 2
    tenant = [lax.broadcasted_iota(jnp.int32, (half, half), d) // RANK for d in range(2)]
    coeffs = []
    for part in (slice(0, half), slice(half, None)):
        weight = jnp.where(tenant[0] == tenant[1], product(left[part], left[part], 1, 1), 0.0)
        coeffs.append(product(weight, right[part]))
    load = product(stacked((f0, f1, f2)), jnp.concatenate(coeffs), 0, 0)
    store_load(load, (x_ref, y_ref))


def scaled_basis(quarter, inverse, refs, out_ref):
    scale = math.sqrt(D)
    for step, ref in zip(STEPS_AWAY, refs):
        rows = pl.ds((quarter ^ step) * len(ref), len(ref))
        out_ref[rows, :] = product(ref[...], inverse, 1, 1) * scale


def left_basis(place_ref, inverse_ref, q0, q1, q2, q3, out_ref):
    scaled_basis(quarter_of(place_ref), inverse_ref[...], (q0, q1, q2, q3), out_ref)


def finish(
    place_ref, mine_ref, other_ref, q0, q1, q2, q3, out_ref, right_ref, inverse_ref, *scratch
):
    quarter = quarter_of(place_ref)
    inverse_factor(core_of(place_ref), mine_ref, other_ref, inverse_ref, *scratch)
    inverse = inverse_ref[...]
    own = matrix(mine_ref[by_distance(pair_of(place_ref), mine_ref)[0], :RANK])
    right_ref[...] = product(own, inverse, 1, 1).reshape(right_ref.shape)
    scaled_basis(quarter, inverse, (q0, q1, q2, q3), out_ref)


def exchanged(tiles, axis):
    return lax.all_to_all(tiles, axis, 0, 0, tiled=True)


def from_peer(x, axis, step):
    count = lax.axis_size(axis)
    return lax.ppermute(x, axis, [(i, i ^ step) for i in range(count)])


def together(x, others):
    return lax.optimization_barrier((x, others))


def from_sibling(x):
    return from_peer(x, "core", 1)


def across(x):
    return from_peer(x, "y_lo", 1)


def plane_total(x, y, besides):
    done = []
    for x_step, y_step, beside in zip((1, 3), (3, 1), besides):
        moved, beside = together((from_peer(x, "z", x_step), from_peer(y, "z", y_step)), beside)
        x, y = x + moved[0], y + moved[1]
        done.append(beside)
    return (x, y), done


def column_half(factors, bit):
    half = factors.shape[1] // 2
    mine, its = (
        lax.dynamic_slice_in_dim(factors, which * half, half, 1) for which in (bit, 1 - bit)
    )
    return mine, across(its)


def column_quarter(halves, core):
    size = halves[0].shape[1] // 2

    def columns(which):
        return [lax.dynamic_slice_in_dim(x, which * size, size, 1) for x in halves]

    return *columns(core), from_sibling(jnp.concatenate(columns(1 - core)))


def with_place(count):
    return [pl.BlockSpec(memory_space=m) for m in (pltpu.SMEM, *[pltpu.VMEM] * count)]


def work(products, size):
    return pl.CostEstimate(flops=6 * products * size**3, bytes_accessed=0, transcendentals=0)


def gram_tiles(place, factors, parts, rank, beside):
    tiles = (lax.axis_size(ROW), RANK + rank // 2 // lax.axis_size(ROW), rank)
    mine, other = call(
        gram_and_cores,
        [tiles, tiles],
        place,
        *factors,
        *parts,
        in_specs=with_place(5),
        scratch_shapes=[pltpu.VMEM((rank, rank), jnp.float32)],
    )
    other, beside = together(from_sibling(other), beside)
    return mine + other, beside


def row_total(tiles):
    tiles = exchanged(tiles, ROW)
    return exchanged(call(owner_sum, [tiles.shape], tiles), ROW)


def local(b_factors, a_factors, u_start, v_start):
    shape = (*b_factors.shape[:2], u_start.shape[1])
    width, rank = u_start.shape
    bit, core = lax.axis_index("y_lo"), lax.axis_index("core")
    place = jnp.reshape(2 * bit + core, (1,)).astype(jnp.int32)
    b = b_factors.reshape(-1, width)
    a = a_factors.reshape(-1, width)
    b_half = column_half(b, bit)

    partial = call(
        projections,
        [(shape[0], 2 * RANK, rank)],
        *(pltpu.with_memory_space_constraint(x, pltpu.HBM) for x in (b, a, u_start, v_start)),
        in_specs=[pl.BlockSpec(memory_space=pltpu.HBM)] * 4,
        scratch_shapes=[
            *(pltpu.VMEM(x.shape, x.dtype) for x in (b, a, u_start, v_start)),
            pltpu.SemaphoreType.DMA((STEPS, 4)),
        ],
    )
    copies = (lax.axis_size(ROW), 2 * RANK, rank)
    tiles, b_half = together(exchanged(partial, "row"), b_half)
    b_quarter = column_quarter(b_half, core)
    pair = exchanged(call(owner_coefficients, [copies], tiles), ROW)
    pair, b_quarter = together(pair, b_quarter)
    pair_other = from_sibling(pair)

    part = (width // 8, rank)
    parts = call(
        load_sum, [part, part], place, *b_quarter, pair, pair_other, in_specs=with_place(5)
    )
    parts, (_, a_half) = plane_total(*parts, ((), column_half(a, bit)))
    a_quarter = column_quarter(a_half, core)
    basis = jnp.concatenate(parts)
    tiles, _ = gram_tiles(place, b_quarter, parts, rank, ())
    mine, a_quarter = together(row_total(tiles), a_quarter)
    inverse, left, *parts = call(
        turn_over,
        [(rank, rank), shape, part, part],
        place,
        mine,
        from_sibling(mine),
        pair,
        pair_other,
        *a_quarter,
        in_specs=with_place(7),
        scratch_shapes=factor_scratch(rank),
        cost_estimate=work(64, rank),
    )
    parts, moved = together(parts, across(basis))
    u_scaled = call(
        left_basis,
        [(width, rank)],
        place,
        inverse,
        basis,
        moved,
        from_sibling(basis),
        from_sibling(moved),
        in_specs=with_place(5),
        cost_estimate=work(4, rank),
    )
    parts, (u_scaled, _) = plane_total(*parts, (u_scaled, ()))
    basis = jnp.concatenate(parts)
    tiles, moved = gram_tiles(place, a_quarter, parts, rank, across(basis))
    mine = row_total(tiles)
    mine, siblings = together(mine, (from_sibling(basis), from_sibling(moved)))
    v_scaled, right = call(
        finish,
        [(width, rank), shape],
        place,
        mine,
        from_sibling(mine),
        basis,
        moved,
        *siblings,
        in_specs=with_place(6),
        scratch_shapes=[pltpu.VMEM((rank, rank), jnp.float32), *factor_scratch(rank)],
    )
    return u_scaled, v_scaled, left, right


def solution(mesh):
    count, rows = mesh.devices.shape
    mesh = Mesh(mesh.devices.reshape(count // 4, 2, 2, rows), ("z", "y_lo", "core", "row"))
    tenant = ("z", "y_lo", "core")
    in_specs = (P(tenant, None, "row"), P(tenant, None, "row"), P("row", None), P("row", None))
    out_specs = (P("row", None), P("row", None), P(tenant, None, None), P(tenant, None, None))
    return jax.shard_map(local, mesh=mesh, in_specs=in_specs, out_specs=out_specs, check_vma=False)
```

```python
import math

import jax
import jax.numpy as jnp
from jax import lax
from jax.experimental import pallas as pl
from jax.experimental.pallas import tpu as pltpu
from jax.sharding import Mesh
from jax.sharding import PartitionSpec as P

D = 8192
RANK = 16
LANES = 128
SUBLANES = 8
PANEL = 32
STEPS = 4
ROW = ("y_lo", "row")
STEPS_AWAY = (0, 2, 1, 3)


def pieces(x):
    high = x.astype(jnp.bfloat16)
    rest = x - high.astype(jnp.float32)
    middle = rest.astype(jnp.bfloat16)
    return high, middle, (rest - middle.astype(jnp.float32)).astype(jnp.bfloat16)


def float32_product(x, y):
    xh, xm, xl = pieces(x)
    yh, ym, yl = pieces(y)
    xs = jnp.concatenate([xh, xh, xm, xh, xl, xm])
    ys = jnp.concatenate([yh, ym, yh, yl, yh, ym])
    return lax.dot_general(xs, ys, (((0,), (0,)), ((), ())), preferred_element_type=jnp.float32)


def column(x, lane):
    return jnp.broadcast_to(x[:, lane : lane + 1], (SUBLANES, LANES))


def spread(ref, row):
    return ref[pl.ds(row, SUBLANES, stride=0), :]


def eliminate(rows, units, start, rows_ref, columns_ref, factors_ref):
    sub = lax.broadcasted_iota(jnp.int32, (SUBLANES, LANES), 0)
    tile = start // LANES
    for m, first in enumerate(range(start % LANES, start % LANES + PANEL, SUBLANES)):
        slot = m % 4
        tiles = [*rows[m], units[m]]
        if m == 0:
            pivots = [column(rows[m][tile], first + j) for j in range(SUBLANES)]
        for j in range(SUBLANES):
            columns_ref[slot, pl.ds(j * SUBLANES, SUBLANES), :] = pivots[j]
        for t, x in enumerate(tiles):
            rows_ref[slot, pl.ds(t * SUBLANES, SUBLANES), :] = x
        r = [
            [spread(rows_ref.at[slot], t * SUBLANES + i) for t in range(len(tiles))]
            for i in range(SUBLANES)
        ]
        d = [
            [spread(columns_ref.at[slot], j * SUBLANES + i) for j in range(SUBLANES)]
            for i in range(SUBLANES)
        ]
        later = range(m + 1, len(rows))
        c = {g: [column(rows[g][tile], first + j) for j in range(SUBLANES)] for g in later}
        if later:
            ahead = first + SUBLANES
            pivots = [column(rows[m + 1][tile], ahead + j) for j in range(SUBLANES)]
        done = tiles
        for j in range(SUBLANES):
            inverse = lax.rsqrt(d[j][j])
            p = [x * inverse for x in r[j]]
            done = [jnp.where(sub == j, x, y) for x, y in zip(p, done)]
            below = range(j + 1, SUBLANES)
            factor = {i: d[j][i] * inverse for i in below}
            for i in below:
                for other in range(i, SUBLANES):
                    d[i][other] -= factor[i] * factor[other]
                r[i] = [x - factor[i] * y for x, y in zip(r[i], p)]
            for g in later:
                scale = c[g][j] * inverse
                if g == m + 1:
                    place = pl.ds(j * SUBLANES, SUBLANES)
                    factors_ref[slot, place, :] = scale
                    for k in range(SUBLANES):
                        pivots[k] -= scale * spread(factors_ref.at[slot], j * SUBLANES + k)
                for i in below:
                    c[g][i] -= scale * factor[i]
                rows[g] = [x - scale * y for x, y in zip(rows[g], p)]
                units[g] -= scale * p[-1]
        rows[m], units[m] = done[:-1], done[-1]
    rows = [jnp.concatenate(tiles, axis=1) for tiles in rows]
    return jnp.concatenate(rows), jnp.concatenate(units)


def split(x):
    high = x.astype(jnp.bfloat16)
    return high, (x - high.astype(jnp.float32)).astype(jnp.bfloat16)


def product(x, y, x_dim=1, y_dim=0):
    dims = (((x_dim,), (y_dim,)), ((), ()))
    xh, xl = split(x)
    yh, yl = split(y)

    def part(p, q):
        return lax.dot_general(p, q, dims, preferred_element_type=jnp.float32)

    return part(xh, yh) + (part(xh, yl) + part(xl, yh))


def matrix(x):
    return x.reshape(-1, x.shape[-1])


def factor_in_place(out_ref, *scratch):
    n = out_ref.shape[0]
    sub = lax.broadcasted_iota(jnp.int32, (SUBLANES, LANES), 0)
    lane = lax.broadcasted_iota(jnp.int32, (SUBLANES, LANES), 1)
    column = lax.broadcasted_iota(jnp.int32, (n, n), 1)
    for start in range(0, n, PANEL):
        end = start + PANEL
        tile = start // LANES
        rows, units = [], []
        for g in range(0, PANEL, SUBLANES):
            place = pl.ds(start + g, SUBLANES)
            rows.append([out_ref[place, pl.ds(t, LANES)] for t in range(0, n, LANES)])
            units.append(jnp.where(lane == sub + (start % LANES + g), 1.0, 0.0))
        rows, units = eliminate(rows, units, start, *scratch)
        blank = jnp.zeros_like(units)
        units = jnp.concatenate([units if t == tile else blank for t in range(n // LANES)], axis=1)
        inside = (column >= start) & (column < end)
        solved = jnp.where(inside[:PANEL], units, rows)
        out_ref[pl.ds(start, PANEL), :] = jnp.where(column[:PANEL] < end, solved, 0.0)
        if end < n:
            aligned = end // LANES * LANES
            update = float32_product(rows[:, aligned:], solved)[end - aligned :]
            rest = out_ref[pl.ds(end, n - end), :]
            out_ref[pl.ds(end, n - end), :] = jnp.where(inside[end:], 0.0, rest) - update


def factor_scratch(n):
    tiles = n // LANES + 1
    return [
        pltpu.VMEM((4, tiles * SUBLANES, LANES), jnp.float32),
        pltpu.VMEM((4, SUBLANES * SUBLANES, LANES), jnp.float32),
        pltpu.VMEM((4, SUBLANES * SUBLANES, LANES), jnp.float32),
    ]


def call(kernel, shapes, *operands, **options):
    shapes = [jax.ShapeDtypeStruct(shape, jnp.float32) for shape in shapes]
    return pl.pallas_call(
        kernel,
        out_shape=shapes if len(shapes) > 1 else shapes[0],
        compiler_params=pltpu.CompilerParams(vmem_limit_bytes=32 << 20),
        name=kernel.__name__,
        **options,
    )(*operands)


def projections(b_hbm, a_hbm, u_hbm, v_hbm, out_ref, b_ref, a_ref, u_ref, v_ref, sems):
    step = b_ref.shape[1] // STEPS
    copies = []
    for i in range(STEPS):
        part = pl.ds(i * step, step)
        pairs = (
            (u_hbm.at[part], u_ref.at[part]),
            (b_hbm.at[:, part], b_ref.at[:, part]),
            (v_hbm.at[part], v_ref.at[part]),
            (a_hbm.at[:, part], a_ref.at[:, part]),
        )
        copies.append([pltpu.make_async_copy(*p, sems.at[i, k]) for k, p in enumerate(pairs)])
    for group in copies:
        for copy in group:
            copy.start()
    left = right = 0.0
    for i, group in enumerate(copies):
        part = pl.ds(i * step, step)
        group[0].wait()
        group[1].wait()
        left += product(b_ref[:, part], u_ref[part])
        group[2].wait()
        group[3].wait()
        right += product(a_ref[:, part], v_ref[part])
    out_ref[:, :RANK] = left.reshape(-1, RANK, left.shape[1])
    out_ref[:, RANK:] = right.reshape(-1, RANK, right.shape[1])


def owner_coefficients(tiles_ref, out_ref):
    total = jnp.sum(tiles_ref[...], axis=0)
    left, right = total[:RANK], total[RANK:]
    coeffs = product(product(right, right, 1, 1), left)
    out_ref[:, :RANK] = jnp.broadcast_to(coeffs, (len(out_ref), *coeffs.shape))
    out_ref[:, RANK:] = jnp.broadcast_to(right, (len(out_ref), *right.shape))


def owner_sum(tiles_ref, out_ref):
    out_ref[...] = jnp.broadcast_to(jnp.sum(tiles_ref[...], axis=0), out_ref.shape)


def stacked(refs):
    return jnp.concatenate([ref[...] for ref in refs])


def quarter_of(place_ref):
    return place_ref[0]


def core_of(place_ref):
    return place_ref[0] % 2


def pair_of(place_ref):
    return place_ref[0] // 2


def by_distance(pair, ref):
    count = len(ref) // 2
    return [pl.ds(place * count, count) for place in (pair, 1 - pair)]


def tenants(pair, refs, first):
    rows = pl.ds(first, RANK)
    tiles = [ref[place, rows] for ref in refs for place in by_distance(pair, ref)]
    return jnp.concatenate([matrix(x) for x in tiles])


def load_sum(place_ref, f0, f1, f2, mine_ref, other_ref, *out_refs):
    coeffs = tenants(pair_of(place_ref), (mine_ref, other_ref), 0)
    store_load(product(stacked((f0, f1, f2)), coeffs, 0, 0), out_refs)


def store_load(load, out_refs):
    count = len(out_refs[0])
    for i, ref in enumerate(out_refs):
        ref[...] = load[i * count : (i + 1) * count]


def gram_and_cores(place_ref, f0, f1, f2, x_ref, y_ref, mine_ref, other_ref, gram_ref):
    basis = stacked((x_ref, y_ref))
    cores = product(stacked((f0, f1, f2)), basis)
    gram_ref[...] = product(basis, basis, 0, 0)
    core, half = core_of(place_ref), len(gram_ref) // 2
    block = len(cores) // 4
    for i, (ref, which) in enumerate(((mine_ref, core), (other_ref, 1 - core))):
        for j, place in enumerate(by_distance(pair_of(place_ref), ref)):
            rows = cores[(2 * i + j) * block : (2 * i + j + 1) * block]
            ref[place, :RANK] = rows.reshape(-1, RANK, rows.shape[1])
        rows = gram_ref[pl.ds(which * half, half), :]
        ref[:, RANK:] = rows.reshape(len(ref), -1, rows.shape[1])


def inverse_factor(core, mine_ref, other_ref, inverse_ref, *scratch):
    half = len(inverse_ref) // 2
    inverse_ref[pl.ds(core * half, half), :] = matrix(mine_ref[:, RANK:])
    inverse_ref[pl.ds((1 - core) * half, half), :] = matrix(other_ref[:, RANK:])
    factor_in_place(inverse_ref, *scratch)


def turn_over(
    place_ref, mine_ref, other_ref, pair_ref, pair_other_ref, f0, f1, f2,
    inverse_ref, left_ref, x_ref, y_ref, *scratch,
):
    pair = pair_of(place_ref)
    inverse_factor(core_of(place_ref), mine_ref, other_ref, inverse_ref, *scratch)
    left = product(tenants(pair, (mine_ref, other_ref), 0), inverse_ref[...], 1, 1)
    right = tenants(pair, (pair_ref, pair_other_ref), RANK)
    own = left[: len(left) // 4]
    left_ref[...] = own.reshape(left_ref.shape)
    half = len(left) // 2
    tenant = [lax.broadcasted_iota(jnp.int32, (half, half), d) // RANK for d in range(2)]
    coeffs = []
    for part in (slice(0, half), slice(half, None)):
        weight = jnp.where(tenant[0] == tenant[1], product(left[part], left[part], 1, 1), 0.0)
        coeffs.append(product(weight, right[part]))
    load = product(stacked((f0, f1, f2)), jnp.concatenate(coeffs), 0, 0)
    store_load(load, (x_ref, y_ref))


def scaled_basis(quarter, inverse, refs, out_ref):
    scale = math.sqrt(D)
    for step, ref in zip(STEPS_AWAY, refs):
        rows = pl.ds((quarter ^ step) * len(ref), len(ref))
        out_ref[rows, :] = product(ref[...], inverse, 1, 1) * scale


def whole_basis(place_ref, inverse_ref, q0, q1, q2, q3, out_ref):
    scaled_basis(quarter_of(place_ref), inverse_ref[...], (q0, q1, q2, q3), out_ref)


def right_cores(place_ref, mine_ref, other_ref, inverse_ref, right_ref, *scratch):
    inverse_factor(core_of(place_ref), mine_ref, other_ref, inverse_ref, *scratch)
    own = matrix(mine_ref[by_distance(pair_of(place_ref), mine_ref)[0], :RANK])
    right_ref[...] = product(own, inverse_ref[...], 1, 1).reshape(right_ref.shape)


def exchanged(tiles, axis):
    return lax.all_to_all(tiles, axis, 0, 0, tiled=True)


def from_peer(x, axis, step):
    count = lax.axis_size(axis)
    return lax.ppermute(x, axis, [(i, i ^ step) for i in range(count)])


def together(x, others):
    return lax.optimization_barrier((x, others))


def from_sibling(x):
    return from_peer(x, "core", 1)


def across(x):
    return from_peer(x, "y_lo", 1)


def plane_total(x, y, besides):
    done = []
    for x_step, y_step, beside in zip((1, 3), (3, 1), besides):
        moved, beside = together((from_peer(x, "z", x_step), from_peer(y, "z", y_step)), beside)
        x, y = x + moved[0], y + moved[1]
        done.append(beside)
    return (x, y), done


def column_half(factors, bit):
    half = factors.shape[1] // 2
    mine, its = (
        lax.dynamic_slice_in_dim(factors, which * half, half, 1) for which in (bit, 1 - bit)
    )
    return mine, across(its)


def column_quarter(halves, core):
    size = halves[0].shape[1] // 2

    def columns(which):
        return [lax.dynamic_slice_in_dim(x, which * size, size, 1) for x in halves]

    return *columns(core), from_sibling(jnp.concatenate(columns(1 - core)))


def with_place(count):
    return [pl.BlockSpec(memory_space=m) for m in (pltpu.SMEM, *[pltpu.VMEM] * count)]


def work(products, size):
    return pl.CostEstimate(flops=6 * products * size**3, bytes_accessed=0, transcendentals=0)


def basis_rows(place, inverse, quarters):
    rank = inverse.shape[0]
    return call(
        whole_basis,
        [(4 * len(quarters[0]), rank)],
        place,
        inverse,
        *quarters,
        in_specs=with_place(5),
        cost_estimate=work(4, rank),
    )


def gram_tiles(place, factors, parts, rank, beside):
    tiles = (lax.axis_size(ROW), RANK + rank // 2 // lax.axis_size(ROW), rank)
    mine, other = call(
        gram_and_cores,
        [tiles, tiles],
        place,
        *factors,
        *parts,
        in_specs=with_place(5),
        scratch_shapes=[pltpu.VMEM((rank, rank), jnp.float32)],
    )
    other, beside = together(from_sibling(other), beside)
    return mine + other, beside


def row_total(tiles):
    tiles = exchanged(tiles, ROW)
    return exchanged(call(owner_sum, [tiles.shape], tiles), ROW)


def local(b_factors, a_factors, u_start, v_start):
    shape = (*b_factors.shape[:2], u_start.shape[1])
    width, rank = u_start.shape
    bit, core = lax.axis_index("y_lo"), lax.axis_index("core")
    place = jnp.reshape(2 * bit + core, (1,)).astype(jnp.int32)
    b = b_factors.reshape(-1, width)
    a = a_factors.reshape(-1, width)
    b_half = column_half(b, bit)

    partial = call(
        projections,
        [(shape[0], 2 * RANK, rank)],
        *(pltpu.with_memory_space_constraint(x, pltpu.HBM) for x in (b, a, u_start, v_start)),
        in_specs=[pl.BlockSpec(memory_space=pltpu.HBM)] * 4,
        scratch_shapes=[
            *(pltpu.VMEM(x.shape, x.dtype) for x in (b, a, u_start, v_start)),
            pltpu.SemaphoreType.DMA((STEPS, 4)),
        ],
    )
    copies = (lax.axis_size(ROW), 2 * RANK, rank)
    tiles, b_half = together(exchanged(partial, "row"), b_half)
    b_quarter = column_quarter(b_half, core)
    pair = exchanged(call(owner_coefficients, [copies], tiles), ROW)
    pair, b_quarter = together(pair, b_quarter)
    pair_other = from_sibling(pair)

    part = (width // 8, rank)
    parts = call(
        load_sum, [part, part], place, *b_quarter, pair, pair_other, in_specs=with_place(5)
    )
    parts, (_, a_half) = plane_total(*parts, ((), column_half(a, bit)))
    a_quarter = column_quarter(a_half, core)
    basis = jnp.concatenate(parts)
    tiles, _ = gram_tiles(place, b_quarter, parts, rank, ())
    mine, a_quarter = together(row_total(tiles), a_quarter)
    inverse, left, *parts = call(
        turn_over,
        [(rank, rank), shape, part, part],
        place,
        mine,
        from_sibling(mine),
        pair,
        pair_other,
        *a_quarter,
        in_specs=with_place(7),
        scratch_shapes=factor_scratch(rank),
        cost_estimate=work(64, rank),
    )
    parts, moved = together(parts, across(basis))
    quarters = (basis, moved, from_sibling(basis), from_sibling(moved))
    u_scaled = basis_rows(place, inverse, quarters)
    parts, (u_scaled, _) = plane_total(*parts, (u_scaled, ()))
    basis = jnp.concatenate(parts)
    tiles, _ = gram_tiles(place, a_quarter, parts, rank, ())
    mine = row_total(tiles)
    inverse, right = call(
        right_cores,
        [(rank, rank), shape],
        place,
        mine,
        from_sibling(mine),
        in_specs=with_place(2),
        scratch_shapes=factor_scratch(rank),
    )
    moved = across(basis)
    quarters = (basis, moved, from_sibling(basis), from_sibling(moved))
    v_scaled = basis_rows(place, inverse, quarters)
    return u_scaled, v_scaled, left, right


def solution(mesh):
    count, rows = mesh.devices.shape
    mesh = Mesh(mesh.devices.reshape(count // 4, 2, 2, rows), ("z", "y_lo", "core", "row"))
    tenant = ("z", "y_lo", "core")
    in_specs = (P(tenant, None, "row"), P(tenant, None, "row"), P("row", None), P("row", None))
    out_specs = (P("row", None), P("row", None), P(tenant, None, None), P(tenant, None, None))
    return jax.shard_map(local, mesh=mesh, in_specs=in_specs, out_specs=out_specs, check_vma=False)
```

```python
import math

import jax
import jax.numpy as jnp
from jax import lax
from jax.experimental import pallas as pl
from jax.experimental.pallas import tpu as pltpu
from jax.sharding import Mesh
from jax.sharding import PartitionSpec as P

D = 8192
RANK = 16
LANES = 128
SUBLANES = 8
PANEL = 32
STEPS = 4
ROW = ("y_lo", "row")
STEPS_AWAY = (0, 2, 1, 3)


def pieces(x):
    high = x.astype(jnp.bfloat16)
    rest = x - high.astype(jnp.float32)
    middle = rest.astype(jnp.bfloat16)
    return high, middle, (rest - middle.astype(jnp.float32)).astype(jnp.bfloat16)


def float32_product(x, y):
    xh, xm, xl = pieces(x)
    yh, ym, yl = pieces(y)
    xs = jnp.concatenate([xh, xh, xm, xh, xl, xm])
    ys = jnp.concatenate([yh, ym, yh, yl, yh, ym])
    return lax.dot_general(xs, ys, (((0,), (0,)), ((), ())), preferred_element_type=jnp.float32)


def column(x, lane):
    return jnp.broadcast_to(x[:, lane : lane + 1], (SUBLANES, LANES))


def spread(ref, row):
    return ref[pl.ds(row, SUBLANES, stride=0), :]


def eliminate(rows, units, start, rows_ref, columns_ref, factors_ref):
    sub = lax.broadcasted_iota(jnp.int32, (SUBLANES, LANES), 0)
    tile = start // LANES
    for m, first in enumerate(range(start % LANES, start % LANES + PANEL, SUBLANES)):
        slot = m % 4
        tiles = [*rows[m], units[m]]
        if m == 0:
            pivots = [column(rows[m][tile], first + j) for j in range(SUBLANES)]
        for j in range(SUBLANES):
            columns_ref[slot, pl.ds(j * SUBLANES, SUBLANES), :] = pivots[j]
        for t, x in enumerate(tiles):
            rows_ref[slot, pl.ds(t * SUBLANES, SUBLANES), :] = x
        r = [
            [spread(rows_ref.at[slot], t * SUBLANES + i) for t in range(len(tiles))]
            for i in range(SUBLANES)
        ]
        d = [
            [spread(columns_ref.at[slot], j * SUBLANES + i) for j in range(SUBLANES)]
            for i in range(SUBLANES)
        ]
        later = range(m + 1, len(rows))
        c = {g: [column(rows[g][tile], first + j) for j in range(SUBLANES)] for g in later}
        if later:
            ahead = first + SUBLANES
            pivots = [column(rows[m + 1][tile], ahead + j) for j in range(SUBLANES)]
        done = tiles
        for j in range(SUBLANES):
            inverse = lax.rsqrt(d[j][j])
            p = [x * inverse for x in r[j]]
            done = [jnp.where(sub == j, x, y) for x, y in zip(p, done)]
            below = range(j + 1, SUBLANES)
            factor = {i: d[j][i] * inverse for i in below}
            for i in below:
                for other in range(i, SUBLANES):
                    d[i][other] -= factor[i] * factor[other]
                r[i] = [x - factor[i] * y for x, y in zip(r[i], p)]
            for g in later:
                scale = c[g][j] * inverse
                if g == m + 1:
                    place = pl.ds(j * SUBLANES, SUBLANES)
                    factors_ref[slot, place, :] = scale
                    for k in range(SUBLANES):
                        pivots[k] -= scale * spread(factors_ref.at[slot], j * SUBLANES + k)
                for i in below:
                    c[g][i] -= scale * factor[i]
                rows[g] = [x - scale * y for x, y in zip(rows[g], p)]
                units[g] -= scale * p[-1]
        rows[m], units[m] = done[:-1], done[-1]
    rows = [jnp.concatenate(tiles, axis=1) for tiles in rows]
    return jnp.concatenate(rows), jnp.concatenate(units)


def split(x):
    high = x.astype(jnp.bfloat16)
    return high, (x - high.astype(jnp.float32)).astype(jnp.bfloat16)


def product(x, y, x_dim=1, y_dim=0):
    dims = (((x_dim,), (y_dim,)), ((), ()))
    xh, xl = split(x)
    yh, yl = split(y)

    def part(p, q):
        return lax.dot_general(p, q, dims, preferred_element_type=jnp.float32)

    return part(xh, yh) + (part(xh, yl) + part(xl, yh))


def matrix(x):
    return x.reshape(-1, x.shape[-1])


def factor_in_place(out_ref, *scratch):
    n = out_ref.shape[0]
    sub = lax.broadcasted_iota(jnp.int32, (SUBLANES, LANES), 0)
    lane = lax.broadcasted_iota(jnp.int32, (SUBLANES, LANES), 1)
    column = lax.broadcasted_iota(jnp.int32, (n, n), 1)
    for start in range(0, n, PANEL):
        end = start + PANEL
        tile = start // LANES
        rows, units = [], []
        for g in range(0, PANEL, SUBLANES):
            place = pl.ds(start + g, SUBLANES)
            rows.append([out_ref[place, pl.ds(t, LANES)] for t in range(0, n, LANES)])
            units.append(jnp.where(lane == sub + (start % LANES + g), 1.0, 0.0))
        rows, units = eliminate(rows, units, start, *scratch)
        blank = jnp.zeros_like(units)
        units = jnp.concatenate([units if t == tile else blank for t in range(n // LANES)], axis=1)
        inside = (column >= start) & (column < end)
        solved = jnp.where(inside[:PANEL], units, rows)
        out_ref[pl.ds(start, PANEL), :] = jnp.where(column[:PANEL] < end, solved, 0.0)
        if end < n:
            aligned = end // LANES * LANES
            update = float32_product(rows[:, aligned:], solved)[end - aligned :]
            rest = out_ref[pl.ds(end, n - end), :]
            out_ref[pl.ds(end, n - end), :] = jnp.where(inside[end:], 0.0, rest) - update


def factor_scratch(n):
    tiles = n // LANES + 1
    return [
        pltpu.VMEM((4, tiles * SUBLANES, LANES), jnp.float32),
        pltpu.VMEM((4, SUBLANES * SUBLANES, LANES), jnp.float32),
        pltpu.VMEM((4, SUBLANES * SUBLANES, LANES), jnp.float32),
    ]


def call(kernel, shapes, *operands, **options):
    shapes = [jax.ShapeDtypeStruct(shape, jnp.float32) for shape in shapes]
    return pl.pallas_call(
        kernel,
        out_shape=shapes if len(shapes) > 1 else shapes[0],
        compiler_params=pltpu.CompilerParams(vmem_limit_bytes=32 << 20),
        name=kernel.__name__,
        **options,
    )(*operands)


def projections(b_hbm, a_hbm, u_hbm, v_hbm, out_ref, b_ref, a_ref, u_ref, v_ref, sems):
    step = b_ref.shape[1] // STEPS
    copies = []
    for i in range(STEPS):
        part = pl.ds(i * step, step)
        pairs = (
            (u_hbm.at[part], u_ref.at[part]),
            (b_hbm.at[:, part], b_ref.at[:, part]),
            (v_hbm.at[part], v_ref.at[part]),
            (a_hbm.at[:, part], a_ref.at[:, part]),
        )
        copies.append([pltpu.make_async_copy(*p, sems.at[i, k]) for k, p in enumerate(pairs)])
    for group in copies:
        for copy in group:
            copy.start()
    left = right = 0.0
    for i, group in enumerate(copies):
        part = pl.ds(i * step, step)
        group[0].wait()
        group[1].wait()
        left += product(b_ref[:, part], u_ref[part])
        group[2].wait()
        group[3].wait()
        right += product(a_ref[:, part], v_ref[part])
    out_ref[:, :RANK] = left.reshape(-1, RANK, left.shape[1])
    out_ref[:, RANK:] = right.reshape(-1, RANK, right.shape[1])


def owner_coefficients(tiles_ref, out_ref):
    total = jnp.sum(tiles_ref[...], axis=0)
    left, right = total[:RANK], total[RANK:]
    coeffs = product(product(right, right, 1, 1), left)
    out_ref[:, :RANK] = jnp.broadcast_to(coeffs, (len(out_ref), *coeffs.shape))
    out_ref[:, RANK:] = jnp.broadcast_to(right, (len(out_ref), *right.shape))


def owner_sum(tiles_ref, out_ref):
    out_ref[...] = jnp.broadcast_to(jnp.sum(tiles_ref[...], axis=0), out_ref.shape)


def stacked(refs):
    return jnp.concatenate([ref[...] for ref in refs])


def quarter_of(place_ref):
    return place_ref[0]


def core_of(place_ref):
    return place_ref[0] % 2


def pair_of(place_ref):
    return place_ref[0] // 2


def by_distance(pair, ref):
    count = len(ref) // 2
    return [pl.ds(place * count, count) for place in (pair, 1 - pair)]


def tenants(pair, refs, first):
    rows = pl.ds(first, RANK)
    tiles = [ref[place, rows] for ref in refs for place in by_distance(pair, ref)]
    return jnp.concatenate([matrix(x) for x in tiles])


def load_sum(place_ref, f0, f1, f2, mine_ref, other_ref, *out_refs):
    coeffs = tenants(pair_of(place_ref), (mine_ref, other_ref), 0)
    store_load(product(stacked((f0, f1, f2)), coeffs, 0, 0), out_refs)


def store_load(load, out_refs):
    count = len(out_refs[0])
    for i, ref in enumerate(out_refs):
        ref[...] = load[i * count : (i + 1) * count]


def gram_and_cores(place_ref, f0, f1, f2, x_ref, y_ref, mine_ref, other_ref, gram_ref):
    basis = stacked((x_ref, y_ref))
    cores = product(stacked((f0, f1, f2)), basis)
    gram_ref[...] = product(basis, basis, 0, 0)
    core, half = core_of(place_ref), len(gram_ref) // 2
    block = len(cores) // 4
    for i, (ref, which) in enumerate(((mine_ref, core), (other_ref, 1 - core))):
        for j, place in enumerate(by_distance(pair_of(place_ref), ref)):
            rows = cores[(2 * i + j) * block : (2 * i + j + 1) * block]
            ref[place, :RANK] = rows.reshape(-1, RANK, rows.shape[1])
        rows = gram_ref[pl.ds(which * half, half), :]
        ref[:, RANK:] = rows.reshape(len(ref), -1, rows.shape[1])


def inverse_factor(core, mine_ref, other_ref, inverse_ref, *scratch):
    half = len(inverse_ref) // 2
    inverse_ref[pl.ds(core * half, half), :] = matrix(mine_ref[:, RANK:])
    inverse_ref[pl.ds((1 - core) * half, half), :] = matrix(other_ref[:, RANK:])
    factor_in_place(inverse_ref, *scratch)


def turn_over(
    place_ref, mine_ref, other_ref, pair_ref, pair_other_ref, f0, f1, f2,
    inverse_ref, left_ref, x_ref, y_ref, *scratch,
):
    pair = pair_of(place_ref)
    inverse_factor(core_of(place_ref), mine_ref, other_ref, inverse_ref, *scratch)
    left = product(tenants(pair, (mine_ref, other_ref), 0), inverse_ref[...], 1, 1)
    right = tenants(pair, (pair_ref, pair_other_ref), RANK)
    own = left[: len(left) // 4]
    left_ref[...] = own.reshape(left_ref.shape)
    half = len(left) // 2
    tenant = [lax.broadcasted_iota(jnp.int32, (half, half), d) // RANK for d in range(2)]
    coeffs = []
    for part in (slice(0, half), slice(half, None)):
        weight = jnp.where(tenant[0] == tenant[1], product(left[part], left[part], 1, 1), 0.0)
        coeffs.append(product(weight, right[part]))
    load = product(stacked((f0, f1, f2)), jnp.concatenate(coeffs), 0, 0)
    store_load(load, (x_ref, y_ref))


def scaled_basis(quarter, inverse, refs, out_ref):
    scale = math.sqrt(D)
    for step, ref in zip(STEPS_AWAY, refs):
        rows = pl.ds((quarter ^ step) * len(ref), len(ref))
        out_ref[rows, :] = product(ref[...], inverse, 1, 1) * scale


def whole_basis(place_ref, inverse_ref, q0, q1, q2, q3, out_ref):
    scaled_basis(quarter_of(place_ref), inverse_ref[...], (q0, q1, q2, q3), out_ref)


def right_cores(place_ref, mine_ref, other_ref, inverse_ref, right_ref, *scratch):
    inverse_factor(core_of(place_ref), mine_ref, other_ref, inverse_ref, *scratch)
    own = matrix(mine_ref[by_distance(pair_of(place_ref), mine_ref)[0], :RANK])
    right_ref[...] = product(own, inverse_ref[...], 1, 1).reshape(right_ref.shape)


def exchanged(tiles, axis):
    return lax.all_to_all(tiles, axis, 0, 0, tiled=True)


def from_peer(x, axis, step):
    count = lax.axis_size(axis)
    return lax.ppermute(x, axis, [(i, i ^ step) for i in range(count)])


def together(x, others):
    return lax.optimization_barrier((x, others))


def from_sibling(x):
    return from_peer(x, "core", 1)


def across(x):
    return from_peer(x, "y_lo", 1)


def plane_total(x, y, besides):
    done = []
    for x_step, y_step, beside in zip((1, 3), (3, 1), besides):
        moved, beside = together((from_peer(x, "z", x_step), from_peer(y, "z", y_step)), beside)
        x, y = x + moved[0], y + moved[1]
        done.append(beside)
    return (x, y), done


def column_half(factors, bit):
    half = factors.shape[1] // 2
    mine, its = (
        lax.dynamic_slice_in_dim(factors, which * half, half, 1) for which in (bit, 1 - bit)
    )
    return mine, across(its)


def column_quarter(halves, core):
    size = halves[0].shape[1] // 2

    def columns(which):
        return [lax.dynamic_slice_in_dim(x, which * size, size, 1) for x in halves]

    return *columns(core), from_sibling(jnp.concatenate(columns(1 - core)))


def with_place(count):
    return [pl.BlockSpec(memory_space=m) for m in (pltpu.SMEM, *[pltpu.VMEM] * count)]


def work(products, size):
    return pl.CostEstimate(flops=6 * products * size**3, bytes_accessed=0, transcendentals=0)


def basis_rows(place, inverse, quarters):
    rank = inverse.shape[0]
    return call(
        whole_basis,
        [(4 * len(quarters[0]), rank)],
        place,
        inverse,
        *quarters,
        in_specs=with_place(5),
        cost_estimate=work(4, rank),
    )


def gram_tiles(place, factors, parts, rank, beside):
    tiles = (lax.axis_size(ROW), RANK + rank // 2 // lax.axis_size(ROW), rank)
    mine, other = call(
        gram_and_cores,
        [tiles, tiles],
        place,
        *factors,
        *parts,
        in_specs=with_place(5),
        scratch_shapes=[pltpu.VMEM((rank, rank), jnp.float32)],
    )
    other, beside = together(from_sibling(other), beside)
    return mine + other, beside


def row_total(tiles, beside=()):
    tiles, beside = together(exchanged(tiles, ROW), beside)
    return exchanged(call(owner_sum, [tiles.shape], tiles), ROW), beside


def local(b_factors, a_factors, u_start, v_start):
    shape = (*b_factors.shape[:2], u_start.shape[1])
    width, rank = u_start.shape
    bit, core = lax.axis_index("y_lo"), lax.axis_index("core")
    place = jnp.reshape(2 * bit + core, (1,)).astype(jnp.int32)
    b = b_factors.reshape(-1, width)
    a = a_factors.reshape(-1, width)
    b_half = column_half(b, bit)

    partial = call(
        projections,
        [(shape[0], 2 * RANK, rank)],
        *(pltpu.with_memory_space_constraint(x, pltpu.HBM) for x in (b, a, u_start, v_start)),
        in_specs=[pl.BlockSpec(memory_space=pltpu.HBM)] * 4,
        scratch_shapes=[
            *(pltpu.VMEM(x.shape, x.dtype) for x in (b, a, u_start, v_start)),
            pltpu.SemaphoreType.DMA((STEPS, 4)),
        ],
    )
    copies = (lax.axis_size(ROW), 2 * RANK, rank)
    b_quarter = column_quarter(b_half, core)
    pair = exchanged(call(owner_coefficients, [copies], exchanged(partial, "row")), ROW)
    pair_other = from_sibling(pair)

    part = (width // 8, rank)
    parts = call(
        load_sum, [part, part], place, *b_quarter, pair, pair_other, in_specs=with_place(5)
    )
    parts, (_, a_half) = plane_total(*parts, ((), column_half(a, bit)))
    basis = jnp.concatenate(parts)
    tiles, _ = gram_tiles(place, b_quarter, parts, rank, ())
    mine, a_half = row_total(tiles, a_half)
    mine, a_quarter = together(mine, column_quarter(a_half, core))
    inverse, left, *parts = call(
        turn_over,
        [(rank, rank), shape, part, part],
        place,
        mine,
        from_sibling(mine),
        pair,
        pair_other,
        *a_quarter,
        in_specs=with_place(7),
        scratch_shapes=factor_scratch(rank),
        cost_estimate=work(64, rank),
    )
    parts, moved = together(parts, across(basis))
    quarters = (basis, moved, from_sibling(basis), from_sibling(moved))
    u_scaled = basis_rows(place, inverse, quarters)
    parts, (u_scaled, _) = plane_total(*parts, (u_scaled, ()))
    basis = jnp.concatenate(parts)
    tiles, _ = gram_tiles(place, a_quarter, parts, rank, ())
    mine, _ = row_total(tiles)
    inverse, right = call(
        right_cores,
        [(rank, rank), shape],
        place,
        mine,
        from_sibling(mine),
        in_specs=with_place(2),
        scratch_shapes=factor_scratch(rank),
    )
    moved = across(basis)
    quarters = (basis, moved, from_sibling(basis), from_sibling(moved))
    v_scaled = basis_rows(place, inverse, quarters)
    return u_scaled, v_scaled, left, right


def solution(mesh):
    count, rows = mesh.devices.shape
    mesh = Mesh(mesh.devices.reshape(count // 4, 2, 2, rows), ("z", "y_lo", "core", "row"))
    tenant = ("z", "y_lo", "core")
    in_specs = (P(tenant, None, "row"), P(tenant, None, "row"), P("row", None), P("row", None))
    out_specs = (P("row", None), P("row", None), P(tenant, None, None), P(tenant, None, None))
    return jax.shard_map(local, mesh=mesh, in_specs=in_specs, out_specs=out_specs, check_vma=False)
```

```python
import math

import jax
import jax.numpy as jnp
from jax import lax
from jax.experimental import pallas as pl
from jax.experimental.pallas import tpu as pltpu
from jax.sharding import Mesh
from jax.sharding import PartitionSpec as P

D = 8192
RANK = 16
LANES = 128
SUBLANES = 8
PANEL = 32
STEPS = 4
ROW = ("y_lo", "row")
STEPS_AWAY = (0, 2, 1, 3)


def pieces(x):
    high = x.astype(jnp.bfloat16)
    rest = x - high.astype(jnp.float32)
    middle = rest.astype(jnp.bfloat16)
    return high, middle, (rest - middle.astype(jnp.float32)).astype(jnp.bfloat16)


def float32_product(x, y):
    xh, xm, xl = pieces(x)
    yh, ym, yl = pieces(y)
    xs = jnp.concatenate([xh, xh, xm, xh, xl, xm])
    ys = jnp.concatenate([yh, ym, yh, yl, yh, ym])
    return lax.dot_general(xs, ys, (((0,), (0,)), ((), ())), preferred_element_type=jnp.float32)


def column(x, lane):
    return jnp.broadcast_to(x[:, lane : lane + 1], (SUBLANES, LANES))


def spread(ref, row):
    return ref[pl.ds(row, SUBLANES, stride=0), :]


def eliminate(rows, units, start, rows_ref, columns_ref, factors_ref):
    sub = lax.broadcasted_iota(jnp.int32, (SUBLANES, LANES), 0)
    tile = start // LANES
    for m, first in enumerate(range(start % LANES, start % LANES + PANEL, SUBLANES)):
        slot = m % 4
        tiles = [*rows[m], units[m]]
        if m == 0:
            pivots = [column(rows[m][tile], first + j) for j in range(SUBLANES)]
        for j in range(SUBLANES):
            columns_ref[slot, pl.ds(j * SUBLANES, SUBLANES), :] = pivots[j]
        for t, x in enumerate(tiles):
            rows_ref[slot, pl.ds(t * SUBLANES, SUBLANES), :] = x
        r = [
            [spread(rows_ref.at[slot], t * SUBLANES + i) for t in range(len(tiles))]
            for i in range(SUBLANES)
        ]
        d = [
            [spread(columns_ref.at[slot], j * SUBLANES + i) for j in range(SUBLANES)]
            for i in range(SUBLANES)
        ]
        later = range(m + 1, len(rows))
        c = {g: [column(rows[g][tile], first + j) for j in range(SUBLANES)] for g in later}
        if later:
            ahead = first + SUBLANES
            pivots = [column(rows[m + 1][tile], ahead + j) for j in range(SUBLANES)]
        done = tiles
        for j in range(SUBLANES):
            inverse = lax.rsqrt(d[j][j])
            p = [x * inverse for x in r[j]]
            done = [jnp.where(sub == j, x, y) for x, y in zip(p, done)]
            below = range(j + 1, SUBLANES)
            factor = {i: d[j][i] * inverse for i in below}
            for i in below:
                for other in range(i, SUBLANES):
                    d[i][other] -= factor[i] * factor[other]
                r[i] = [x - factor[i] * y for x, y in zip(r[i], p)]
            for g in later:
                scale = c[g][j] * inverse
                if g == m + 1:
                    place = pl.ds(j * SUBLANES, SUBLANES)
                    factors_ref[slot, place, :] = scale
                    for k in range(SUBLANES):
                        pivots[k] -= scale * spread(factors_ref.at[slot], j * SUBLANES + k)
                for i in below:
                    c[g][i] -= scale * factor[i]
                rows[g] = [x - scale * y for x, y in zip(rows[g], p)]
                units[g] -= scale * p[-1]
        rows[m], units[m] = done[:-1], done[-1]
    rows = [jnp.concatenate(tiles, axis=1) for tiles in rows]
    return jnp.concatenate(rows), jnp.concatenate(units)


def split(x):
    high = x.astype(jnp.bfloat16)
    return high, (x - high.astype(jnp.float32)).astype(jnp.bfloat16)


def product(x, y, x_dim=1, y_dim=0):
    dims = (((x_dim,), (y_dim,)), ((), ()))
    xh, xl = split(x)
    yh, yl = split(y)

    def part(p, q):
        return lax.dot_general(p, q, dims, preferred_element_type=jnp.float32)

    return part(xh, yh) + (part(xh, yl) + part(xl, yh))


def matrix(x):
    return x.reshape(-1, x.shape[-1])


def factor_in_place(out_ref, *scratch):
    n = out_ref.shape[0]
    sub = lax.broadcasted_iota(jnp.int32, (SUBLANES, LANES), 0)
    lane = lax.broadcasted_iota(jnp.int32, (SUBLANES, LANES), 1)
    column = lax.broadcasted_iota(jnp.int32, (n, n), 1)
    for start in range(0, n, PANEL):
        end = start + PANEL
        tile = start // LANES
        rows, units = [], []
        for g in range(0, PANEL, SUBLANES):
            place = pl.ds(start + g, SUBLANES)
            rows.append([out_ref[place, pl.ds(t, LANES)] for t in range(0, n, LANES)])
            units.append(jnp.where(lane == sub + (start % LANES + g), 1.0, 0.0))
        rows, units = eliminate(rows, units, start, *scratch)
        blank = jnp.zeros_like(units)
        units = jnp.concatenate([units if t == tile else blank for t in range(n // LANES)], axis=1)
        inside = (column >= start) & (column < end)
        solved = jnp.where(inside[:PANEL], units, rows)
        out_ref[pl.ds(start, PANEL), :] = jnp.where(column[:PANEL] < end, solved, 0.0)
        if end < n:
            aligned = end // LANES * LANES
            update = float32_product(rows[:, aligned:], solved)[end - aligned :]
            rest = out_ref[pl.ds(end, n - end), :]
            out_ref[pl.ds(end, n - end), :] = jnp.where(inside[end:], 0.0, rest) - update


def factor_scratch(n):
    tiles = n // LANES + 1
    return [
        pltpu.VMEM((4, tiles * SUBLANES, LANES), jnp.float32),
        pltpu.VMEM((4, SUBLANES * SUBLANES, LANES), jnp.float32),
        pltpu.VMEM((4, SUBLANES * SUBLANES, LANES), jnp.float32),
    ]


def call(kernel, shapes, *operands, **options):
    shapes = [jax.ShapeDtypeStruct(shape, jnp.float32) for shape in shapes]
    return pl.pallas_call(
        kernel,
        out_shape=shapes if len(shapes) > 1 else shapes[0],
        compiler_params=pltpu.CompilerParams(vmem_limit_bytes=32 << 20),
        name=kernel.__name__,
        **options,
    )(*operands)


def projections(b_hbm, a_hbm, u_hbm, v_hbm, out_ref, b_ref, a_ref, u_ref, v_ref, sems):
    step = b_ref.shape[1] // STEPS
    copies = []
    for i in range(STEPS):
        part = pl.ds(i * step, step)
        pairs = (
            (u_hbm.at[part], u_ref.at[part]),
            (b_hbm.at[:, part], b_ref.at[:, part]),
            (v_hbm.at[part], v_ref.at[part]),
            (a_hbm.at[:, part], a_ref.at[:, part]),
        )
        copies.append([pltpu.make_async_copy(*p, sems.at[i, k]) for k, p in enumerate(pairs)])
    for group in copies:
        for copy in group:
            copy.start()
    left = right = 0.0
    for i, group in enumerate(copies):
        part = pl.ds(i * step, step)
        group[0].wait()
        group[1].wait()
        left += product(b_ref[:, part], u_ref[part])
        group[2].wait()
        group[3].wait()
        right += product(a_ref[:, part], v_ref[part])
    out_ref[:, :RANK] = left.reshape(-1, RANK, left.shape[1])
    out_ref[:, RANK:] = right.reshape(-1, RANK, right.shape[1])


def owner_coefficients(tiles_ref, out_ref):
    total = jnp.sum(tiles_ref[...], axis=0)
    left, right = total[:RANK], total[RANK:]
    coeffs = product(product(right, right, 1, 1), left)
    out_ref[:, :RANK] = jnp.broadcast_to(coeffs, (len(out_ref), *coeffs.shape))
    out_ref[:, RANK:] = jnp.broadcast_to(right, (len(out_ref), *right.shape))


def owner_sum(tiles_ref, out_ref):
    out_ref[...] = jnp.broadcast_to(jnp.sum(tiles_ref[...], axis=0), out_ref.shape)


def stacked(refs):
    return jnp.concatenate([ref[...] for ref in refs])


def quarter_of(place_ref):
    return place_ref[0]


def core_of(place_ref):
    return place_ref[0] % 2


def pair_of(place_ref):
    return place_ref[0] // 2


def by_distance(pair, ref):
    count = len(ref) // 2
    return [pl.ds(place * count, count) for place in (pair, 1 - pair)]


def tenants(pair, refs, first):
    rows = pl.ds(first, RANK)
    tiles = [ref[place, rows] for ref in refs for place in by_distance(pair, ref)]
    return jnp.concatenate([matrix(x) for x in tiles])


def load_sum(place_ref, f0, f1, f2, mine_ref, other_ref, *out_refs):
    coeffs = tenants(pair_of(place_ref), (mine_ref, other_ref), 0)
    store_load(product(stacked((f0, f1, f2)), coeffs, 0, 0), out_refs)


def store_load(load, out_refs):
    count = len(out_refs[0])
    for i, ref in enumerate(out_refs):
        ref[...] = load[i * count : (i + 1) * count]


def gram_and_cores(place_ref, f0, f1, f2, x_ref, y_ref, mine_ref, other_ref, gram_ref):
    basis = stacked((x_ref, y_ref))
    cores = product(stacked((f0, f1, f2)), basis)
    gram_ref[...] = product(basis, basis, 0, 0)
    core, half = core_of(place_ref), len(gram_ref) // 2
    block = len(cores) // 4
    for i, (ref, which) in enumerate(((mine_ref, core), (other_ref, 1 - core))):
        for j, place in enumerate(by_distance(pair_of(place_ref), ref)):
            rows = cores[(2 * i + j) * block : (2 * i + j + 1) * block]
            ref[place, :RANK] = rows.reshape(-1, RANK, rows.shape[1])
        rows = gram_ref[pl.ds(which * half, half), :]
        ref[:, RANK:] = rows.reshape(len(ref), -1, rows.shape[1])


def inverse_factor(core, mine_ref, other_ref, inverse_ref, *scratch):
    half = len(inverse_ref) // 2
    inverse_ref[pl.ds(core * half, half), :] = matrix(mine_ref[:, RANK:])
    inverse_ref[pl.ds((1 - core) * half, half), :] = matrix(other_ref[:, RANK:])
    factor_in_place(inverse_ref, *scratch)


def turn_over(
    place_ref, mine_ref, other_ref, pair_ref, pair_other_ref, f0, f1, f2,
    inverse_ref, left_ref, x_ref, y_ref, *scratch,
):
    pair = pair_of(place_ref)
    inverse_factor(core_of(place_ref), mine_ref, other_ref, inverse_ref, *scratch)
    left = product(tenants(pair, (mine_ref, other_ref), 0), inverse_ref[...], 1, 1)
    right = tenants(pair, (pair_ref, pair_other_ref), RANK)
    own = left[: len(left) // 4]
    left_ref[...] = own.reshape(left_ref.shape)
    half = len(left) // 2
    tenant = [lax.broadcasted_iota(jnp.int32, (half, half), d) // RANK for d in range(2)]
    coeffs = []
    for part in (slice(0, half), slice(half, None)):
        weight = jnp.where(tenant[0] == tenant[1], product(left[part], left[part], 1, 1), 0.0)
        coeffs.append(product(weight, right[part]))
    load = product(stacked((f0, f1, f2)), jnp.concatenate(coeffs), 0, 0)
    store_load(load, (x_ref, y_ref))


def scaled_basis(quarter, inverse, refs, out_ref):
    scale = math.sqrt(D)
    for step, ref in zip(STEPS_AWAY, refs):
        rows = pl.ds((quarter ^ step) * len(ref), len(ref))
        out_ref[rows, :] = product(ref[...], inverse, 1, 1) * scale


def whole_basis(place_ref, inverse_ref, q0, q1, q2, q3, out_ref):
    scaled_basis(quarter_of(place_ref), inverse_ref[...], (q0, q1, q2, q3), out_ref)


def right_cores(place_ref, mine_ref, other_ref, inverse_ref, right_ref, *scratch):
    inverse_factor(core_of(place_ref), mine_ref, other_ref, inverse_ref, *scratch)
    own = matrix(mine_ref[by_distance(pair_of(place_ref), mine_ref)[0], :RANK])
    right_ref[...] = product(own, inverse_ref[...], 1, 1).reshape(right_ref.shape)


def exchanged(tiles, axis):
    return lax.all_to_all(tiles, axis, 0, 0, tiled=True)


def from_peer(x, axis, step):
    count = lax.axis_size(axis)
    return lax.ppermute(x, axis, [(i, i ^ step) for i in range(count)])


def together(x, others):
    return lax.optimization_barrier((x, others))


def from_sibling(x):
    return from_peer(x, "core", 1)


def across(x):
    return from_peer(x, "y_lo", 1)


def plane_total(x, y, besides):
    done = []
    for x_step, y_step, beside in zip((1, 3), (3, 1), besides):
        moved, beside = together((from_peer(x, "z", x_step), from_peer(y, "z", y_step)), beside)
        x, y = x + moved[0], y + moved[1]
        done.append(beside)
    return (x, y), done


def column_half(factors, bit):
    half = factors.shape[1] // 2
    mine, its = (
        lax.dynamic_slice_in_dim(factors, which * half, half, 1) for which in (bit, 1 - bit)
    )
    return mine, across(its)


def column_quarter(halves, core):
    size = halves[0].shape[1] // 2

    def columns(which):
        return [lax.dynamic_slice_in_dim(x, which * size, size, 1) for x in halves]

    return *columns(core), from_sibling(jnp.concatenate(columns(1 - core)))


def with_place(count):
    return [pl.BlockSpec(memory_space=m) for m in (pltpu.SMEM, *[pltpu.VMEM] * count)]


def work(products, size):
    return pl.CostEstimate(flops=6 * products * size**3, bytes_accessed=0, transcendentals=0)


def basis_rows(place, inverse, quarters):
    rank = inverse.shape[0]
    return call(
        whole_basis,
        [(4 * len(quarters[0]), rank)],
        place,
        inverse,
        *quarters,
        in_specs=with_place(5),
        cost_estimate=work(4, rank),
    )


def gram_tiles(place, factors, parts, rank, beside):
    tiles = (lax.axis_size(ROW), RANK + rank // 2 // lax.axis_size(ROW), rank)
    mine, other = call(
        gram_and_cores,
        [tiles, tiles],
        place,
        *factors,
        *parts,
        in_specs=with_place(5),
        scratch_shapes=[pltpu.VMEM((rank, rank), jnp.float32)],
    )
    other, beside = together(from_sibling(other), beside)
    return mine + other, beside


def row_total(tiles):
    tiles = exchanged(tiles, ROW)
    return exchanged(call(owner_sum, [tiles.shape], tiles), ROW)


def local(b_factors, a_factors, u_start, v_start):
    shape = (*b_factors.shape[:2], u_start.shape[1])
    width, rank = u_start.shape
    bit, core = lax.axis_index("y_lo"), lax.axis_index("core")
    place = jnp.reshape(2 * bit + core, (1,)).astype(jnp.int32)
    b = b_factors.reshape(-1, width)
    a = a_factors.reshape(-1, width)
    b_half = column_half(b, bit)

    partial = call(
        projections,
        [(shape[0], 2 * RANK, rank)],
        *(pltpu.with_memory_space_constraint(x, pltpu.HBM) for x in (b, a, u_start, v_start)),
        in_specs=[pl.BlockSpec(memory_space=pltpu.HBM)] * 4,
        scratch_shapes=[
            *(pltpu.VMEM(x.shape, x.dtype) for x in (b, a, u_start, v_start)),
            pltpu.SemaphoreType.DMA((STEPS, 4)),
        ],
    )
    copies = (lax.axis_size(ROW), 2 * RANK, rank)
    tiles, b_half = together(exchanged(partial, "row"), b_half)
    b_quarter = column_quarter(b_half, core)
    pair = exchanged(call(owner_coefficients, [copies], tiles), ROW)
    pair, b_quarter = together(pair, b_quarter)
    pair_other = from_sibling(pair)

    part = (width // 8, rank)
    parts = call(
        load_sum, [part, part], place, *b_quarter, pair, pair_other, in_specs=with_place(5)
    )
    parts, (_, a_half) = plane_total(*parts, ((), column_half(a, bit)))
    a_quarter = column_quarter(a_half, core)
    basis = jnp.concatenate(parts)
    tiles, _ = gram_tiles(place, b_quarter, parts, rank, ())
    mine, a_quarter = together(row_total(tiles), a_quarter)
    inverse, left, *parts = call(
        turn_over,
        [(rank, rank), shape, part, part],
        place,
        mine,
        from_sibling(mine),
        pair,
        pair_other,
        *a_quarter,
        in_specs=with_place(7),
        scratch_shapes=factor_scratch(rank),
        cost_estimate=work(64, rank),
    )
    parts, moved = together(parts, across(basis))
    quarters = (basis, moved, from_sibling(basis), from_sibling(moved))
    u_scaled = basis_rows(place, inverse, quarters)
    parts, _ = plane_total(*parts, ((), ()))
    basis = jnp.concatenate(parts)
    tiles, u_scaled = gram_tiles(place, a_quarter, parts, rank, u_scaled)
    mine = row_total(tiles)
    inverse, right = call(
        right_cores,
        [(rank, rank), shape],
        place,
        mine,
        from_sibling(mine),
        in_specs=with_place(2),
        scratch_shapes=factor_scratch(rank),
    )
    moved = across(basis)
    quarters = (basis, moved, from_sibling(basis), from_sibling(moved))
    v_scaled = basis_rows(place, inverse, quarters)
    return u_scaled, v_scaled, left, right


def solution(mesh):
    count, rows = mesh.devices.shape
    mesh = Mesh(mesh.devices.reshape(count // 4, 2, 2, rows), ("z", "y_lo", "core", "row"))
    tenant = ("z", "y_lo", "core")
    in_specs = (P(tenant, None, "row"), P(tenant, None, "row"), P("row", None), P("row", None))
    out_specs = (P("row", None), P("row", None), P(tenant, None, None), P(tenant, None, None))
    return jax.shard_map(local, mesh=mesh, in_specs=in_specs, out_specs=out_specs, check_vma=False)
```

```python
import math

import jax
import jax.numpy as jnp
from jax import lax
from jax.experimental import pallas as pl
from jax.experimental.pallas import tpu as pltpu
from jax.sharding import Mesh
from jax.sharding import PartitionSpec as P

D = 8192
RANK = 16
LANES = 128
SUBLANES = 8
PANEL = 32
STEPS = 4
ROW = ("y_lo", "row")
STEPS_AWAY = (0, 2, 1, 3)


def pieces(x):
    high = x.astype(jnp.bfloat16)
    rest = x - high.astype(jnp.float32)
    middle = rest.astype(jnp.bfloat16)
    return high, middle, (rest - middle.astype(jnp.float32)).astype(jnp.bfloat16)


def float32_product(x, y):
    xh, xm, xl = pieces(x)
    yh, ym, yl = pieces(y)
    xs = jnp.concatenate([xh, xh, xm, xh, xl, xm])
    ys = jnp.concatenate([yh, ym, yh, yl, yh, ym])
    return lax.dot_general(xs, ys, (((0,), (0,)), ((), ())), preferred_element_type=jnp.float32)


def column(x, lane):
    return jnp.broadcast_to(x[:, lane : lane + 1], (SUBLANES, LANES))


def spread(ref, row):
    return ref[pl.ds(row, SUBLANES, stride=0), :]


def eliminate(rows, units, start, rows_ref, columns_ref, factors_ref):
    sub = lax.broadcasted_iota(jnp.int32, (SUBLANES, LANES), 0)
    tile = start // LANES
    for m, first in enumerate(range(start % LANES, start % LANES + PANEL, SUBLANES)):
        slot = m % 4
        tiles = [*rows[m], units[m]]
        if m == 0:
            pivots = [column(rows[m][tile], first + j) for j in range(SUBLANES)]
        for j in range(SUBLANES):
            columns_ref[slot, pl.ds(j * SUBLANES, SUBLANES), :] = pivots[j]
        for t, x in enumerate(tiles):
            rows_ref[slot, pl.ds(t * SUBLANES, SUBLANES), :] = x
        r = [
            [spread(rows_ref.at[slot], t * SUBLANES + i) for t in range(len(tiles))]
            for i in range(SUBLANES)
        ]
        d = [
            [spread(columns_ref.at[slot], j * SUBLANES + i) for j in range(SUBLANES)]
            for i in range(SUBLANES)
        ]
        later = range(m + 1, len(rows))
        c = {g: [column(rows[g][tile], first + j) for j in range(SUBLANES)] for g in later}
        if later:
            ahead = first + SUBLANES
            pivots = [column(rows[m + 1][tile], ahead + j) for j in range(SUBLANES)]
        done = tiles
        for j in range(SUBLANES):
            inverse = lax.rsqrt(d[j][j])
            p = [x * inverse for x in r[j]]
            done = [jnp.where(sub == j, x, y) for x, y in zip(p, done)]
            below = range(j + 1, SUBLANES)
            factor = {i: d[j][i] * inverse for i in below}
            for i in below:
                for other in range(i, SUBLANES):
                    d[i][other] -= factor[i] * factor[other]
                r[i] = [x - factor[i] * y for x, y in zip(r[i], p)]
            for g in later:
                scale = c[g][j] * inverse
                if g == m + 1:
                    place = pl.ds(j * SUBLANES, SUBLANES)
                    factors_ref[slot, place, :] = scale
                    for k in range(SUBLANES):
                        pivots[k] -= scale * spread(factors_ref.at[slot], j * SUBLANES + k)
                for i in below:
                    c[g][i] -= scale * factor[i]
                rows[g] = [x - scale * y for x, y in zip(rows[g], p)]
                units[g] -= scale * p[-1]
        rows[m], units[m] = done[:-1], done[-1]
    rows = [jnp.concatenate(tiles, axis=1) for tiles in rows]
    return jnp.concatenate(rows), jnp.concatenate(units)


def split(x):
    high = x.astype(jnp.bfloat16)
    return high, (x - high.astype(jnp.float32)).astype(jnp.bfloat16)


def product(x, y, x_dim=1, y_dim=0):
    dims = (((x_dim,), (y_dim,)), ((), ()))
    xh, xl = split(x)
    yh, yl = split(y)

    def part(p, q):
        return lax.dot_general(p, q, dims, preferred_element_type=jnp.float32)

    return part(xh, yh) + (part(xh, yl) + part(xl, yh))


def matrix(x):
    return x.reshape(-1, x.shape[-1])


def factor_in_place(out_ref, *scratch):
    n = out_ref.shape[0]
    sub = lax.broadcasted_iota(jnp.int32, (SUBLANES, LANES), 0)
    lane = lax.broadcasted_iota(jnp.int32, (SUBLANES, LANES), 1)
    column = lax.broadcasted_iota(jnp.int32, (n, n), 1)
    for start in range(0, n, PANEL):
        end = start + PANEL
        tile = start // LANES
        rows, units = [], []
        for g in range(0, PANEL, SUBLANES):
            place = pl.ds(start + g, SUBLANES)
            rows.append([out_ref[place, pl.ds(t, LANES)] for t in range(0, n, LANES)])
            units.append(jnp.where(lane == sub + (start % LANES + g), 1.0, 0.0))
        rows, units = eliminate(rows, units, start, *scratch)
        blank = jnp.zeros_like(units)
        units = jnp.concatenate([units if t == tile else blank for t in range(n // LANES)], axis=1)
        inside = (column >= start) & (column < end)
        solved = jnp.where(inside[:PANEL], units, rows)
        out_ref[pl.ds(start, PANEL), :] = jnp.where(column[:PANEL] < end, solved, 0.0)
        if end < n:
            aligned = end // LANES * LANES
            update = float32_product(rows[:, aligned:], solved)[end - aligned :]
            rest = out_ref[pl.ds(end, n - end), :]
            out_ref[pl.ds(end, n - end), :] = jnp.where(inside[end:], 0.0, rest) - update


def factor_scratch(n):
    tiles = n // LANES + 1
    return [
        pltpu.VMEM((4, tiles * SUBLANES, LANES), jnp.float32),
        pltpu.VMEM((4, SUBLANES * SUBLANES, LANES), jnp.float32),
        pltpu.VMEM((4, SUBLANES * SUBLANES, LANES), jnp.float32),
    ]


def call(kernel, shapes, *operands, **options):
    shapes = [jax.ShapeDtypeStruct(shape, jnp.float32) for shape in shapes]
    return pl.pallas_call(
        kernel,
        out_shape=shapes if len(shapes) > 1 else shapes[0],
        compiler_params=pltpu.CompilerParams(vmem_limit_bytes=32 << 20),
        name=kernel.__name__,
        **options,
    )(*operands)


def projections(b_hbm, a_hbm, u_hbm, v_hbm, out_ref, b_ref, a_ref, u_ref, v_ref, sems):
    step = b_ref.shape[1] // STEPS
    copies = []
    for i in range(STEPS):
        part = pl.ds(i * step, step)
        pairs = (
            (u_hbm.at[part], u_ref.at[part]),
            (b_hbm.at[:, part], b_ref.at[:, part]),
            (v_hbm.at[part], v_ref.at[part]),
            (a_hbm.at[:, part], a_ref.at[:, part]),
        )
        copies.append([pltpu.make_async_copy(*p, sems.at[i, k]) for k, p in enumerate(pairs)])
    for group in copies:
        for copy in group:
            copy.start()
    left = right = 0.0
    for i, group in enumerate(copies):
        part = pl.ds(i * step, step)
        group[0].wait()
        group[1].wait()
        left += product(b_ref[:, part], u_ref[part])
        group[2].wait()
        group[3].wait()
        right += product(a_ref[:, part], v_ref[part])
    out_ref[:, :RANK] = left.reshape(-1, RANK, left.shape[1])
    out_ref[:, RANK:] = right.reshape(-1, RANK, right.shape[1])


def owner_coefficients(tiles_ref, out_ref):
    total = jnp.sum(tiles_ref[...], axis=0)
    left, right = total[:RANK], total[RANK:]
    coeffs = product(product(right, right, 1, 1), left)
    out_ref[:, :RANK] = jnp.broadcast_to(coeffs, (len(out_ref), *coeffs.shape))
    out_ref[:, RANK:] = jnp.broadcast_to(right, (len(out_ref), *right.shape))


def owner_sum(tiles_ref, out_ref):
    out_ref[...] = jnp.broadcast_to(jnp.sum(tiles_ref[...], axis=0), out_ref.shape)


def stacked(refs):
    return jnp.concatenate([ref[...] for ref in refs])


def quarter_of(place_ref):
    return place_ref[0]


def core_of(place_ref):
    return place_ref[0] % 2


def pair_of(place_ref):
    return place_ref[0] // 2


def by_distance(pair, ref):
    count = len(ref) // 2
    return [pl.ds(place * count, count) for place in (pair, 1 - pair)]


def tenants(pair, refs, first):
    rows = pl.ds(first, RANK)
    tiles = [ref[place, rows] for ref in refs for place in by_distance(pair, ref)]
    return jnp.concatenate([matrix(x) for x in tiles])


def load_sum(place_ref, f0, f1, f2, mine_ref, other_ref, *out_refs):
    coeffs = tenants(pair_of(place_ref), (mine_ref, other_ref), 0)
    store_load(product(stacked((f0, f1, f2)), coeffs, 0, 0), out_refs)


def store_load(load, out_refs):
    count = len(out_refs[0])
    for i, ref in enumerate(out_refs):
        ref[...] = load[i * count : (i + 1) * count]


def gram_and_cores(place_ref, f0, f1, f2, x_ref, y_ref, mine_ref, other_ref, gram_ref):
    basis = stacked((x_ref, y_ref))
    cores = product(stacked((f0, f1, f2)), basis)
    gram_ref[...] = product(basis, basis, 0, 0)
    core, half = core_of(place_ref), len(gram_ref) // 2
    block = len(cores) // 4
    for i, (ref, which) in enumerate(((mine_ref, core), (other_ref, 1 - core))):
        for j, place in enumerate(by_distance(pair_of(place_ref), ref)):
            rows = cores[(2 * i + j) * block : (2 * i + j + 1) * block]
            ref[place, :RANK] = rows.reshape(-1, RANK, rows.shape[1])
        rows = gram_ref[pl.ds(which * half, half), :]
        ref[:, RANK:] = rows.reshape(len(ref), -1, rows.shape[1])


def inverse_factor(core, mine_ref, other_ref, inverse_ref, *scratch):
    half = len(inverse_ref) // 2
    inverse_ref[pl.ds(core * half, half), :] = matrix(mine_ref[:, RANK:])
    inverse_ref[pl.ds((1 - core) * half, half), :] = matrix(other_ref[:, RANK:])
    factor_in_place(inverse_ref, *scratch)


def turn_over(
    place_ref, mine_ref, other_ref, pair_ref, pair_other_ref, f0, f1, f2,
    inverse_ref, left_ref, x_ref, y_ref, *scratch,
):
    pair = pair_of(place_ref)
    inverse_factor(core_of(place_ref), mine_ref, other_ref, inverse_ref, *scratch)
    left = product(tenants(pair, (mine_ref, other_ref), 0), inverse_ref[...], 1, 1)
    right = tenants(pair, (pair_ref, pair_other_ref), RANK)
    own = left[: len(left) // 4]
    left_ref[...] = own.reshape(left_ref.shape)
    half = len(left) // 2
    tenant = [lax.broadcasted_iota(jnp.int32, (half, half), d) // RANK for d in range(2)]
    coeffs = []
    for part in (slice(0, half), slice(half, None)):
        weight = jnp.where(tenant[0] == tenant[1], product(left[part], left[part], 1, 1), 0.0)
        coeffs.append(product(weight, right[part]))
    load = product(stacked((f0, f1, f2)), jnp.concatenate(coeffs), 0, 0)
    store_load(load, (x_ref, y_ref))


def scaled_basis(quarter, inverse, refs, out_ref):
    scale = math.sqrt(D)
    for step, ref in zip(STEPS_AWAY, refs):
        rows = pl.ds((quarter ^ step) * len(ref), len(ref))
        out_ref[rows, :] = product(ref[...], inverse, 1, 1) * scale


def whole_basis(place_ref, inverse_ref, q0, q1, q2, q3, out_ref):
    scaled_basis(quarter_of(place_ref), inverse_ref[...], (q0, q1, q2, q3), out_ref)


def right_cores(place_ref, mine_ref, other_ref, inverse_ref, right_ref, *scratch):
    inverse_factor(core_of(place_ref), mine_ref, other_ref, inverse_ref, *scratch)
    own = matrix(mine_ref[by_distance(pair_of(place_ref), mine_ref)[0], :RANK])
    right_ref[...] = product(own, inverse_ref[...], 1, 1).reshape(right_ref.shape)


def exchanged(tiles, axis):
    return lax.all_to_all(tiles, axis, 0, 0, tiled=True)


def from_peer(x, axis, step):
    count = lax.axis_size(axis)
    return lax.ppermute(x, axis, [(i, i ^ step) for i in range(count)])


def together(x, others):
    return lax.optimization_barrier((x, others))


def from_sibling(x):
    return from_peer(x, "core", 1)


def across(x):
    return from_peer(x, "y_lo", 1)


def plane_total(x, y, besides):
    done = []
    for x_step, y_step, beside in zip((1, 3), (3, 1), besides):
        moved, beside = together((from_peer(x, "z", x_step), from_peer(y, "z", y_step)), beside)
        x, y = x + moved[0], y + moved[1]
        done.append(beside)
    return (x, y), done


def column_half(factors, bit):
    half = factors.shape[1] // 2
    mine, its = (
        lax.dynamic_slice_in_dim(factors, which * half, half, 1) for which in (bit, 1 - bit)
    )
    return mine, across(its)


def column_quarter(halves, core):
    size = halves[0].shape[1] // 2

    def columns(which):
        return [lax.dynamic_slice_in_dim(x, which * size, size, 1) for x in halves]

    return *columns(core), from_sibling(jnp.concatenate(columns(1 - core)))


def with_place(count):
    return [pl.BlockSpec(memory_space=m) for m in (pltpu.SMEM, *[pltpu.VMEM] * count)]


def work(products, size):
    return pl.CostEstimate(flops=6 * products * size**3, bytes_accessed=0, transcendentals=0)


def basis_rows(place, inverse, quarters):
    rank = inverse.shape[0]
    return call(
        whole_basis,
        [(4 * len(quarters[0]), rank)],
        place,
        inverse,
        *quarters,
        in_specs=with_place(5),
        cost_estimate=work(4, rank),
    )


def gram_tiles(place, factors, parts, rank, beside):
    tiles = (lax.axis_size(ROW), RANK + rank // 2 // lax.axis_size(ROW), rank)
    mine, other = call(
        gram_and_cores,
        [tiles, tiles],
        place,
        *factors,
        *parts,
        in_specs=with_place(5),
        scratch_shapes=[pltpu.VMEM((rank, rank), jnp.float32)],
    )
    other, beside = together(from_sibling(other), beside)
    return mine + other, beside


def row_total(tiles, beside=()):
    tiles, beside = together(exchanged(tiles, ROW), beside)
    return exchanged(call(owner_sum, [tiles.shape], tiles), ROW), beside


def local(b_factors, a_factors, u_start, v_start):
    shape = (*b_factors.shape[:2], u_start.shape[1])
    width, rank = u_start.shape
    bit, core = lax.axis_index("y_lo"), lax.axis_index("core")
    place = jnp.reshape(2 * bit + core, (1,)).astype(jnp.int32)
    b = b_factors.reshape(-1, width)
    a = a_factors.reshape(-1, width)
    b_half = column_half(b, bit)

    partial = call(
        projections,
        [(shape[0], 2 * RANK, rank)],
        *(pltpu.with_memory_space_constraint(x, pltpu.HBM) for x in (b, a, u_start, v_start)),
        in_specs=[pl.BlockSpec(memory_space=pltpu.HBM)] * 4,
        scratch_shapes=[
            *(pltpu.VMEM(x.shape, x.dtype) for x in (b, a, u_start, v_start)),
            pltpu.SemaphoreType.DMA((STEPS, 4)),
        ],
    )
    copies = (lax.axis_size(ROW), 2 * RANK, rank)
    tiles, b_half = together(exchanged(partial, "row"), b_half)
    b_quarter = column_quarter(b_half, core)
    pair = exchanged(call(owner_coefficients, [copies], tiles), ROW)
    pair, b_quarter = together(pair, b_quarter)
    pair_other = from_sibling(pair)

    part = (width // 8, rank)
    parts = call(
        load_sum, [part, part], place, *b_quarter, pair, pair_other, in_specs=with_place(5)
    )
    parts, (_, a_half) = plane_total(*parts, ((), column_half(a, bit)))
    basis = jnp.concatenate(parts)
    tiles, _ = gram_tiles(place, b_quarter, parts, rank, ())
    mine, a_half = row_total(tiles, a_half)
    mine, a_quarter = together(mine, column_quarter(a_half, core))
    inverse, left, *parts = call(
        turn_over,
        [(rank, rank), shape, part, part],
        place,
        mine,
        from_sibling(mine),
        pair,
        pair_other,
        *a_quarter,
        in_specs=with_place(7),
        scratch_shapes=factor_scratch(rank),
        cost_estimate=work(64, rank),
    )
    parts, moved = together(parts, across(basis))
    quarters = (basis, moved, from_sibling(basis), from_sibling(moved))
    u_scaled = basis_rows(place, inverse, quarters)
    parts, (u_scaled, _) = plane_total(*parts, (u_scaled, ()))
    basis = jnp.concatenate(parts)
    tiles, _ = gram_tiles(place, a_quarter, parts, rank, ())
    mine, _ = row_total(tiles)
    inverse, right = call(
        right_cores,
        [(rank, rank), shape],
        place,
        mine,
        from_sibling(mine),
        in_specs=with_place(2),
        scratch_shapes=factor_scratch(rank),
    )
    moved = across(basis)
    quarters = (basis, moved, from_sibling(basis), from_sibling(moved))
    v_scaled = basis_rows(place, inverse, quarters)
    return u_scaled, v_scaled, left, right


def solution(mesh):
    count, rows = mesh.devices.shape
    mesh = Mesh(mesh.devices.reshape(count // 4, 2, 2, rows), ("z", "y_lo", "core", "row"))
    tenant = ("z", "y_lo", "core")
    in_specs = (P(tenant, None, "row"), P(tenant, None, "row"), P("row", None), P("row", None))
    out_specs = (P("row", None), P("row", None), P(tenant, None, None), P(tenant, None, None))
    return jax.shard_map(local, mesh=mesh, in_specs=in_specs, out_specs=out_specs, check_vma=False)
```
